32 devices in a mesh: cfg: 2 (over y), slab: 4 (over z), energy: 4 (over x, core).
Axes of the slice: x: 2, y: 2, z: 4, core: 2. Of those that a mesh axis runs over, the one named last changes fastest.
Arguments:
- energy_index: int32 [4], P('energy'), may hold values from 0 to 8190, as said below
- diag_blocks: float32 [16, 192, 192], P(('cfg', 'slab')), parts along dimension 0, may hold values from -3 to 7, as said below
- couple: float32 [16, 192, 192], P(('cfg', 'slab')), parts along dimension 0, may hold values from -4 to 4, as said below
- probes: float32 [1536, 128], P('slab'), may hold values from -12 to 12
- orbital_cell: int32 [1536], P('slab'), may hold values from 0 to 262143, as said below
- dopant_cells: int32 [2048], P('cfg'), parts along dimension 0, may hold values from 0 to 262143
- initial_potential: float32 [64, 64, 128], P(('cfg', 'slab'), 'energy'), parts along dimension 0, may hold values from -4 to 4
Outputs:
- potential: float32 [64, 64, 128], P(('cfg', 'slab'), 'energy'), parts along dimension 0
- density: float32 [3072], P(('cfg', 'slab')), parts along dimension 0
The draws below stay inside these ranges and needn't reach their ends.
There are 2 independent parts, one for each index of `cfg`. The reference program is written for one: setup_inputs(seed, part) draws one part's arguments, and reference() takes and returns one part's arrays. A program takes and returns all parts, laid end to end along the dimension named above; an argument that names none is the same for every part. Nothing has to cross between parts.
Inputs may be any that keep to these rules, and one draw needn't show every extreme that they name: `energy_index`: one energy point has index 0 and another has index 8190. Each placement has its own operator: diag_blocks and couple are the diagonal and below-diagonal blocks of a symmetric positive semidefinite block-tridiagonal matrix; each diagonal block is symmetric. couple[i] is the block of that same matrix in block row i and block column i - 1. `orbital_cell`: orbital o lies in a cell whose z index is at least (o // 384) * 8 and below that plus 8.
All inputs are finite; a program needn't handle non-finite values.
Results may differ from the reference program's by a relative error of at most 0.0003.
Values sent between devices are 32-bit elements; how exact they have to be, the bound alone decides.
No kernel may reach another device: no remote copies, remote signals or barrier semaphores. Data moves between devices by JAX's collectives and lax.ppermute only.
A program may use at most 64 MiB of HBM per device.

```python
import jax
import jax.numpy as jnp
from jax import lax

NB = 192
BLK_DEV = 2
NBLK = 8
NORB = 1536
PROBES = 128
NE = 4
GX = 64
GY = 128
CZ = 8
NZ = 32
NDOP = 1024
SWEEPS = 2


coupling_scale = 1.58


def hamiltonian(key):
    keys = jax.random.split(jax.random.fold_in(key, 11), 2)
    spread = 0.3 / NB ** 0.5
    unit = jnp.eye(NB, dtype=jnp.float32)
    own = coupling_scale * (unit + spread * jax.random.truncated_normal(keys[0], -4.0, 4.0, (NBLK, NB, NB), jnp.float32))
    behind = -coupling_scale * (unit + spread * jax.random.truncated_normal(keys[1], -4.0, 4.0, (NBLK, NB, NB), jnp.float32))
    own_square = jnp.einsum('kji,kjl->kil', own, own, precision=lax.Precision.HIGHEST)
    behind_square = jnp.einsum('kji,kjl->kil', behind, behind, precision=lax.Precision.HIGHEST)
    following = jnp.concatenate([behind_square[1:], jnp.zeros_like(behind_square[:1])], axis=0)
    diagonal = own_square + following
    diagonal = 0.5 * (diagonal + jnp.swapaxes(diagonal, 1, 2))
    lower = jnp.einsum('kji,kjl->kil', own, behind, precision=lax.Precision.HIGHEST)
    return (diagonal, lower)


def draw_diag_blocks(key, part):
    return hamiltonian(key)[0]


def draw_couple(key, part):
    return hamiltonian(key)[1]


def draw_energy_index(key, part):
    keys = jax.random.split(jax.random.fold_in(key, 31), 4)
    count = NE
    level = jax.random.randint(keys[0], (count,), 0, 13, dtype=jnp.int32)
    width_here = jnp.power(jnp.full((count,), 2, jnp.int32), level)
    offset = jax.random.randint(keys[1], (count,), 0, 8192, dtype=jnp.int32) % width_here
    index = width_here - 1 + offset
    lowest = jax.random.randint(keys[2], (), 0, count, dtype=jnp.int32)
    highest = (lowest + 1 + jax.random.randint(keys[3], (), 0, count - 1, dtype=jnp.int32)) % count
    positions = jnp.arange(count, dtype=jnp.int32)
    index = jnp.where(positions == lowest, 0, jnp.where(positions == highest, 8190, index))
    return index.astype(jnp.int32)


def draw_orbital_cell(key, part):
    keys = jax.random.split(jax.random.fold_in(key, 23), 3)
    orbital = jnp.arange(NORB, dtype=jnp.int32)
    depth = orbital // (NB * BLK_DEV) * CZ + jax.random.randint(keys[0], (NORB,), 0, CZ, dtype=jnp.int32)
    row = jax.random.randint(keys[1], (NORB,), 0, GX, dtype=jnp.int32)
    column = jax.random.randint(keys[2], (NORB,), 0, GY, dtype=jnp.int32)
    return ((depth * GX + row) * GY + column).astype(jnp.int32)


def touch_ends(array, stream_key, least, largest):
    longest = array.shape.index(max(array.shape))
    spots = []
    for shift in (0, 1):
        where = [jax.random.randint(jax.random.fold_in(stream_key, axis), (), 0, length) for axis, length in enumerate(array.shape)]
        where[longest] = (where[longest] + shift) % array.shape[longest]
        spots.append(tuple(where))
    return array.at[spots[0]].set(least).at[spots[1]].set(largest)


def steps_of(rng, dims, shards, least, top_value):
    def one(dim, parts):
        draws = jax.random.uniform(jax.random.fold_in(jax.random.fold_in(rng, 6), dim), (parts,), jnp.float32, least / len(shards), top_value / len(shards))
        return jnp.repeat(jnp.exp(draws), dims[dim] // parts).reshape((-1,) + (1,) * (len(dims) - dim - 1))

    level = one(*shards[0])
    for cut in shards[1:]:
        level = level * one(*cut)
    return level


def noise(rng, shape, width, reach, shards=(), held_as=jnp.bfloat16):
    entries = jax.random.normal(rng, shape, jnp.float32) * width
    if len(shards) > 0:
        entries = steps_of(rng, shape, shards, -0.22, 0.18) * entries
    return jnp.clip(entries, min=-reach, max=reach).astype(held_as)


def setup_inputs(seed: int = 0, part: int = 0) -> dict:
    seeds = jax.random.split(jax.random.key(seed), 8)
    part_splits = jax.random.split(jax.random.fold_in(seeds[7], part), 8)
    return {
        "energy_index": draw_energy_index(jax.random.fold_in(seeds[7], 71), part),
        "diag_blocks": draw_diag_blocks(jax.random.fold_in(jax.random.fold_in(seeds[7], part), 71), part),
        "couple": draw_couple(jax.random.fold_in(jax.random.fold_in(seeds[7], part), 71), part),
        "probes": noise(seeds[3], (NORB, PROBES), 2.0, 12.0, ((0, 4),), jnp.float32),
        "orbital_cell": draw_orbital_cell(jax.random.fold_in(seeds[7], 71), part),
        "dopant_cells": touch_ends(jax.random.randint(part_splits[5], (NDOP,), 0, NZ * GX * GY), jax.random.fold_in(part_splits[5], 1), 0, (NZ * GX * GY) - 1).astype(jnp.int32),
        "initial_potential": noise(part_splits[6], (NZ, GX, GY), 0.5, 4.0, ((0, 4), (1, 4)), jnp.float32),
    }


sigma_base = 0.02
sigma_step = 0.01
coupling_beta = 0.5
dopant_charge = 4.0

def product(left, right):
    return jnp.dot(left.astype(jnp.float32), right.astype(jnp.float32), precision=lax.Precision.HIGHEST, preferred_element_type=jnp.float32)

def reference(energy_index, diag_blocks, couple, probes, orbital_cell, dopant_cells, initial_potential):
    keep = (jnp.arange(NBLK) > 0).astype(jnp.float32)[:, None, None]
    lowers = couple * keep
    next_lowers = jnp.concatenate([lowers[1:], jnp.zeros_like(lowers[:1])], axis=0)
    sources = probes.reshape(NBLK, NB, PROBES)
    unit = jnp.eye(NB, dtype=jnp.float32)

    def one_energy(index):
        shift = sigma_base + sigma_step * index.astype(jnp.float32)

        def forward(carry, inputs):
            carry_couple, carry_value = carry
            diagonal, lower, upper_next, source = inputs
            pivot = diagonal + shift * unit - product(lower, carry_couple)
            reduced = source - product(lower, carry_value)
            solved = jnp.linalg.solve(pivot, jnp.concatenate([upper_next.T, reduced], axis=1))
            pair = (solved[:, :NB], solved[:, NB:])
            return (pair, pair)
        start = (jnp.zeros((NB, NB), jnp.float32), jnp.zeros((NB, PROBES), jnp.float32))
        unused, stored = lax.scan(forward, start, (diag_blocks, lowers, next_lowers, sources))
        factors, values = stored

        def backward(later, inputs):
            factor, value = inputs
            current = value - product(factor, later)
            return (current, current)
        unused_last, solution = lax.scan(backward, jnp.zeros((NB, PROBES), jnp.float32), (factors, values), reverse=True)
        return jnp.sum(sources * solution, axis=2).reshape(NORB)
    density = jnp.sum(lax.map(one_energy, energy_index), axis=0) / (PROBES * NE)
    cells = NZ * GX * GY
    electrons = jax.ops.segment_sum(density, orbital_cell, num_segments=cells).reshape(NZ, GX, GY)
    counted = jax.ops.segment_sum(jnp.ones(dopant_cells.shape, jnp.float32), dopant_cells, num_segments=cells)
    dopants = dopant_charge * counted.reshape(NZ, GX, GY)
    potential = initial_potential
    for sweep in range(SWEEPS):
        padded = jnp.pad(potential, 1)
        beside_all = padded[2:, 1:-1, 1:-1] + padded[:-2, 1:-1, 1:-1]
        beside_all = beside_all + padded[1:-1, 2:, 1:-1] + padded[1:-1, :-2, 1:-1]
        beside_all = beside_all + padded[1:-1, 1:-1, 2:] + padded[1:-1, 1:-1, :-2]
        growth = jnp.exp(potential - initial_potential)
        residual = beside_all - 6.0 * potential + coupling_beta * (dopants - electrons * growth)
        potential = potential + residual / (6.0 + coupling_beta * jnp.abs(electrons) * growth)
    return (potential, density)
```

```python
import functools

import jax
import jax.numpy as jnp
from jax import lax
from jax.experimental import pallas as pl
from jax.experimental.pallas import tpu as pltpu
from jax.sharding import PartitionSpec as P

SWEEPS = 2

sigma_base = 0.02
sigma_step = 0.01
coupling_beta = 0.5
dopant_charge = 4.0

F32 = jnp.float32
BF16 = jnp.bfloat16
NT = (((1,), (1,)), ((), ()))
NN = (((1,), (0,)), ((), ()))


def split2(a):
    high = a.astype(BF16)
    return high, (a - high.astype(F32)).astype(BF16)


def one_pass(a, b, dims=NN):
    return lax.dot_general(a, b, dims, preferred_element_type=F32)


def dot3(a, b):
    ah, al = split2(a)
    bh, bl = split2(b)
    return one_pass(ah, bh) + (one_pass(ah, bl) + one_pass(al, bh))


def dot6(a, b, dims=NN):
    return lax.dot_general(
        a, b, dims, precision=lax.Precision.HIGHEST, preferred_element_type=F32
    )


def eye(n):
    return (
        lax.broadcasted_iota(jnp.int32, (n, n), 0) == lax.broadcasted_iota(jnp.int32, (n, n), 1)
    ).astype(F32)


def invert(matrix, hold, ratio, doublings):
    unit = eye(matrix.shape[0])
    sums = jnp.sum(jnp.abs(matrix), axis=0, keepdims=True)
    bound = jnp.max(sums, axis=1, keepdims=True)
    first = 2.0 / (bound * (1.0 + ratio))
    error = unit - first * matrix
    guess = first * unit
    tau = (1.0 + ratio) / (1.0 - ratio)
    for k in range(doublings):
        after = 2.0 * tau * tau - 1.0
        scale = (after + 1.0) / after
        if k == 0:
            grown = guess + first * error
        else:
            grown = guess + dot3(guess, error)
        if k + 1 < doublings:
            error = scale * dot3(error, error) - (scale - 1.0) * unit
        guess = scale * grown
        tau = after
    residual = unit - dot6(matrix, guess)
    size = jnp.sum(residual * residual)
    hold[...] = guess + dot3(guess, residual)

    @pl.when(jnp.logical_not(size < 0.9))
    def _():
        hold[...] = first * unit

    def go_on(state):
        count, last = state
        return jnp.logical_and(count < 64, jnp.logical_not(last < 1e-5))

    def newton(state):
        count, _ = state
        now = hold[...]
        left = unit - dot6(matrix, now)
        hold[...] = now + dot6(now, left)
        return count + 1, jnp.sum(left * left)

    lax.while_loop(go_on, newton, (jnp.int32(0), size))
    return hold[...]


def pack_symmetric(matrix, out):
    half = matrix.shape[0] // 3
    out[0:half, :] = matrix[half : 2 * half, 0 : 2 * half]
    out[half : 2 * half, :] = matrix[2 * half :, 0 : 2 * half]
    out[2 * half : 3 * half, :] = jnp.concatenate(
        [matrix[0:half, 0:half], matrix[2 * half :, 2 * half :]], axis=1
    )


def unpack_symmetric(packed):
    third = packed.shape[0] // 3
    row1 = packed[0:third]
    row2 = packed[third : 2 * third]
    ends = packed[2 * third :]
    b10, b11 = row1[:, :third], row1[:, third:]
    b20, b21 = row2[:, :third], row2[:, third:]
    b00, b22 = ends[:, :third], ends[:, third:]
    return jnp.concatenate(
        [
            jnp.concatenate([b00, b10.T, b20.T], axis=1),
            jnp.concatenate([b10, b11, b21.T], axis=1),
            jnp.concatenate([b20, b21, b22], axis=1),
        ],
        axis=0,
    )


def stage_kernel(has_message, ratios, doublings, place, energy, diag, couple, probes, message,
                 factor_p, value_p, matrix_q, source_q, inverse_q, value_q, out, hold):
    left = place[0] > 0
    right_index = 1 - place[0]
    width = diag.shape[1]
    unit = eye(width)
    shift = sigma_base + sigma_step * jnp.full((1, 1), energy[0], jnp.int32).astype(F32)
    shifted = shift * unit
    sp = diag[right_index] + shifted
    rp = probes[pl.ds(pl.multiple_of(right_index * width, width), width), :]
    rq = probes[pl.ds(pl.multiple_of((1 - right_index) * width, width), width), :]
    if has_message:
        taken = place[1] > 0
        block = jnp.where(taken, unpack_symmetric(message[0:width, :]), 0.0)
        column = jnp.where(taken, message[width : 2 * width, :], 0.0)
        outer = couple[0]
        matrix_q[...] = block
        source_q[...] = column

        @pl.when(left)
        def _():
            matrix_q[...] = dot3(outer, dot3(block, outer.T))
            source_q[...] = dot3(outer, column)

        sp = sp - matrix_q[...]
        rp = rp - source_q[...]
    inner = couple[1]
    inner_t = inner.T
    apq = jnp.where(left, inner_t, inner)
    aqp = jnp.where(left, inner, inner_t)
    xp = invert(sp, hold, ratios[0], doublings[0])
    fp = dot3(xp, apq)
    yp = dot3(xp, rp)
    factor_p[...] = fp
    value_p[...] = yp
    sq = diag[1 - right_index] + shifted - dot3(aqp, fp)
    rq = rq - dot3(aqp, yp)
    matrix_q[...] = sq
    source_q[...] = rq
    xq = invert(sq, hold, ratios[1], doublings[1])
    yq = dot3(xq, rq)
    inverse_q[...] = xq
    value_q[...] = yq

    @pl.when(left)
    def _():
        pack_symmetric(xq, out)
        out[width : 2 * width, :] = yq

    @pl.when(jnp.logical_not(left))
    def _():
        own = couple[0]
        own_t = own.T
        pack_symmetric(dot3(own_t, dot3(xq, own)), out)
        out[width : 2 * width, :] = dot3(own_t, yq)


def join_kernel(ratio, doublings, place, couple, message, factor_p, value_p, matrix_q, source_q,
                out_p, out_q, out, hold, hold_r):
    left = place[0] > 0
    width = couple.shape[1]
    block = unpack_symmetric(message[0:width, :])
    column = message[width : 2 * width, :]
    hold[...] = block
    hold_r[...] = column

    @pl.when(jnp.logical_not(left))
    def _():
        own = couple[0]
        hold[...] = dot3(own, dot3(block, own.T))
        hold_r[...] = dot3(own, column)

    sq = matrix_q[...] - hold[...]
    rq = source_q[...] - hold_r[...]
    xq = dot3(invert(sq, hold, ratio, doublings), rq)
    xp = value_p[...] - dot3(factor_p[...], xq)
    out_p[...] = xp
    out_q[...] = xq
    out[...] = xp

    @pl.when(left)
    def _():
        out[...] = dot3(couple[0].T, xp)


def back_kernel(place, couple, probes, message, known_p, known_q, factor_p, value_p, inverse_q,
                value_q, out_p, out_q, out, dens):
    left = place[0] > 0
    width = couple.shape[1]
    out_p[...] = known_p[...]
    out_q[...] = known_q[...]

    @pl.when(place[1] > 0)
    def _():
        out_q[...] = message[...]

        @pl.when(jnp.logical_not(left))
        def _():
            out_q[...] = dot3(couple[0], message[...])

        xq = value_q[...] - dot3(inverse_q[...], out_q[...])
        out_q[...] = xq
        out_p[...] = value_p[...] - dot3(factor_p[...], xq)

    xp = out_p[...]
    xq = out_q[...]
    out[...] = xp

    @pl.when(left)
    def _():
        out[...] = dot3(couple[0].T, xp)

    xa = jnp.where(left, xp, xq)
    xb = jnp.where(left, xq, xp)
    terms = jnp.concatenate([probes[0:width, :] * xa, probes[width:, :] * xb], axis=0)
    dens[...] = dot6(jnp.ones((8, terms.shape[1]), F32), terms, NT)


def poisson_kernel(rows_all, cells, place, weights, orbitals, dopants, around, out, fine):
    depth, pitch, across = around.shape
    total = depth * pitch
    first_z, first_x, planes = place[0], place[1], place[2]
    plane = rows_all * across

    def spots(index):
        z = index // plane - first_z
        x = index // across % rows_all - first_x
        y = index % across
        inside = (z >= 0) & (z < depth) & (x >= 0) & (x < pitch)
        row = jnp.where(inside, z * pitch + x, -1)
        n = index.shape[1]
        pick_row = lax.broadcasted_iota(jnp.int32, (total, n), 0) == row
        pick_y = lax.broadcasted_iota(jnp.int32, (across, n), 0) == y
        return pick_row.astype(F32).astype(BF16), pick_y.astype(F32)

    rows, ys = spots(dopants[...])
    dopant = dopant_charge * one_pass(rows, ys.astype(BF16), NT)
    rows, ys = spots(orbitals[...])
    spread = ys * weights[...]
    h = spread.astype(BF16)
    rest = spread - h.astype(F32)
    m = rest.astype(BF16)
    low = (rest - m.astype(F32)).astype(BF16)
    electron = one_pass(rows, h, NT) + (one_pass(rows, m, NT) + one_pass(rows, low, NT))
    electron = electron.reshape(depth, pitch, across)
    dopant = dopant.reshape(depth, pitch, across)
    start = around[...]
    zs = lax.broadcasted_iota(jnp.int32, start.shape, 0) + first_z
    xs = lax.broadcasted_iota(jnp.int32, start.shape, 1) + first_x
    ys = lax.broadcasted_iota(jnp.int32, start.shape, 2)
    exists = (zs >= 0) & (zs < planes) & (xs >= 0) & (xs < rows_all)
    potential = jnp.where(exists, start, 0.0)
    start = potential
    strength = coupling_beta * jnp.abs(electron)
    for _ in range(SWEEPS):
        blank = jnp.zeros((1, pitch, across), F32)
        beside = jnp.concatenate([potential[1:], blank], axis=0)
        beside = beside + jnp.concatenate([blank, potential[:-1]], axis=0)
        beside = beside + pltpu.roll(potential, 1, 1) + pltpu.roll(potential, pitch - 1, 1)
        beside = beside + jnp.where(ys > 0, pltpu.roll(potential, 1, 2), 0.0)
        beside = beside + jnp.where(ys < across - 1, pltpu.roll(potential, across - 1, 2), 0.0)
        growth = jnp.exp(potential - start)
        residual = beside - 6.0 * potential + coupling_beta * (dopant - electron * growth)
        potential = potential + residual / (6.0 + strength * growth)
        potential = jnp.where(exists, potential, 0.0)
    halo = SWEEPS
    out[...] = potential[halo : halo + out.shape[0], halo : halo + out.shape[1], :]


VM = pl.BlockSpec(memory_space=pltpu.VMEM)
SM = pl.BlockSpec(memory_space=pltpu.SMEM)


def like(*shape, dtype=F32):
    return jax.ShapeDtypeStruct(shape, dtype)


def pairs_of(count, odd):
    found = []
    for first in range(1 if odd else 0, count - 1, 2):
        found += [(first, first + 1), (first + 1, first)]
    return found


def slab_exchange(value, odd):
    slabs, energies = lax.axis_size("slab"), lax.axis_size("energy")
    pairs = pairs_of(slabs, odd)
    busy = {a for a, _ in pairs}
    whole = [(a * energies + e, b * energies + e) for a, b in pairs for e in range(energies)]
    for a in range(slabs):
        if a not in busy:
            whole += [(a * energies + e, a * energies + (e ^ 1)) for e in range(energies)]
    return lax.ppermute(value, ("slab", "energy"), whole)


def energy_exchange(value, odd):
    energies = lax.axis_size("energy")
    pairs = pairs_of(energies, odd)
    if odd:
        pairs += [(energies - 1, 0), (0, energies - 1)]
    return lax.ppermute(value, "energy", pairs)


def body(energy_index, diag_blocks, couple, probes, orbital_cell, dopant_cells, initial_potential):
    width = diag_blocks.shape[1]
    probe_count = probes.shape[1]
    slab, slabs = lax.axis_index("slab"), lax.axis_size("slab")
    energy, energies = lax.axis_index("energy"), lax.axis_size("energy")
    half = slabs // 2
    left = slab < half
    distance = jnp.where(left, slab, slabs - 1 - slab)
    left_flag = left.astype(jnp.int32)
    square, column = like(width, width), like(width, probe_count)
    letter = like(2 * width, probe_count)

    def flags(second):
        return jnp.stack([left_flag, second.astype(jnp.int32)])

    message = None
    for t in range(half):
        if t == 0:
            inbound = jnp.zeros((8, 128), F32)
        elif t == 1:
            inbound = message
        else:
            inbound = jnp.where(distance == t, message, kept)
        kept = inbound
        if t == 1:
            kept = jnp.where(distance == t, message, 0.0) if half > 2 else inbound
        accept = (distance >= 1) & (distance <= t)
        state = pl.pallas_call(
            functools.partial(stage_kernel, t > 0, (1 / 16, 1 / 16), (4, 4)),
            out_shape=(square, column, square, column, square, column, letter),
            in_specs=[SM, SM, VM, VM, VM, VM],
            out_specs=(VM,) * 7,
            scratch_shapes=[pltpu.VMEM((width, width), F32)],
            name=f"stage{t}",
        )(flags(accept), energy_index, diag_blocks, couple, probes, inbound)
        factor_p, value_p, matrix_q, source_q, inverse_q, value_q, sent = state
        message = slab_exchange(sent, t % 2 == 1)
    out_p, out_q, sent = pl.pallas_call(
        functools.partial(join_kernel, 1 / 128, 6),
        out_shape=(column, column, column),
        in_specs=[SM] + [VM] * 6,
        out_specs=(VM,) * 3,
        scratch_shapes=[pltpu.VMEM((width, width), F32), pltpu.VMEM((width, probe_count), F32)],
        name="join",
    )(flags(left), couple, message, factor_p, value_p, matrix_q, source_q)
    for t in range(half - 2, -1, -1):
        message = slab_exchange(sent, t % 2 == 1)
        out_p, out_q, sent, dens = pl.pallas_call(
            back_kernel,
            out_shape=(column, column, column, like(8, 2 * width)),
            in_specs=[SM] + [VM] * 9,
            out_specs=(VM,) * 4,
            name=f"back{t}",
        )(flags(distance == t), couple, probes, message, out_p, out_q, factor_p, value_p,
          inverse_q, value_q)
    total = dens
    for k in range(1, energies):
        total = total + lax.ppermute(
            dens, "energy", [(e, e ^ k) for e in range(energies)]
        )
    total = total[0:1] * (1.0 / (probe_count * energies))
    density = total.reshape(-1)

    cells_here = orbital_cell.reshape(1, -1)
    packet = jnp.concatenate([total, cells_here.astype(F32)], axis=0)
    near = slab_exchange(packet, False)
    far = slab_exchange(packet, True)
    weights = jnp.concatenate([total, near[0:1], far[0:1]], axis=1)
    alone = (slab == 0) | (slab == slabs - 1)
    nobody = jnp.int32(-(2**30))
    orbitals = jnp.concatenate(
        [cells_here, near[1:2].astype(jnp.int32),
         jnp.where(alone, nobody, far[1:2].astype(jnp.int32))],
        axis=1,
    )

    depth, rows_here, across = initial_potential.shape
    halo = SWEEPS
    odd_e = energy % 2 == 1
    low, high = initial_potential[:, :halo], initial_potential[:, rows_here - halo :]
    got_even = energy_exchange(jnp.where(odd_e, low, high), False)
    got_odd = energy_exchange(jnp.where(odd_e, high, low), True)
    below = jnp.where(odd_e, got_even, got_odd)
    above = jnp.where(odd_e, got_odd, got_even)
    wide = jnp.concatenate([below, initial_potential, above], axis=1)
    odd_s = slab % 2 == 1
    low, high = wide[:halo], wide[depth - halo :]
    got_even = slab_exchange(jnp.where(odd_s, low, high), False)
    got_odd = slab_exchange(jnp.where(odd_s, high, low), True)
    below = jnp.where(odd_s, got_even, got_odd)
    above = jnp.where(odd_s, got_odd, got_even)
    region = jnp.concatenate([below, wide, above], axis=0)
    pitch = -(-region.shape[1] // 8) * 8
    region = jnp.pad(region, ((0, 0), (0, pitch - region.shape[1]), (0, 0)))
    rows_all = rows_here * energies
    place = jnp.stack([slab * depth - halo, energy * rows_here - halo, jnp.int32(depth * slabs)])
    potential = pl.pallas_call(
        functools.partial(poisson_kernel, rows_all, None),
        out_shape=like(depth, rows_here, across),
        in_specs=[SM] + [VM] * 4,
        out_specs=VM,
        scratch_shapes=[pltpu.VMEM((8, 128), F32)],
        name="poisson",
    )(place, weights, orbitals, dopant_cells.reshape(1, -1), region)
    return (potential, density)


def solution(mesh):
    placed = (
        P("energy"),
        P(("cfg", "slab"), None, None),
        P(("cfg", "slab"), None, None),
        P("slab", None),
        P("slab"),
        P("cfg"),
        P(("cfg", "slab"), "energy", None),
    )
    return jax.shard_map(
        body,
        mesh=mesh,
        in_specs=placed,
        out_specs=(P(("cfg", "slab"), "energy", None), P(("cfg", "slab"))),
        check_vma=False,
    )
```

```python
import functools

import jax
import jax.numpy as jnp
from jax import lax
from jax.experimental import pallas as pl
from jax.experimental.pallas import tpu as pltpu
from jax.sharding import PartitionSpec as P

SWEEPS = 2

sigma_base = 0.02
sigma_step = 0.01
coupling_beta = 0.5
dopant_charge = 4.0

F32 = jnp.float32
BF16 = jnp.bfloat16
NT = (((1,), (1,)), ((), ()))
NN = (((1,), (0,)), ((), ()))


def split2(a):
    high = a.astype(BF16)
    return high, (a - high.astype(F32)).astype(BF16)


def one_pass(a, b, dims=NN):
    return lax.dot_general(a, b, dims, preferred_element_type=F32)


def dot3(a, b):
    ah, al = split2(a)
    bh, bl = split2(b)
    return one_pass(ah, bh) + (one_pass(ah, bl) + one_pass(al, bh))


def dot6(a, b, dims=NN):
    return lax.dot_general(
        a, b, dims, precision=lax.Precision.HIGHEST, preferred_element_type=F32
    )


def eye(n):
    return (
        lax.broadcasted_iota(jnp.int32, (n, n), 0) == lax.broadcasted_iota(jnp.int32, (n, n), 1)
    ).astype(F32)


def invert(matrix, hold, ratio, doublings):
    unit = eye(matrix.shape[0])
    sums = jnp.sum(jnp.abs(matrix), axis=0, keepdims=True)
    bound = jnp.max(sums, axis=1, keepdims=True)
    first = 2.0 / (bound * (1.0 + ratio))
    error = unit - first * matrix
    guess = first * unit
    tau = (1.0 + ratio) / (1.0 - ratio)
    for k in range(doublings):
        after = 2.0 * tau * tau - 1.0
        scale = (after + 1.0) / after
        if k == 0:
            grown = guess + first * error
        else:
            grown = guess + dot3(guess, error)
        if k + 1 < doublings:
            error = scale * dot3(error, error) - (scale - 1.0) * unit
        guess = scale * grown
        tau = after
    residual = unit - dot6(matrix, guess)
    size = jnp.sum(residual * residual)
    hold[...] = guess + dot3(guess, residual)

    @pl.when(jnp.logical_not(size < 0.9))
    def _():
        hold[...] = first * unit

    def go_on(state):
        count, last = state
        return jnp.logical_and(count < 64, jnp.logical_not(last < 1e-5))

    def newton(state):
        count, _ = state
        now = hold[...]
        left = unit - dot6(matrix, now)
        hold[...] = now + dot6(now, left)
        return count + 1, jnp.sum(left * left)

    lax.while_loop(go_on, newton, (jnp.int32(0), size))
    return hold[...]


def pack_symmetric(matrix, out):
    half = matrix.shape[0] // 3
    out[0:half, :] = matrix[half : 2 * half, 0 : 2 * half]
    out[half : 2 * half, :] = matrix[2 * half :, 0 : 2 * half]
    out[2 * half : 3 * half, :] = jnp.concatenate(
        [matrix[0:half, 0:half], matrix[2 * half :, 2 * half :]], axis=1
    )


def unpack_symmetric(packed):
    third = packed.shape[0] // 3
    row1 = packed[0:third]
    row2 = packed[third : 2 * third]
    ends = packed[2 * third :]
    b10, b11 = row1[:, :third], row1[:, third:]
    b20, b21 = row2[:, :third], row2[:, third:]
    b00, b22 = ends[:, :third], ends[:, third:]
    return jnp.concatenate(
        [
            jnp.concatenate([b00, b10.T, b20.T], axis=1),
            jnp.concatenate([b10, b11, b21.T], axis=1),
            jnp.concatenate([b20, b21, b22], axis=1),
        ],
        axis=0,
    )


def place():
    slab, slabs = lax.axis_index("slab"), lax.axis_size("slab")
    left = slab < slabs // 2
    return slab, left, jnp.where(left, slab, slabs - 1 - slab)


def take_message(message, couple, left, transform_left, block, column):
    width = block.shape[0]
    block[...] = unpack_symmetric(message[0:width, :])
    column[...] = message[width : 2 * width, :]

    @pl.when(left if transform_left else jnp.logical_not(left))
    def _():
        own = couple[0]
        term = dot3(own, dot3(block[...], own.T))
        column[...] = dot3(own, column[...])
        block[...] = term


def stage_kernel(step, energy, diag, couple, probes, *rest):
    if step > 0:
        message, rest = rest[0], rest[1:]
    factor_p, value_p, inverse_p, matrix_q, source_q, inverse_q, value_q, out, hold, column = rest
    _, left, distance = place()
    centre = lax.axis_size("slab") // 2 - 1
    forward = jnp.logical_and(left, distance < centre)
    first = jnp.where(forward, 0, 1)
    width = diag.shape[1]
    shift = sigma_base + sigma_step * jnp.full((1, 1), energy[0], jnp.int32).astype(F32)
    shifted = shift * eye(width)
    sp = diag[first] + shifted
    rp = probes[pl.ds(pl.multiple_of(first * width, width), width), :]
    rq = probes[pl.ds(pl.multiple_of((1 - first) * width, width), width), :]
    if step > 0:
        taken = jnp.logical_and(distance >= 1, distance <= step)
        take_message(message, couple, left, True, matrix_q, source_q)
        sp = sp - jnp.where(taken, matrix_q[...], 0.0)
        rp = rp - jnp.where(taken, source_q[...], 0.0)
    inner = couple[1]
    inner_t = inner.T
    apq = jnp.where(forward, inner_t, inner)
    aqp = jnp.where(forward, inner, inner_t)
    xp = invert(sp, hold, 1 / 16, 4)
    inverse_p[...] = xp
    fp = dot3(xp, apq)
    yp = dot3(xp, rp)
    factor_p[...] = fp
    value_p[...] = yp
    sq = diag[1 - first] + shifted - dot3(aqp, fp)
    rq = rq - dot3(aqp, yp)
    matrix_q[...] = sq
    source_q[...] = rq

    @pl.when(distance < centre)
    def _():
        xq = invert(sq, hold, 1 / 16, 4)
        yq = dot3(xq, rq)
        inverse_q[...] = xq
        value_q[...] = yq

        @pl.when(left)
        def _():
            pack_symmetric(xq, out)
            out[width : 2 * width, :] = yq

        @pl.when(jnp.logical_not(left))
        def _():
            own = couple[0]
            own_t = own.T
            pack_symmetric(dot3(own_t, dot3(xq, own)), out)
            out[width : 2 * width, :] = dot3(own_t, yq)


def ready_kernel(energy, diag, couple, probes, following, factor_p, value_p, inverse_p, matrix_q,
                 source_q, matrix, source, link, base, base_source, reach):
    slab, left, distance = place()
    half = lax.axis_size("slab") // 2
    width = diag.shape[1]

    @pl.when(slab == half - 1)
    def _():
        ahead = following[...]
        across = dot3(inverse_p[...], ahead.T)
        reach[...] = across
        matrix[...] = matrix_q[...]
        source[...] = source_q[...]
        link[...] = dot3(couple[1].T, across)
        base[...] = dot3(ahead, across)
        base_source[...] = dot3(ahead, value_p[...])

    @pl.when(slab == half)
    def _():
        shift = sigma_base + sigma_step * jnp.full((1, 1), energy[0], jnp.int32).astype(F32)
        shifted = shift * eye(width)
        matrix[...] = diag[1] + shifted
        source[...] = probes[width : 2 * width, :]
        link[...] = couple[1]
        base[...] = diag[0] + shifted
        base_source[...] = probes[0:width, :]


def centre_kernel(couple, message, matrix, source, link, base, base_source, factor, value,
                  total, total_source, out, hold, block, column):
    slab, left, distance = place()
    half = lax.axis_size("slab") // 2
    width = matrix.shape[0]

    @pl.when(jnp.logical_or(slab == half - 1, slab == half))
    def _():
        take_message(message, couple, left, True, block, column)
        solved = invert(matrix[...] - block[...], hold, 1 / 16, 4)
        right_side = source[...] - column[...]
        near = link[...]
        near_t = near.T
        reach = dot3(solved, near)
        found = dot3(solved, right_side)
        factor[...] = reach
        value[...] = found
        sign = jnp.where(left, 1.0, -1.0)
        both = base[...] + sign * dot3(near_t, reach)
        both_source = base_source[...] - dot3(near_t, found)
        total[...] = both
        total_source[...] = both_source
        pack_symmetric(both, out)
        out[width : 2 * width, :] = both_source


def join_kernel(couple, message, total, total_source, factor, value, out_first, out_middle, out,
                hold):
    slab, left, distance = place()
    half = lax.axis_size("slab") // 2
    width = total.shape[0]

    @pl.when(jnp.logical_or(slab == half - 1, slab == half))
    def _():
        sign = jnp.where(left, 1.0, -1.0)
        matrix = sign * (unpack_symmetric(message[0:width, :]) - total[...])
        right_side = sign * (message[width : 2 * width, :] - total_source[...])
        middle = dot3(invert(matrix, hold, 1 / 64, 5), right_side)
        first = value[...] + sign * dot3(factor[...], middle)
        out_first[...] = first
        out_middle[...] = middle
        out[...] = first

        @pl.when(left)
        def _():
            out[...] = dot3(couple[0].T, first)


def back_kernel(step, cells, couple, probes, message, first, middle, known_p, known_q, factor_p,
                value_p, inverse_q, value_q, reach, out_p, out_q, out, dens):
    slab, left, distance = place()
    centre = lax.axis_size("slab") // 2 - 1
    width = couple.shape[1]

    @pl.when(jnp.logical_and(distance < centre, distance != step))
    def _():
        out_p[...] = known_p[...]
        out_q[...] = known_q[...]

    @pl.when(distance == step)
    def _():
        out_q[...] = message[...]

        @pl.when(jnp.logical_not(left))
        def _():
            out_q[...] = dot3(couple[0], message[...])

        xq = value_q[...] - dot3(inverse_q[...], out_q[...])
        out_q[...] = xq
        out_p[...] = value_p[...] - dot3(factor_p[...], xq)

    @pl.when(jnp.logical_and(distance == centre, left))
    def _():
        xa = first[...]
        out_p[...] = xa
        out_q[...] = value_p[...] - dot3(factor_p[...], xa) - dot3(reach[...], middle[...])

    @pl.when(jnp.logical_and(distance == centre, jnp.logical_not(left)))
    def _():
        out_p[...] = first[...]
        out_q[...] = middle[...]

    xp = out_p[...]
    xq = out_q[...]
    out[...] = xp

    if step > 0:

        @pl.when(left)
        def _():
            out[...] = dot3(couple[0].T, xp)

    xa = jnp.where(left, xp, xq)
    xb = jnp.where(left, xq, xp)
    terms = jnp.concatenate([probes[0:width, :] * xa, probes[width:, :] * xb], axis=0)
    dens[...] = dot6(jnp.ones((8, terms.shape[1]), F32), terms, NT)


def total_kernel(scale, cells, *rest):
    parts, out = rest[:-1], rest[-1]
    total = parts[0][0:1, :]
    for part in parts[1:]:
        total = total + part[0:1, :]
    out[0:1, :] = total * scale
    out[1:2, :] = cells[...].astype(F32)


def poisson_kernel(rows_all, planes, packet, near, far, dopants, around, out):
    slab, slabs = lax.axis_index("slab"), lax.axis_size("slab")
    depth, pitch, across = around.shape
    total = depth * pitch
    first_z = slab * out.shape[0] - SWEEPS
    first_x = lax.axis_index("energy") * out.shape[1] - SWEEPS
    plane = rows_all * across

    def spots(index):
        z = index // plane - first_z
        x = index // across % rows_all - first_x
        y = index % across
        inside = (z >= 0) & (z < depth) & (x >= 0) & (x < pitch)
        row = jnp.where(inside, z * pitch + x, -1)
        n = index.shape[1]
        pick_row = lax.broadcasted_iota(jnp.int32, (total, n), 0) == row
        pick_y = lax.broadcasted_iota(jnp.int32, (across, n), 0) == y
        return pick_row.astype(F32).astype(BF16), pick_y.astype(F32)

    rows, ys = spots(dopants[...])
    dopant = dopant_charge * one_pass(rows, ys.astype(BF16), NT)
    alone = jnp.logical_or(slab == 0, slab == slabs - 1)
    lonely = jnp.where(alone, 0.0, far[0:1, :])
    weights = jnp.concatenate([packet[0:1, :], near[0:1, :], lonely], axis=1)
    orbitals = jnp.concatenate([packet[1:2, :], near[1:2, :], far[1:2, :]], axis=1)
    rows, ys = spots(orbitals.astype(jnp.int32))
    spread = ys * weights
    h = spread.astype(BF16)
    rest = spread - h.astype(F32)
    m = rest.astype(BF16)
    low = (rest - m.astype(F32)).astype(BF16)
    electron = one_pass(rows, h, NT) + (one_pass(rows, m, NT) + one_pass(rows, low, NT))
    electron = electron.reshape(depth, pitch, across)
    dopant = dopant.reshape(depth, pitch, across)
    start = around[...]
    zs = lax.broadcasted_iota(jnp.int32, start.shape, 0) + first_z
    xs = lax.broadcasted_iota(jnp.int32, start.shape, 1) + first_x
    ys = lax.broadcasted_iota(jnp.int32, start.shape, 2)
    exists = (zs >= 0) & (zs < planes) & (xs >= 0) & (xs < rows_all)
    potential = jnp.where(exists, start, 0.0)
    start = potential
    strength = coupling_beta * jnp.abs(electron)
    for _ in range(SWEEPS):
        blank = jnp.zeros((1, pitch, across), F32)
        beside = jnp.concatenate([potential[1:], blank], axis=0)
        beside = beside + jnp.concatenate([blank, potential[:-1]], axis=0)
        beside = beside + pltpu.roll(potential, 1, 1) + pltpu.roll(potential, pitch - 1, 1)
        beside = beside + jnp.where(ys > 0, pltpu.roll(potential, 1, 2), 0.0)
        beside = beside + jnp.where(ys < across - 1, pltpu.roll(potential, across - 1, 2), 0.0)
        growth = jnp.exp(potential - start)
        residual = beside - 6.0 * potential + coupling_beta * (dopant - electron * growth)
        potential = potential + residual / (6.0 + strength * growth)
        potential = jnp.where(exists, potential, 0.0)
    halo = SWEEPS
    out[...] = potential[halo : halo + out.shape[0], halo : halo + out.shape[1], :]


VM = pl.BlockSpec(memory_space=pltpu.VMEM)
SM = pl.BlockSpec(memory_space=pltpu.SMEM)
GRANT = 16 << 20


def like(*shape, dtype=F32):
    return jax.ShapeDtypeStruct(shape, dtype)


def call(kernel, name, outs, args, scratch=(), scalars=0, flops=10**8):
    return pl.pallas_call(
        kernel,
        out_shape=outs,
        in_specs=[SM] * scalars + [VM] * (len(args) - scalars),
        out_specs=jax.tree.map(lambda _: VM, outs),
        scratch_shapes=[pltpu.VMEM(shape, F32) for shape in scratch],
        compiler_params=pltpu.CompilerParams(vmem_limit_bytes=GRANT),
        cost_estimate=pl.CostEstimate(flops=flops, bytes_accessed=10**6, transcendentals=0),
        name=name,
    )(*args)


def pairs_of(count, odd):
    found = []
    for first in range(1 if odd else 0, count - 1, 2):
        found += [(first, first + 1), (first + 1, first)]
    return found


def slab_exchange(value, odd):
    slabs, energies = lax.axis_size("slab"), lax.axis_size("energy")
    pairs = pairs_of(slabs, odd)
    busy = {a for a, _ in pairs}
    whole = [(a * energies + e, b * energies + e) for a, b in pairs for e in range(energies)]
    for a in range(slabs):
        if a not in busy:
            whole += [(a * energies + e, a * energies + (e ^ 1)) for e in range(energies)]
    return lax.ppermute(value, ("slab", "energy"), whole)


def energy_exchange(value, odd):
    energies = lax.axis_size("energy")
    pairs = pairs_of(energies, odd)
    if odd:
        pairs += [(energies - 1, 0), (0, energies - 1)]
    return lax.ppermute(value, "energy", pairs)


def body(energy_index, diag_blocks, couple, probes, orbital_cell, dopant_cells, initial_potential):
    width = diag_blocks.shape[1]
    probe_count = probes.shape[1]
    slab, slabs = lax.axis_index("slab"), lax.axis_size("slab")
    energy, energies = lax.axis_index("energy"), lax.axis_size("energy")
    half = slabs // 2
    square, column = like(width, width), like(width, probe_count)
    letter = like(2 * width, probe_count)
    sq, col = (width, width), (width, probe_count)

    following = lax.ppermute(couple[0], "slab", [(s + 1, s) for s in range(half - 1, half)])

    message = None
    for t in range(half - 1):
        args = [energy_index, diag_blocks, couple, probes]
        if t > 0:
            if t > 1:
                _, _, distance = place()
                message = jnp.where(distance == t, message, kept)
            kept = message
            args.append(message)
        state = call(
            functools.partial(stage_kernel, t), f"stage{t}",
            (square, column, square, square, column, square, column, letter),
            args, (sq, col), 1,
        )
        if t == 0:
            prepared = state
        message = slab_exchange(state[-1], t % 2 == 1)
    factor_p, value_p, _, _, _, inverse_q, value_q, _ = state
    matrix, source, link, base, base_source, reach = call(
        ready_kernel, "ready", (square, column, square, square, column, square),
        [energy_index, diag_blocks, couple, probes, following, *prepared[:5]], (), 1,
    )
    factor, value, total, total_source, sent = call(
        centre_kernel, "centre", (square, column, square, column, letter),
        [couple, message, matrix, source, link, base, base_source], (sq, sq, col),
    )
    message = slab_exchange(sent, half % 2 == 0)
    first, middle, sent = call(
        join_kernel, "join", (column, column, column),
        [couple, message, total, total_source, factor, value], (sq,),
    )
    cells_here = orbital_cell.reshape(1, -1)
    centred = lax.axis_index("slab") == half - 1
    if half > 2:
        factor_p = jnp.where(centred, prepared[0], factor_p)
        value_p = jnp.where(centred, prepared[1], value_p)
    known_p, known_q = first, middle
    for t in range(half - 2, -1, -1):
        message = slab_exchange(sent, t % 2 == 1)
        known_p, known_q, sent, dens = call(
            functools.partial(back_kernel, t), f"back{t}",
            (column, column, column, like(8, 2 * width)),
            [cells_here, couple, probes, message, first, middle, known_p, known_q, factor_p,
             value_p, inverse_q, value_q, reach],
        )
    parts = [dens] + [
        lax.ppermute(dens, "energy", [(e, e ^ k) for e in range(energies)])
        for k in range(1, energies)
    ]
    packet = call(
        functools.partial(total_kernel, 1.0 / (probe_count * energies)), "total",
        like(8, 2 * width), [cells_here, *parts],
    )
    density = packet[0]
    near = slab_exchange(packet, False)
    far = slab_exchange(packet, True)

    depth, rows_here, across = initial_potential.shape
    halo = SWEEPS
    odd_e = energy % 2 == 1
    low, high = initial_potential[:, :halo], initial_potential[:, rows_here - halo :]
    got_even = energy_exchange(jnp.where(odd_e, low, high), False)
    got_odd = energy_exchange(jnp.where(odd_e, high, low), True)
    below = jnp.where(odd_e, got_even, got_odd)
    above = jnp.where(odd_e, got_odd, got_even)
    wide = jnp.concatenate([below, initial_potential, above], axis=1)
    odd_s = slab % 2 == 1
    low, high = wide[:halo], wide[depth - halo :]
    got_even = slab_exchange(jnp.where(odd_s, low, high), False)
    got_odd = slab_exchange(jnp.where(odd_s, high, low), True)
    below = jnp.where(odd_s, got_even, got_odd)
    above = jnp.where(odd_s, got_odd, got_even)
    region = jnp.concatenate([below, wide, above], axis=0)
    pitch = -(-region.shape[1] // 8) * 8
    region = jnp.pad(region, ((0, 0), (0, pitch - region.shape[1]), (0, 0)))
    rows_all = rows_here * energies
    potential = call(
        functools.partial(poisson_kernel, rows_all, depth * slabs), "poisson",
        like(depth, rows_here, across),
        [packet, near, far, dopant_cells.reshape(1, -1), region],
    )
    return (potential, density)


def solution(mesh):
    placed = (
        P("energy"),
        P(("cfg", "slab"), None, None),
        P(("cfg", "slab"), None, None),
        P("slab", None),
        P("slab"),
        P("cfg"),
        P(("cfg", "slab"), "energy", None),
    )
    return jax.shard_map(
        body,
        mesh=mesh,
        in_specs=placed,
        out_specs=(P(("cfg", "slab"), "energy", None), P(("cfg", "slab"))),
        check_vma=False,
    )
```

```python
import functools

import jax
import jax.numpy as jnp
from jax import lax
from jax.experimental import pallas as pl
from jax.experimental.pallas import tpu as pltpu
from jax.sharding import PartitionSpec as P

SWEEPS = 2

sigma_base = 0.02
sigma_step = 0.01
coupling_beta = 0.5
dopant_charge = 4.0

F32 = jnp.float32
BF16 = jnp.bfloat16
NT = (((1,), (1,)), ((), ()))
NN = (((1,), (0,)), ((), ()))


def split2(a):
    high = a.astype(BF16)
    return high, (a - high.astype(F32)).astype(BF16)


def one_pass(a, b, dims=NN):
    return lax.dot_general(a, b, dims, preferred_element_type=F32)


def dot3(a, b):
    ah, al = split2(a)
    bh, bl = split2(b)
    return one_pass(ah, bh) + (one_pass(ah, bl) + one_pass(al, bh))


def dot6(a, b, dims=NN):
    return lax.dot_general(
        a, b, dims, precision=lax.Precision.HIGHEST, preferred_element_type=F32
    )


def eye(n):
    return (
        lax.broadcasted_iota(jnp.int32, (n, n), 0) == lax.broadcasted_iota(jnp.int32, (n, n), 1)
    ).astype(F32)


def invert(matrix, hold, ratio, doublings):
    unit = eye(matrix.shape[0])
    sums = jnp.sum(jnp.abs(matrix), axis=0, keepdims=True)
    bound = jnp.max(sums, axis=1, keepdims=True)
    first = 2.0 / (bound * (1.0 + ratio))
    error = unit - first * matrix
    guess = first * unit
    tau = (1.0 + ratio) / (1.0 - ratio)
    for k in range(doublings):
        after = 2.0 * tau * tau - 1.0
        scale = (after + 1.0) / after
        if k == 0:
            grown = guess + first * error
        else:
            grown = guess + dot3(guess, error)
        if k + 1 < doublings:
            error = scale * dot3(error, error) - (scale - 1.0) * unit
        guess = scale * grown
        tau = after
    residual = unit - dot6(matrix, guess)
    size = jnp.sum(residual * residual)
    hold[...] = guess + dot3(guess, residual)

    @pl.when(jnp.logical_not(size < 0.9))
    def _():
        hold[...] = first * unit

    def go_on(state):
        count, last = state
        return jnp.logical_and(count < 64, jnp.logical_not(last < 1e-5))

    def newton(state):
        count, _ = state
        now = hold[...]
        left = unit - dot6(matrix, now)
        hold[...] = now + dot6(now, left)
        return count + 1, jnp.sum(left * left)

    lax.while_loop(go_on, newton, (jnp.int32(0), size))
    return hold[...]


def pack_symmetric(matrix, out):
    half = matrix.shape[0] // 3
    out[0:half, :] = matrix[half : 2 * half, 0 : 2 * half]
    out[half : 2 * half, :] = matrix[2 * half :, 0 : 2 * half]
    out[2 * half : 3 * half, :] = jnp.concatenate(
        [matrix[0:half, 0:half], matrix[2 * half :, 2 * half :]], axis=1
    )


def unpack_symmetric(packed):
    third = packed.shape[0] // 3
    row1 = packed[0:third]
    row2 = packed[third : 2 * third]
    ends = packed[2 * third :]
    b10, b11 = row1[:, :third], row1[:, third:]
    b20, b21 = row2[:, :third], row2[:, third:]
    b00, b22 = ends[:, :third], ends[:, third:]
    return jnp.concatenate(
        [
            jnp.concatenate([b00, b10.T, b20.T], axis=1),
            jnp.concatenate([b10, b11, b21.T], axis=1),
            jnp.concatenate([b20, b21, b22], axis=1),
        ],
        axis=0,
    )


def place():
    slab, slabs = lax.axis_index("slab"), lax.axis_size("slab")
    left = slab < slabs // 2
    return slab, left, jnp.where(left, slab, slabs - 1 - slab)


def take_message(message, couple, following, left, block, column):
    width = block.shape[0]
    link = jnp.where(left, couple[0], following[...].T)
    link_t = jnp.where(left, couple[0].T, following[...])
    block[...] = dot3(link, dot3(unpack_symmetric(message[0:width, :]), link_t))
    column[...] = dot3(link, message[width : 2 * width, :])


def stage_kernel(step, energy, diag, couple, probes, *rest):
    if step > 0:
        message, following, rest = rest[0], rest[1], rest[2:]
    factor_p, value_p, inverse_p, matrix_q, source_q, inverse_q, value_q, out, hold = rest
    _, left, distance = place()
    centre = lax.axis_size("slab") // 2 - 1
    forward = jnp.logical_and(left, distance < centre)
    first = jnp.where(forward, 0, 1)
    width = diag.shape[1]
    shift = sigma_base + sigma_step * jnp.full((1, 1), energy[0], jnp.int32).astype(F32)
    shifted = shift * eye(width)
    sp = diag[first] + shifted
    rp = probes[pl.ds(pl.multiple_of(first * width, width), width), :]
    rq = probes[pl.ds(pl.multiple_of((1 - first) * width, width), width), :]
    if step > 0:
        taken = jnp.logical_and(distance >= 1, distance <= step)
        take_message(message, couple, following, left, matrix_q, source_q)
        sp = sp - jnp.where(taken, matrix_q[...], 0.0)
        rp = rp - jnp.where(taken, source_q[...], 0.0)
    inner = couple[1]
    inner_t = inner.T
    apq = jnp.where(forward, inner_t, inner)
    aqp = jnp.where(forward, inner, inner_t)
    xp = invert(sp, hold, 1 / 16, 4)
    inverse_p[...] = xp
    fp = dot3(xp, apq)
    yp = dot3(xp, rp)
    factor_p[...] = fp
    value_p[...] = yp
    sq = diag[1 - first] + shifted - dot3(aqp, fp)
    rq = rq - dot3(aqp, yp)
    matrix_q[...] = sq
    source_q[...] = rq

    @pl.when(distance < centre)
    def _():
        xq = invert(sq, hold, 1 / 16, 4)
        yq = dot3(xq, rq)
        inverse_q[...] = xq
        value_q[...] = yq

        pack_symmetric(xq, out)
        out[width : 2 * width, :] = yq


def pack_full(matrix, out):
    n = matrix.shape[0]
    lanes = out.shape[1]
    out[0:n, :] = matrix[:, 0:lanes]
    out[n : n + n // 2, :] = jnp.concatenate(
        [matrix[0 : n // 2, lanes:], matrix[n // 2 :, lanes:]], axis=1
    )


def unpack_full(packed, n):
    rest = packed[n : n + n // 2]
    lanes = packed.shape[1]
    tail = jnp.concatenate([rest[:, : n - lanes], rest[:, n - lanes :]], axis=0)
    return jnp.concatenate([packed[0:n], tail], axis=1)


def spots(index, rows_all, depth, pitch, across, first_z, first_x):
    plane = rows_all * across
    z = index // plane - first_z
    x = index // across % rows_all - first_x
    y = index % across
    inside = (z >= 0) & (z < depth) & (x >= 0) & (x < pitch)
    row = jnp.where(inside, z * pitch + x, -1)
    n = index.shape[1]
    pick_row = lax.broadcasted_iota(jnp.int32, (depth * pitch, n), 0) == row
    pick_y = lax.broadcasted_iota(jnp.int32, (across, n), 0) == y
    return pick_row.astype(F32).astype(BF16), pick_y.astype(F32)


def region_start(depth_here, rows_here):
    first_z = lax.axis_index("slab") * depth_here - SWEEPS
    return first_z, lax.axis_index("energy") * rows_here - SWEEPS


def ready_kernel(rows_all, energy, diag, couple, probes, following, dopants, potential, got_even,
                 got_odd, factor_p, value_p, inverse_p, matrix_q, source_q, matrix, source, link,
                 base, base_source, reach, out, wide, dopant):
    slab, left, distance = place()
    half = lax.axis_size("slab") // 2
    width = diag.shape[1]
    packed = width + width // 2

    @pl.when(slab == half - 1)
    def _():
        ahead = following[...]
        across = dot3(inverse_p[...], ahead.T)
        reach[...] = across
        matrix[...] = matrix_q[...]
        source[...] = source_q[...]
        link[...] = dot3(couple[1].T, across)
        base[...] = dot3(ahead, across)
        base_source[...] = dot3(ahead, value_p[...])

    @pl.when(slab == half)
    def _():
        shift = sigma_base + sigma_step * jnp.full((1, 1), energy[0], jnp.int32).astype(F32)
        shifted = shift * eye(width)
        matrix[...] = diag[1] + shifted
        source[...] = probes[width : 2 * width, :]
        link[...] = couple[1]
        base[...] = diag[0] + shifted
        base_source[...] = probes[0:width, :]

    @pl.when(distance < half - 1)
    def _():
        pack_full(factor_p[...], out)
        out[packed : packed + width, :] = value_p[...]

    depth, rows_here, across = potential.shape
    even_e = lax.axis_index("energy") % 2 == 0
    below = jnp.where(even_e, got_odd[...], got_even[...])
    above = jnp.where(even_e, got_even[...], got_odd[...])
    spare = wide.shape[1] - rows_here - 2 * SWEEPS
    parts = [below, potential[...], above]
    if spare > 0:
        parts.append(jnp.zeros((depth, spare, across), F32))
    wide[...] = jnp.concatenate(parts, axis=1)
    put_planes(out, packed + width, wide, slab % 2 == 0)
    first_z, first_x = region_start(depth, rows_here)
    rows, ys = spots(dopants[...], rows_all, depth + 2 * SWEEPS, wide.shape[1], across, first_z,
                     first_x)
    dopant[...] = dopant_charge * one_pass(rows, ys.astype(BF16), NT)


def put_planes(out, start, wide, high):
    pitch = wide.shape[1]
    last = wide.shape[0] - SWEEPS
    for k in range(SWEEPS):
        plane = jnp.where(high, wide[last + k], wide[k])
        out[start + k * pitch : start + (k + 1) * pitch, :] = plane


def centre_kernel(couple, following, message, matrix, source, link, base, base_source, wide,
                  factor, value, total, total_source, out, hold, block, column):
    slab, left, distance = place()
    half = lax.axis_size("slab") // 2
    width = matrix.shape[0]
    put_planes(out, 2 * width, wide, slab % 2 == 1)

    @pl.when(jnp.logical_or(slab == half - 1, slab == half))
    def _():
        take_message(message, couple, following, left, block, column)
        solved = invert(matrix[...] - block[...], hold, 1 / 16, 4)
        right_side = source[...] - column[...]
        near = link[...]
        near_t = near.T
        reach = dot3(solved, near)
        found = dot3(solved, right_side)
        factor[...] = reach
        value[...] = found
        sign = jnp.where(left, 1.0, -1.0)
        both = base[...] + sign * dot3(near_t, reach)
        both_source = base_source[...] - dot3(near_t, found)
        total[...] = both
        total_source[...] = both_source
        pack_symmetric(both, out)
        out[width : 2 * width, :] = both_source


def expand_kernel(couple, following, probes, probes_near, letter, second, factor, value, factor_p,
                  value_p, reach, slope, offset, weights):
    slab, left, distance = place()
    half = lax.axis_size("slab") // 2
    width = value.shape[0]
    packed = width + width // 2

    def put(block, m, v):
        at = pl.ds(pl.multiple_of(block * width, width), width)
        slope[at, :] = m
        offset[at, :] = v

    @pl.when(jnp.logical_or(slab == half - 1, slab == half))
    def _():
        own = jnp.where(left, 0, 1)
        sign = jnp.where(left, 1.0, -1.0)
        m1 = sign * factor[...]
        v1 = value[...]
        put(own, m1, v1)

        @pl.when(left)
        def _():
            put(1, -(dot3(factor_p[...], m1) + reach[...]), value_p[...] - dot3(factor_p[...], v1))

        @pl.when(jnp.logical_not(left))
        def _():
            put(0, eye(width), jnp.zeros_like(v1))

        link = jnp.where(left, couple[0].T, following[...])
        carry = dot3(unpack_symmetric(letter[0:width, :]), link)
        mq = -dot3(carry, m1)
        vq = letter[width : 2 * width, :] - dot3(carry, v1)
        put(jnp.where(left, 3, 2), mq, vq)
        outer = unpack_full(second[0:packed, :], width)
        put(jnp.where(left, 2, 3), -dot3(outer, mq),
            second[packed : packed + width, :] - dot3(outer, vq))
        weights[0 : 2 * width, :] = probes[...]
        weights[2 * width :, :] = probes_near[...]


def join_middle(message, total, total_source, hold, left):
    width = total.shape[0]
    sign = jnp.where(left, 1.0, -1.0)
    matrix = sign * (unpack_symmetric(message[0:width, :]) - total[...])
    right_side = sign * (message[width : 2 * width, :] - total_source[...])
    return dot3(invert(matrix, hold, 1 / 64, 5), right_side)


def join_pair_kernel(message, total, total_source, slope, offset, weights, dens, hold):
    slab, left, distance = place()
    half = lax.axis_size("slab") // 2

    @pl.when(jnp.logical_or(slab == half - 1, slab == half))
    def _():
        middle = join_middle(message, total, total_source, hold, left)
        terms = weights[...] * (offset[...] + dot3(slope[...], middle))
        dens[...] = dot6(jnp.ones((8, terms.shape[1]), F32), terms, NT)


def join_kernel(message, total, total_source, factor, value, out_first, out_middle, hold):
    slab, left, distance = place()
    half = lax.axis_size("slab") // 2

    @pl.when(jnp.logical_or(slab == half - 1, slab == half))
    def _():
        middle = join_middle(message, total, total_source, hold, left)
        sign = jnp.where(left, 1.0, -1.0)
        out_first[...] = value[...] + sign * dot3(factor[...], middle)
        out_middle[...] = middle


def back_kernel(step, couple, following, probes, message, first, middle, known_p, known_q,
                factor_p, value_p, inverse_q, value_q, reach, out_p, out_q, dens):
    slab, left, distance = place()
    centre = lax.axis_size("slab") // 2 - 1
    width = couple.shape[1]

    @pl.when(jnp.logical_and(distance < centre, distance != step))
    def _():
        out_p[...] = known_p[...]
        out_q[...] = known_q[...]

    @pl.when(distance == step)
    def _():
        link = jnp.where(left, following[...].T, couple[0])
        xq = value_q[...] - dot3(inverse_q[...], dot3(link, message[...]))
        out_q[...] = xq
        out_p[...] = value_p[...] - dot3(factor_p[...], xq)

    @pl.when(jnp.logical_and(distance == centre, left))
    def _():
        xa = first[...]
        out_p[...] = xa
        out_q[...] = value_p[...] - dot3(factor_p[...], xa) - dot3(reach[...], middle[...])

    @pl.when(jnp.logical_and(distance == centre, jnp.logical_not(left)))
    def _():
        out_p[...] = first[...]
        out_q[...] = middle[...]

    xp = out_p[...]
    xq = out_q[...]
    xa = jnp.where(left, xp, xq)
    xb = jnp.where(left, xq, xp)
    terms = jnp.concatenate([probes[0:width, :] * xa, probes[width:, :] * xb], axis=0)
    dens[...] = dot6(jnp.ones((8, terms.shape[1]), F32), terms, NT)


def total_kernel(scale, cells, *rest):
    parts, out = rest[:-1], rest[-1]
    total = parts[0][0:1, :]
    for part in parts[1:]:
        total = total + part[0:1, :]
    out[0:1, :] = total * scale
    out[1:2, 0 : cells.shape[1]] = cells[...].astype(F32)


def poisson_kernel(rows_all, planes, paired, packet, near, far, dopant_grid, wide, near_letter,
                   near_at, far_letter, far_at, out, density):
    slab, slabs = lax.axis_index("slab"), lax.axis_size("slab")
    depth, pitch, across = wide.shape
    depth = depth + 2 * SWEEPS
    first_z, first_x = region_start(out.shape[0], out.shape[1])
    n = density.shape[1]
    even = slab % 2 == 0
    alone = jnp.logical_or(slab == 0, slab == slabs - 1)
    own, beside, beyond = packet[0:1, 0:n], near[0:1, 0:n], far[0:1, 0:n]
    if paired:
        own = jnp.where(alone, near[0:1, n : 2 * n], own)
        beside = jnp.where(alone, beside, packet[0:1, n : 2 * n])
    density[...] = own
    weights = jnp.concatenate([own, beside, jnp.where(alone, 0.0, beyond)], axis=1)
    orbitals = jnp.concatenate([packet[1:2, 0:n], near[1:2, 0:n], far[1:2, 0:n]], axis=1)
    orbitals = jnp.where(jnp.abs(orbitals) < 2.0**30, orbitals, -1.0).astype(jnp.int32)
    rows, ys = spots(orbitals, rows_all, depth, pitch, across, first_z, first_x)
    spread = ys * weights
    h = spread.astype(BF16)
    rest = spread - h.astype(F32)
    m = rest.astype(BF16)
    low = (rest - m.astype(F32)).astype(BF16)
    electron = one_pass(rows, h, NT) + (one_pass(rows, m, NT) + one_pass(rows, low, NT))
    electron = electron.reshape(depth, pitch, across)
    dopant = dopant_grid[...].reshape(depth, pitch, across)
    size = SWEEPS * pitch
    near_planes = near_letter[near_at : near_at + size, :].reshape(SWEEPS, pitch, across)
    far_planes = far_letter[far_at : far_at + size, :].reshape(SWEEPS, pitch, across)
    start = jnp.concatenate(
        [jnp.where(even, far_planes, near_planes), wide[...],
         jnp.where(even, near_planes, far_planes)],
        axis=0,
    )
    zs = lax.broadcasted_iota(jnp.int32, start.shape, 0) + first_z
    xs = lax.broadcasted_iota(jnp.int32, start.shape, 1) + first_x
    ys = lax.broadcasted_iota(jnp.int32, start.shape, 2)
    exists = (zs >= 0) & (zs < planes) & (xs >= 0) & (xs < rows_all)
    potential = jnp.where(exists, start, 0.0)
    start = potential
    strength = coupling_beta * jnp.abs(electron)
    for _ in range(SWEEPS):
        blank = jnp.zeros((1, pitch, across), F32)
        beside = jnp.concatenate([potential[1:], blank], axis=0)
        beside = beside + jnp.concatenate([blank, potential[:-1]], axis=0)
        beside = beside + pltpu.roll(potential, 1, 1) + pltpu.roll(potential, pitch - 1, 1)
        beside = beside + jnp.where(ys > 0, pltpu.roll(potential, 1, 2), 0.0)
        beside = beside + jnp.where(ys < across - 1, pltpu.roll(potential, across - 1, 2), 0.0)
        growth = jnp.exp(potential - start)
        residual = beside - 6.0 * potential + coupling_beta * (dopant - electron * growth)
        potential = potential + residual / (6.0 + strength * growth)
        potential = jnp.where(exists, potential, 0.0)
    halo = SWEEPS
    out[...] = potential[halo : halo + out.shape[0], halo : halo + out.shape[1], :]


VM = pl.BlockSpec(memory_space=pltpu.VMEM)
SM = pl.BlockSpec(memory_space=pltpu.SMEM)
GRANT = 16 << 20


def like(*shape, dtype=F32):
    return jax.ShapeDtypeStruct(shape, dtype)


def call(kernel, name, outs, args, scratch=(), scalars=0, flops=10**8):
    return pl.pallas_call(
        kernel,
        out_shape=outs,
        in_specs=[SM] * scalars + [VM] * (len(args) - scalars),
        out_specs=jax.tree.map(lambda _: VM, outs),
        scratch_shapes=[pltpu.VMEM(shape, F32) for shape in scratch],
        compiler_params=pltpu.CompilerParams(vmem_limit_bytes=GRANT),
        cost_estimate=pl.CostEstimate(flops=flops, bytes_accessed=10**6, transcendentals=0),
        name=name,
    )(*args)


def pairs_of(count, odd):
    found = []
    for first in range(1 if odd else 0, count - 1, 2):
        found += [(first, first + 1), (first + 1, first)]
    return found


def slab_exchange(value, odd):
    slabs, energies = lax.axis_size("slab"), lax.axis_size("energy")
    pairs = pairs_of(slabs, odd)
    busy = {a for a, _ in pairs}
    whole = [(a * energies + e, b * energies + e) for a, b in pairs for e in range(energies)]
    for a in range(slabs):
        if a not in busy:
            whole += [(a * energies + e, a * energies + (e ^ 1)) for e in range(energies)]
    return lax.ppermute(value, ("slab", "energy"), whole)


def energy_exchange(value, odd):
    energies = lax.axis_size("energy")
    pairs = pairs_of(energies, odd)
    if odd:
        pairs += [(energies - 1, 0), (0, energies - 1)]
    return lax.ppermute(value, "energy", pairs)


def body(energy_index, diag_blocks, couple, probes, orbital_cell, dopant_cells, initial_potential):
    width = diag_blocks.shape[1]
    probe_count = probes.shape[1]
    slab, slabs = lax.axis_index("slab"), lax.axis_size("slab")
    energy, energies = lax.axis_index("energy"), lax.axis_size("energy")
    half = slabs // 2
    square, column = like(width, width), like(width, probe_count)
    letter = like(2 * width, probe_count)
    sq, col = (width, width), (width, probe_count)

    following = lax.ppermute(couple[0], "slab", [((s + 1) % slabs, s) for s in range(slabs)])
    paired = half == 2
    probes_near = slab_exchange(probes, False) if paired else None

    message = None
    for t in range(half - 1):
        args = [energy_index, diag_blocks, couple, probes]
        if t > 0:
            if t > 1:
                _, _, distance = place()
                message = jnp.where(distance == t, message, kept)
            kept = message
            args += [message, following]
        state = call(
            functools.partial(stage_kernel, t), f"stage{t}",
            (square, column, square, square, column, square, column, letter),
            args, (sq,), 1,
        )
        if t == 0:
            prepared = state
        message = slab_exchange(state[-1], t % 2 == 1)
    factor_p, value_p, _, _, _, inverse_q, value_q, _ = state

    depth, rows_here, across = initial_potential.shape
    halo = SWEEPS
    rows_all = rows_here * energies
    pitch = -(-(rows_here + 2 * halo) // 8) * 8
    strip = halo * pitch
    odd_e = lax.axis_index("energy") % 2 == 1
    low, high = initial_potential[:, :halo], initial_potential[:, rows_here - halo :]
    got_even = energy_exchange(jnp.where(odd_e, low, high), False)
    got_odd = energy_exchange(jnp.where(odd_e, high, low), True)
    packed = width + width // 2
    near_at, far_at = packed + width, 2 * width
    cells = (depth + 2 * halo) * pitch

    matrix, source, link, base, base_source, reach, second, wide, dopant_grid = call(
        functools.partial(ready_kernel, rows_all), "ready",
        (square, column, square, square, column, square, like(near_at + strip, probe_count),
         like(depth, pitch, across), like(cells, across)),
        [energy_index, diag_blocks, couple, probes, following, dopant_cells.reshape(1, -1),
         initial_potential, got_even, got_odd, *prepared[:5]], (), 1,
    )
    message, second = lax.optimization_barrier((message, second))
    second = slab_exchange(second, False)
    factor, value, total, total_source, sent = call(
        centre_kernel, "centre",
        (square, column, square, column, like(far_at + strip, probe_count)),
        [couple, following, message, matrix, source, link, base, base_source, wide],
        (sq, sq, col),
    )
    across_middle = slab_exchange(sent, half % 2 == 0)
    far_letter = across_middle if paired else slab_exchange(sent, True)
    if paired:
        slope, offset, weights = call(
            expand_kernel, "expand",
            (like(4 * width, width), like(4 * width, probe_count), like(4 * width, probe_count)),
            [couple, following, probes, probes_near, message, second, factor, value,
             prepared[0], prepared[1], reach],
        )
        dens = call(
            join_pair_kernel, "join", like(8, 4 * width),
            [across_middle, total, total_source, slope, offset, weights], (sq,),
        )
    else:
        first, middle = call(
            join_kernel, "join", (column, column),
            [across_middle, total, total_source, factor, value], (sq,),
        )
        centred = lax.axis_index("slab") == half - 1
        factor_p = jnp.where(centred, prepared[0], factor_p)
        value_p = jnp.where(centred, prepared[1], value_p)
        known_p, known_q = first, middle
        for t in range(half - 2, -1, -1):
            known_p, known_q, dens = call(
                functools.partial(back_kernel, t), f"back{t}",
                (column, column, like(8, 2 * width)),
                [couple, following, probes, slab_exchange(known_p, t % 2 == 1), first, middle,
                 known_p, known_q, factor_p, value_p, inverse_q, value_q, reach],
            )
    parts = [dens] + [
        lax.ppermute(dens, "energy", [(e, e ^ k) for e in range(energies)])
        for k in range(1, energies)
    ]
    packet = call(
        functools.partial(total_kernel, 1.0 / (probe_count * energies)), "total",
        like(*dens.shape), [orbital_cell.reshape(1, -1), *parts],
    )
    near = slab_exchange(packet, False)
    far = slab_exchange(packet, True)

    def poisson(packet, near, far, dopant_grid, wide, near_letter, far_letter, out, density):
        poisson_kernel(rows_all, depth * slabs, paired, packet, near, far, dopant_grid, wide,
                       near_letter, near_at, far_letter, far_at, out, density)

    potential, density = call(
        poisson, "poisson", (like(depth, rows_here, across), like(1, 2 * width)),
        [packet, near, far, dopant_grid, wide, second, far_letter],
    )
    density = density.reshape(-1)
    return (potential, density)


def solution(mesh):
    placed = (
        P("energy"),
        P(("cfg", "slab"), None, None),
        P(("cfg", "slab"), None, None),
        P("slab", None),
        P("slab"),
        P("cfg"),
        P(("cfg", "slab"), "energy", None),
    )
    return jax.shard_map(
        body,
        mesh=mesh,
        in_specs=placed,
        out_specs=(P(("cfg", "slab"), "energy", None), P(("cfg", "slab"))),
        check_vma=False,
    )
```

```python
import functools

import jax
import jax.numpy as jnp
from jax import lax
from jax.experimental import pallas as pl
from jax.experimental.pallas import tpu as pltpu
from jax.sharding import PartitionSpec as P

SWEEPS = 2

sigma_base = 0.02
sigma_step = 0.01
coupling_beta = 0.5
dopant_charge = 4.0

F32 = jnp.float32
BF16 = jnp.bfloat16
NT = (((1,), (1,)), ((), ()))
NN = (((1,), (0,)), ((), ()))


def split2(a):
    high = a.astype(BF16)
    return high, (a - high.astype(F32)).astype(BF16)


def one_pass(a, b, dims=NN):
    return lax.dot_general(a, b, dims, preferred_element_type=F32)


def dot3(a, b):
    ah, al = split2(a)
    bh, bl = split2(b)
    return one_pass(ah, bh) + (one_pass(ah, bl) + one_pass(al, bh))


def dot6(a, b, dims=NN):
    return lax.dot_general(
        a, b, dims, precision=lax.Precision.HIGHEST, preferred_element_type=F32
    )


def eye(n):
    return (
        lax.broadcasted_iota(jnp.int32, (n, n), 0) == lax.broadcasted_iota(jnp.int32, (n, n), 1)
    ).astype(F32)


def invert(matrix, hold, ratio, doublings):
    unit = eye(matrix.shape[0])
    sums = jnp.sum(jnp.abs(matrix), axis=0, keepdims=True)
    bound = jnp.max(sums, axis=1, keepdims=True)
    first = 2.0 / (bound * (1.0 + ratio))
    error = unit - first * matrix
    guess = first * unit
    tau = (1.0 + ratio) / (1.0 - ratio)
    for k in range(doublings):
        after = 2.0 * tau * tau - 1.0
        scale = (after + 1.0) / after
        if k == 0:
            grown = guess + first * error
        else:
            grown = guess + dot3(guess, error)
        if k + 1 < doublings:
            error = scale * dot3(error, error) - (scale - 1.0) * unit
        guess = scale * grown
        tau = after
    residual = unit - dot6(matrix, guess)
    size = jnp.sum(residual * residual)
    hold[...] = guess + dot3(guess, residual)

    @pl.when(jnp.logical_not(size < 0.9))
    def _():
        hold[...] = first * unit

    def go_on(state):
        count, last = state
        return jnp.logical_and(count < 64, jnp.logical_not(last < 1e-5))

    def newton(state):
        count, _ = state
        now = hold[...]
        left = unit - dot6(matrix, now)
        hold[...] = now + dot6(now, left)
        return count + 1, jnp.sum(left * left)

    lax.while_loop(go_on, newton, (jnp.int32(0), size))
    return hold[...]


def pack_symmetric(matrix, out):
    half = matrix.shape[0] // 3
    out[0:half, :] = matrix[half : 2 * half, 0 : 2 * half]
    out[half : 2 * half, :] = matrix[2 * half :, 0 : 2 * half]
    out[2 * half : 3 * half, :] = jnp.concatenate(
        [matrix[0:half, 0:half], matrix[2 * half :, 2 * half :]], axis=1
    )


def unpack_symmetric(packed):
    third = packed.shape[0] // 3
    row1 = packed[0:third]
    row2 = packed[third : 2 * third]
    ends = packed[2 * third :]
    b10, b11 = row1[:, :third], row1[:, third:]
    b20, b21 = row2[:, :third], row2[:, third:]
    b00, b22 = ends[:, :third], ends[:, third:]
    return jnp.concatenate(
        [
            jnp.concatenate([b00, b10.T, b20.T], axis=1),
            jnp.concatenate([b10, b11, b21.T], axis=1),
            jnp.concatenate([b20, b21, b22], axis=1),
        ],
        axis=0,
    )


def place():
    slab, slabs = lax.axis_index("slab"), lax.axis_size("slab")
    left = slab < slabs // 2
    return slab, left, jnp.where(left, slab, slabs - 1 - slab)


def following(ahead):
    even, odd = ahead
    return jnp.where(lax.axis_index("slab") % 2 == 0, even[0], odd[0])


def take_message(message, couple, ahead, left, block, column):
    width = block.shape[0]
    link_t = jnp.where(left, couple[0].T, following(ahead))
    link = jnp.where(left, couple[0], following(ahead).T)
    block[...] = dot3(link, dot3(unpack_symmetric(message[0:width, :]), link_t))
    column[...] = dot3(link, message[width : 2 * width, :])


def stage_kernel(step, energy, diag_far, couple_far, probes_far, *rest):
    if step > 0:
        message, even, odd, rest = rest[0], rest[1], rest[2], rest[3:]
    factor_p, value_p, inverse_p, matrix_q, source_q, inverse_q, value_q, out = rest[:8]
    hold, diag, couple, probes, sems = rest[8:]
    _, left, distance = place()
    centre = lax.axis_size("slab") // 2 - 1
    forward = jnp.logical_and(left, distance < centre)
    first = jnp.where(forward, 0, 1)
    width = diag.shape[1]
    loads = [
        pltpu.make_async_copy(diag_far.at[first], diag.at[0], sems.at[0]),
        pltpu.make_async_copy(couple_far, couple, sems.at[1]),
        pltpu.make_async_copy(probes_far, probes, sems.at[2]),
        pltpu.make_async_copy(diag_far.at[1 - first], diag.at[1], sems.at[3]),
    ]
    for load in loads:
        load.start()
    loads[0].wait()
    shift = sigma_base + sigma_step * jnp.full((1, 1), energy[0], jnp.int32).astype(F32)
    shifted = shift * eye(width)
    sp = diag[0] + shifted
    if step > 0:
        loads[1].wait()
        taken = jnp.logical_and(distance >= 1, distance <= step)
        take_message(message, couple, (even, odd), left, matrix_q, source_q)
        sp = sp - jnp.where(taken, matrix_q[...], 0.0)
        extra = jnp.where(taken, source_q[...], 0.0)
    xp = invert(sp, hold, 1 / 16, 4)
    inverse_p[...] = xp
    for k in range(2 if step > 0 else 1, 4):
        loads[k].wait()
    rp = probes[pl.ds(pl.multiple_of(first * width, width), width), :]
    rq = probes[pl.ds(pl.multiple_of((1 - first) * width, width), width), :]
    if step > 0:
        rp = rp - extra
    inner = couple[1]
    inner_t = inner.T
    apq = jnp.where(forward, inner_t, inner)
    aqp = jnp.where(forward, inner, inner_t)
    fp = dot3(xp, apq)
    yp = dot3(xp, rp)
    factor_p[...] = fp
    value_p[...] = yp
    sq = diag[1] + shifted - dot3(aqp, fp)
    rq = rq - dot3(aqp, yp)
    matrix_q[...] = sq
    source_q[...] = rq

    @pl.when(distance < centre)
    def _():
        xq = invert(sq, hold, 1 / 16, 4)
        yq = dot3(xq, rq)
        inverse_q[...] = xq
        value_q[...] = yq

        pack_symmetric(xq, out)
        out[width : 2 * width, :] = yq


def pack_full(matrix, out):
    n = matrix.shape[0]
    lanes = out.shape[1]
    out[0:n, :] = matrix[:, 0:lanes]
    out[n : n + n // 2, :] = jnp.concatenate(
        [matrix[0 : n // 2, lanes:], matrix[n // 2 :, lanes:]], axis=1
    )


def unpack_full(packed, n):
    rest = packed[n : n + n // 2]
    lanes = packed.shape[1]
    tail = jnp.concatenate([rest[:, : n - lanes], rest[:, n - lanes :]], axis=0)
    return jnp.concatenate([packed[0:n], tail], axis=1)


def spots(index, rows_all, depth, pitch, across, first_z, first_x):
    plane = rows_all * across
    z = index // plane - first_z
    x = index // across % rows_all - first_x
    y = index % across
    inside = (z >= 0) & (z < depth) & (x >= 0) & (x < pitch)
    row = jnp.where(inside, z * pitch + x, -1)
    n = index.shape[1]
    pick_row = lax.broadcasted_iota(jnp.int32, (depth * pitch, n), 0) == row
    pick_y = lax.broadcasted_iota(jnp.int32, (across, n), 0) == y
    return pick_row.astype(F32).astype(BF16), pick_y.astype(F32)


def region_start(depth_here, rows_here):
    first_z = lax.axis_index("slab") * depth_here - SWEEPS
    return first_z, lax.axis_index("energy") * rows_here - SWEEPS


def ready_kernel(rows_all, energy, diag, couple, probes, even, odd, dopants, potential, got_even,
                 got_odd, factor_p, value_p, inverse_p, matrix_q, source_q, matrix, source, link,
                 base, base_source, reach, out, wide, dopant):
    slab, left, distance = place()
    half = lax.axis_size("slab") // 2
    width = diag.shape[1]
    packed = width + width // 2

    @pl.when(slab == half - 1)
    def _():
        ahead = following((even, odd))
        across = dot3(inverse_p[...], ahead.T)
        reach[...] = across
        matrix[...] = matrix_q[...]
        source[...] = source_q[...]
        link[...] = dot3(couple[1].T, across)
        base[...] = dot3(ahead, across)
        base_source[...] = dot3(ahead, value_p[...])

    @pl.when(slab == half)
    def _():
        shift = sigma_base + sigma_step * jnp.full((1, 1), energy[0], jnp.int32).astype(F32)
        shifted = shift * eye(width)
        matrix[...] = diag[1] + shifted
        source[...] = probes[width : 2 * width, :]
        link[...] = couple[1]
        base[...] = diag[0] + shifted
        base_source[...] = probes[0:width, :]

    @pl.when(distance < half - 1)
    def _():
        pack_full(factor_p[...], out)
        out[packed : packed + width, :] = value_p[...]
        if out.shape[0] > packed + 3 * width:
            out[packed + width : packed + 3 * width, :] = probes[...]

    depth, rows_here, across = potential.shape
    even_e = lax.axis_index("energy") % 2 == 0
    below = jnp.where(even_e, got_odd[...], got_even[...])
    above = jnp.where(even_e, got_even[...], got_odd[...])
    spare = wide.shape[1] - rows_here - 2 * SWEEPS
    parts = [below, potential[...], above]
    if spare > 0:
        parts.append(jnp.zeros((depth, spare, across), F32))
    wide[...] = jnp.concatenate(parts, axis=1)
    put_planes(out, out.shape[0] - SWEEPS * wide.shape[1], wide, slab % 2 == 0)
    first_z, first_x = region_start(depth, rows_here)
    rows, ys = spots(dopants[...], rows_all, depth + 2 * SWEEPS, wide.shape[1], across, first_z,
                     first_x)
    dopant[...] = dopant_charge * one_pass(rows, ys.astype(BF16), NT)


def put_planes(out, start, wide, high):
    pitch = wide.shape[1]
    last = wide.shape[0] - SWEEPS
    for k in range(SWEEPS):
        plane = jnp.where(high, wide[last + k], wide[k])
        out[start + k * pitch : start + (k + 1) * pitch, :] = plane


def centre_kernel(couple, even, odd, message, matrix, source, link, base, base_source, wide,
                  factor, value, total, total_source, out, hold, block, column):
    slab, left, distance = place()
    half = lax.axis_size("slab") // 2
    width = matrix.shape[0]
    put_planes(out, 2 * width, wide, slab % 2 == 1)

    @pl.when(jnp.logical_or(slab == half - 1, slab == half))
    def _():
        take_message(message, couple, (even, odd), left, block, column)
        solved = invert(matrix[...] - block[...], hold, 1 / 16, 4)
        right_side = source[...] - column[...]
        near = link[...]
        near_t = near.T
        reach = dot3(solved, near)
        found = dot3(solved, right_side)
        factor[...] = reach
        value[...] = found
        sign = jnp.where(left, 1.0, -1.0)
        both = base[...] + sign * dot3(near_t, reach)
        both_source = base_source[...] - dot3(near_t, found)
        total[...] = both
        total_source[...] = both_source
        pack_symmetric(both, out)
        out[width : 2 * width, :] = both_source


def expand_kernel(couple, even, odd, probes, letter, second, factor, value, factor_p,
                  value_p, reach, slope, offset, weights):
    slab, left, distance = place()
    half = lax.axis_size("slab") // 2
    width = value.shape[0]
    packed = width + width // 2

    def put(block, m, v):
        at = pl.ds(pl.multiple_of(block * width, width), width)
        slope[at, :] = m
        offset[at, :] = v

    @pl.when(jnp.logical_or(slab == half - 1, slab == half))
    def _():
        own = jnp.where(left, 0, 1)
        sign = jnp.where(left, 1.0, -1.0)
        m1 = sign * factor[...]
        v1 = value[...]
        put(own, m1, v1)

        @pl.when(left)
        def _():
            put(1, -(dot3(factor_p[...], m1) + reach[...]), value_p[...] - dot3(factor_p[...], v1))

        @pl.when(jnp.logical_not(left))
        def _():
            put(0, eye(width), jnp.zeros_like(v1))

        link = jnp.where(left, couple[0].T, following((even, odd)))
        carry = dot3(unpack_symmetric(letter[0:width, :]), link)
        mq = -dot3(carry, m1)
        vq = letter[width : 2 * width, :] - dot3(carry, v1)
        put(jnp.where(left, 3, 2), mq, vq)
        outer = unpack_full(second[0:packed, :], width)
        put(jnp.where(left, 2, 3), -dot3(outer, mq),
            second[packed : packed + width, :] - dot3(outer, vq))
        weights[0 : 2 * width, :] = probes[...]
        weights[2 * width :, :] = second[packed + width : packed + 3 * width, :]


def join_middle(message, total, total_source, hold, left):
    width = total.shape[0]
    sign = jnp.where(left, 1.0, -1.0)
    matrix = sign * (unpack_symmetric(message[0:width, :]) - total[...])
    right_side = sign * (message[width : 2 * width, :] - total_source[...])
    return dot3(invert(matrix, hold, 1 / 64, 5), right_side)


def join_pair_kernel(message, total, total_source, slope, offset, weights, dens, hold):
    slab, left, distance = place()
    half = lax.axis_size("slab") // 2

    @pl.when(jnp.logical_or(slab == half - 1, slab == half))
    def _():
        middle = join_middle(message, total, total_source, hold, left)
        terms = weights[...] * (offset[...] + dot3(slope[...], middle))
        dens[...] = dot6(jnp.ones((8, terms.shape[1]), F32), terms, NT)[0:1]


def join_kernel(message, total, total_source, factor, value, out_first, out_middle, hold):
    slab, left, distance = place()
    half = lax.axis_size("slab") // 2

    @pl.when(jnp.logical_or(slab == half - 1, slab == half))
    def _():
        middle = join_middle(message, total, total_source, hold, left)
        sign = jnp.where(left, 1.0, -1.0)
        out_first[...] = value[...] + sign * dot3(factor[...], middle)
        out_middle[...] = middle


def back_kernel(step, couple, even, odd, probes, message, first, middle, known_p, known_q,
                factor_p, value_p, inverse_q, value_q, reach, out_p, out_q, dens):
    slab, left, distance = place()
    centre = lax.axis_size("slab") // 2 - 1
    width = couple.shape[1]

    @pl.when(jnp.logical_and(distance < centre, distance != step))
    def _():
        out_p[...] = known_p[...]
        out_q[...] = known_q[...]

    @pl.when(distance == step)
    def _():
        link = jnp.where(left, following((even, odd)).T, couple[0])
        xq = value_q[...] - dot3(inverse_q[...], dot3(link, message[...]))
        out_q[...] = xq
        out_p[...] = value_p[...] - dot3(factor_p[...], xq)

    @pl.when(jnp.logical_and(distance == centre, left))
    def _():
        xa = first[...]
        out_p[...] = xa
        out_q[...] = value_p[...] - dot3(factor_p[...], xa) - dot3(reach[...], middle[...])

    @pl.when(jnp.logical_and(distance == centre, jnp.logical_not(left)))
    def _():
        out_p[...] = first[...]
        out_q[...] = middle[...]

    xp = out_p[...]
    xq = out_q[...]
    xa = jnp.where(left, xp, xq)
    xb = jnp.where(left, xq, xp)
    terms = jnp.concatenate([probes[0:width, :] * xa, probes[width:, :] * xb], axis=0)
    dens[...] = dot6(jnp.ones((8, terms.shape[1]), F32), terms, NT)[0:1]


def total_kernel(scale, cells, *rest):
    parts, out = rest[:-1], rest[-1]
    total = parts[0][0:1, :]
    for part in parts[1:]:
        total = total + part[0:1, :]
    out[0:1, :] = total * scale
    out[1:2, 0 : cells.shape[1]] = cells[...].astype(F32)


def poisson_kernel(rows_all, planes, paired, packet, near, far, dopant_grid, wide, near_letter,
                   near_at, far_letter, far_at, out, density):
    slab, slabs = lax.axis_index("slab"), lax.axis_size("slab")
    depth, pitch, across = wide.shape
    depth = depth + 2 * SWEEPS
    first_z, first_x = region_start(out.shape[0], out.shape[1])
    n = density.shape[1]
    even = slab % 2 == 0
    alone = jnp.logical_or(slab == 0, slab == slabs - 1)
    own, beside, beyond = packet[0:1, 0:n], near[0:1, 0:n], far[0:1, 0:n]
    if paired:
        own = jnp.where(alone, near[0:1, n : 2 * n], own)
        beside = jnp.where(alone, beside, packet[0:1, n : 2 * n])
    density[...] = own
    weights = jnp.concatenate([own, beside, jnp.where(alone, 0.0, beyond)], axis=1)
    orbitals = jnp.concatenate([packet[1:2, 0:n], near[1:2, 0:n], far[1:2, 0:n]], axis=1)
    orbitals = jnp.where(jnp.abs(orbitals) < 2.0**30, orbitals, -1.0).astype(jnp.int32)
    rows, ys = spots(orbitals, rows_all, depth, pitch, across, first_z, first_x)
    spread = ys * weights
    h = spread.astype(BF16)
    rest = spread - h.astype(F32)
    m = rest.astype(BF16)
    low = (rest - m.astype(F32)).astype(BF16)
    electron = one_pass(rows, h, NT) + (one_pass(rows, m, NT) + one_pass(rows, low, NT))
    electron = electron.reshape(depth, pitch, across)
    dopant = dopant_grid[...].reshape(depth, pitch, across)
    size = SWEEPS * pitch
    near_planes = near_letter[near_at : near_at + size, :].reshape(SWEEPS, pitch, across)
    far_planes = far_letter[far_at : far_at + size, :].reshape(SWEEPS, pitch, across)
    start = jnp.concatenate(
        [jnp.where(even, far_planes, near_planes), wide[...],
         jnp.where(even, near_planes, far_planes)],
        axis=0,
    )
    zs = lax.broadcasted_iota(jnp.int32, start.shape, 0) + first_z
    xs = lax.broadcasted_iota(jnp.int32, start.shape, 1) + first_x
    ys = lax.broadcasted_iota(jnp.int32, start.shape, 2)
    exists = (zs >= 0) & (zs < planes) & (xs >= 0) & (xs < rows_all)
    potential = jnp.where(exists, start, 0.0)
    start = potential
    strength = coupling_beta * jnp.abs(electron)
    for _ in range(SWEEPS):
        blank = jnp.zeros((1, pitch, across), F32)
        beside = jnp.concatenate([potential[1:], blank], axis=0)
        beside = beside + jnp.concatenate([blank, potential[:-1]], axis=0)
        beside = beside + pltpu.roll(potential, 1, 1) + pltpu.roll(potential, pitch - 1, 1)
        beside = beside + jnp.where(ys > 0, pltpu.roll(potential, 1, 2), 0.0)
        beside = beside + jnp.where(ys < across - 1, pltpu.roll(potential, across - 1, 2), 0.0)
        growth = jnp.exp(potential - start)
        residual = beside - 6.0 * potential + coupling_beta * (dopant - electron * growth)
        potential = potential + residual / (6.0 + strength * growth)
        potential = jnp.where(exists, potential, 0.0)
    halo = SWEEPS
    out[...] = potential[halo : halo + out.shape[0], halo : halo + out.shape[1], :]


VM = pl.BlockSpec(memory_space=pltpu.VMEM)
SM = pl.BlockSpec(memory_space=pltpu.SMEM)
FAR = pl.BlockSpec(memory_space=pltpu.HBM)
GRANT = 16 << 20


def like(*shape, dtype=F32):
    return jax.ShapeDtypeStruct(shape, dtype)


def call(kernel, name, outs, args, scratch=(), scalars=0, distant=0, flops=10**8):
    near = len(args) - scalars - distant
    args = list(args)
    for k in range(scalars, scalars + distant):
        args[k] = pltpu.with_memory_space_constraint(args[k], pltpu.HBM)
    sems = [pltpu.SemaphoreType.DMA((4,))] if distant else []
    return pl.pallas_call(
        kernel,
        out_shape=outs,
        in_specs=[SM] * scalars + [FAR] * distant + [VM] * near,
        out_specs=jax.tree.map(lambda _: VM, outs),
        scratch_shapes=[pltpu.VMEM(shape, F32) for shape in scratch] + sems,
        compiler_params=pltpu.CompilerParams(vmem_limit_bytes=GRANT),
        cost_estimate=pl.CostEstimate(flops=flops, bytes_accessed=10**6, transcendentals=0),
        name=name,
    )(*args)


def pairs_of(count, odd):
    found = []
    for first in range(1 if odd else 0, count - 1, 2):
        found += [(first, first + 1), (first + 1, first)]
    return found


def slab_exchange(value, odd):
    slabs, energies = lax.axis_size("slab"), lax.axis_size("energy")
    pairs = pairs_of(slabs, odd)
    busy = {a for a, _ in pairs}
    whole = [(a * energies + e, b * energies + e) for a, b in pairs for e in range(energies)]
    for a in range(slabs):
        if a not in busy:
            whole += [(a * energies + e, a * energies + (e ^ 1)) for e in range(energies)]
    return lax.ppermute(value, ("slab", "energy"), whole)


def energy_exchange(value, odd):
    energies = lax.axis_size("energy")
    pairs = pairs_of(energies, odd)
    if odd:
        pairs += [(energies - 1, 0), (0, energies - 1)]
    return lax.ppermute(value, "energy", pairs)


def body(energy_index, diag_blocks, couple, probes, orbital_cell, dopant_cells, initial_potential):
    width = diag_blocks.shape[1]
    probe_count = probes.shape[1]
    slab, slabs = lax.axis_index("slab"), lax.axis_size("slab")
    energy, energies = lax.axis_index("energy"), lax.axis_size("energy")
    half = slabs // 2
    square, column = like(width, width), like(width, probe_count)
    letter = like(2 * width, probe_count)
    sq, col = (width, width), (width, probe_count)

    even = slab_exchange(couple, False)
    odd = lax.ppermute(couple, "slab", [(s + 1, s) for s in range(1, slabs - 1, 2)])
    paired = half == 2

    message = None
    for t in range(half - 1):
        args = [energy_index, diag_blocks, couple, probes]
        if t > 0:
            if t > 1:
                _, _, distance = place()
                message = jnp.where(distance == t, message, kept)
            kept = message
            args += [message, even, odd]
        state = call(
            functools.partial(stage_kernel, t), f"stage{t}",
            (square, column, square, square, column, square, column, letter),
            args, (sq, diag_blocks.shape, couple.shape, probes.shape), 1, 3,
        )
        if t == 0:
            prepared = state
        message = slab_exchange(state[-1], t % 2 == 1)
    factor_p, value_p, _, _, _, inverse_q, value_q, _ = state

    depth, rows_here, across = initial_potential.shape
    halo = SWEEPS
    rows_all = rows_here * energies
    pitch = -(-(rows_here + 2 * halo) // 8) * 8
    strip = halo * pitch
    odd_e = lax.axis_index("energy") % 2 == 1
    low, high = initial_potential[:, :halo], initial_potential[:, rows_here - halo :]
    got_even = energy_exchange(jnp.where(odd_e, low, high), False)
    got_odd = energy_exchange(jnp.where(odd_e, high, low), True)
    packed = width + width // 2
    near_at, far_at = packed + (3 if paired else 1) * width, 2 * width
    cells = (depth + 2 * halo) * pitch

    matrix, source, link, base, base_source, reach, second, wide, dopant_grid = call(
        functools.partial(ready_kernel, rows_all), "ready",
        (square, column, square, square, column, square, like(near_at + strip, probe_count),
         like(depth, pitch, across), like(cells, across)),
        [energy_index, diag_blocks, couple, probes, even, odd, dopant_cells.reshape(1, -1),
         initial_potential, got_even, got_odd, *prepared[:5]], (), 1,
    )
    message, second = lax.optimization_barrier((message, second))
    second = slab_exchange(second, False)
    factor, value, total, total_source, sent = call(
        centre_kernel, "centre",
        (square, column, square, column, like(far_at + strip, probe_count)),
        [couple, even, odd, message, matrix, source, link, base, base_source, wide],
        (sq, sq, col),
    )
    across_middle = slab_exchange(sent, half % 2 == 0)
    far_letter = across_middle if paired else slab_exchange(sent, True)
    if paired:
        slope, offset, weights = call(
            expand_kernel, "expand",
            (like(4 * width, width), like(4 * width, probe_count), like(4 * width, probe_count)),
            [couple, even, odd, probes, message, second, factor, value,
             prepared[0], prepared[1], reach],
        )
        dens = call(
            join_pair_kernel, "join", like(1, 4 * width),
            [across_middle, total, total_source, slope, offset, weights], (sq,),
        )
    else:
        first, middle = call(
            join_kernel, "join", (column, column),
            [across_middle, total, total_source, factor, value], (sq,),
        )
        centred = lax.axis_index("slab") == half - 1
        factor_p = jnp.where(centred, prepared[0], factor_p)
        value_p = jnp.where(centred, prepared[1], value_p)
        known_p, known_q = first, middle
        for t in range(half - 2, -1, -1):
            known_p, known_q, dens = call(
                functools.partial(back_kernel, t), f"back{t}",
                (column, column, like(1, 2 * width)),
                [couple, even, odd, probes, slab_exchange(known_p, t % 2 == 1), first, middle,
                 known_p, known_q, factor_p, value_p, inverse_q, value_q, reach],
            )
    parts = [dens] + [
        lax.ppermute(dens, "energy", [(e, e ^ k) for e in range(energies)])
        for k in range(1, energies)
    ]
    packet = call(
        functools.partial(total_kernel, 1.0 / (probe_count * energies)), "total",
        like(2, dens.shape[1]), [orbital_cell.reshape(1, -1), *parts],
    )
    near = slab_exchange(packet, False)
    far = slab_exchange(packet, True)

    def poisson(packet, near, far, dopant_grid, wide, near_letter, far_letter, out, density):
        poisson_kernel(rows_all, depth * slabs, paired, packet, near, far, dopant_grid, wide,
                       near_letter, near_at, far_letter, far_at, out, density)

    potential, density = call(
        poisson, "poisson", (like(depth, rows_here, across), like(1, 2 * width)),
        [packet, near, far, dopant_grid, wide, second, far_letter],
    )
    density = density.reshape(-1)
    return (potential, density)


def solution(mesh):
    placed = (
        P("energy"),
        P(("cfg", "slab"), None, None),
        P(("cfg", "slab"), None, None),
        P("slab", None),
        P("slab"),
        P("cfg"),
        P(("cfg", "slab"), "energy", None),
    )
    return jax.shard_map(
        body,
        mesh=mesh,
        in_specs=placed,
        out_specs=(P(("cfg", "slab"), "energy", None), P(("cfg", "slab"))),
        check_vma=False,
    )
```

```python
import functools

import jax
import jax.numpy as jnp
from jax import lax
from jax.experimental import pallas as pl
from jax.experimental.pallas import tpu as pltpu
from jax.sharding import PartitionSpec as P

SWEEPS = 2

sigma_base = 0.02
sigma_step = 0.01
coupling_beta = 0.5
dopant_charge = 4.0

F32 = jnp.float32
BF16 = jnp.bfloat16
NT = (((1,), (1,)), ((), ()))
NN = (((1,), (0,)), ((), ()))


def split2(a):
    high = a.astype(BF16)
    return high, (a - high.astype(F32)).astype(BF16)


def one_pass(a, b, dims=NN):
    return lax.dot_general(a, b, dims, preferred_element_type=F32)


def dot3(a, b):
    ah, al = split2(a)
    bh, bl = split2(b)
    return one_pass(ah, bh) + (one_pass(ah, bl) + one_pass(al, bh))


def dot6(a, b, dims=NN):
    return lax.dot_general(
        a, b, dims, precision=lax.Precision.HIGHEST, preferred_element_type=F32
    )


def eye(n):
    return (
        lax.broadcasted_iota(jnp.int32, (n, n), 0) == lax.broadcasted_iota(jnp.int32, (n, n), 1)
    ).astype(F32)


def estimate(matrix, ratio, doublings):
    unit = eye(matrix.shape[0])
    square = dot3(matrix, matrix)
    sums = jnp.sum(jnp.abs(square), axis=0, keepdims=True)
    bound = jnp.sqrt(jnp.max(sums, axis=1, keepdims=True))
    first = 2.0 / (bound * (1.0 + ratio))
    tau = (1.0 + ratio) / (1.0 - ratio)
    for k in range(doublings):
        after = 2.0 * tau * tau - 1.0
        scale = (after + 1.0) / after
        if k == 0:
            grown = (2.0 * first) * unit - (first * first) * matrix
            squared = unit - (2.0 * first) * matrix + (first * first) * square
        else:
            grown = guess + dot3(guess, error)
            squared = dot3(error, error) if k + 1 < doublings else None
        guess = scale * grown
        if k + 1 < doublings:
            error = scale * squared - (scale - 1.0) * unit
        tau = after
    residual = unit - dot6(matrix, guess)
    return guess + dot3(guess, residual), jnp.sum(residual * residual), first


def fast(matrix, hold, ratio, doublings):
    found, size, _ = estimate(matrix, ratio, doublings)
    return found, size


def careful(matrix, hold, ratio, doublings):
    unit = eye(matrix.shape[0])
    found, size, first = estimate(matrix, ratio, doublings)
    hold[...] = found

    @pl.when(jnp.logical_not(size < 0.9))
    def _():
        hold[...] = first * unit

    def go_on(state):
        count, last = state
        return jnp.logical_and(count < 64, jnp.logical_not(last < 1e-6))

    def newton(state):
        count, _ = state
        now = hold[...]
        left = unit - dot6(matrix, now)
        hold[...] = now + dot6(now, left)
        return count + 1, jnp.sum(left * left)

    lax.while_loop(go_on, newton, (jnp.int32(0), size))
    return hold[...], size


def guarded(run):
    worst = run(fast)

    @pl.when(jnp.logical_not(worst < 4e-5))
    def _():
        run(careful)


def pack_symmetric(matrix, out):
    half = matrix.shape[0] // 3
    out[0:half, :] = matrix[half : 2 * half, 0 : 2 * half]
    out[half : 2 * half, :] = matrix[2 * half :, 0 : 2 * half]
    out[2 * half : 3 * half, :] = jnp.concatenate(
        [matrix[0:half, 0:half], matrix[2 * half :, 2 * half :]], axis=1
    )


def unpack_symmetric(packed):
    third = packed.shape[0] // 3
    row1 = packed[0:third]
    row2 = packed[third : 2 * third]
    ends = packed[2 * third :]
    b10, b11 = row1[:, :third], row1[:, third:]
    b20, b21 = row2[:, :third], row2[:, third:]
    b00, b22 = ends[:, :third], ends[:, third:]
    return jnp.concatenate(
        [
            jnp.concatenate([b00, b10.T, b20.T], axis=1),
            jnp.concatenate([b10, b11, b21.T], axis=1),
            jnp.concatenate([b20, b21, b22], axis=1),
        ],
        axis=0,
    )


def place():
    slab, slabs = lax.axis_index("slab"), lax.axis_size("slab")
    left = slab < slabs // 2
    return slab, left, jnp.where(left, slab, slabs - 1 - slab)


def following(ahead):
    even, odd = ahead
    return jnp.where(lax.axis_index("slab") % 2 == 0, even[0], odd[0])


def take_message(message, couple, ahead, left, block, column):
    width = block.shape[0]
    link_t = jnp.where(left, couple[0].T, following(ahead))
    link = jnp.where(left, couple[0], following(ahead).T)
    block[...] = dot3(link, dot3(unpack_symmetric(message[0:width, :]), link_t))
    column[...] = dot3(link, message[width : 2 * width, :])


def stage_kernel(step, diag_far, couple_far, probes_far, energy, *rest):
    if step > 0:
        message, even, odd, rest = rest[0], rest[1], rest[2], rest[3:]
    factor_p, value_p, inverse_p, matrix_q, source_q, inverse_q, value_q, out = rest[:8]
    hold, diag, couple, probes, sems = rest[8:]
    _, left, distance = place()
    centre = lax.axis_size("slab") // 2 - 1
    forward = jnp.logical_and(left, distance < centre)
    first = jnp.where(forward, 0, 1)
    width = diag.shape[1]
    loads = [
        pltpu.make_async_copy(diag_far.at[first], diag.at[0], sems.at[0]),
        pltpu.make_async_copy(couple_far, couple, sems.at[1]),
        pltpu.make_async_copy(probes_far, probes, sems.at[2]),
        pltpu.make_async_copy(diag_far.at[1 - first], diag.at[1], sems.at[3]),
    ]
    for load in loads:
        load.start()
    for load in loads:
        load.wait()
    shift = sigma_base + sigma_step * energy[...].astype(F32)
    shifted = shift * eye(width)
    sp = diag[0] + shifted
    rp = probes[pl.ds(pl.multiple_of(first * width, width), width), :]
    rq = probes[pl.ds(pl.multiple_of((1 - first) * width, width), width), :]
    if step > 0:
        taken = jnp.logical_and(distance >= 1, distance <= step)
        take_message(message, couple, (even, odd), left, matrix_q, source_q)
        sp = sp - jnp.where(taken, matrix_q[...], 0.0)
        rp = rp - jnp.where(taken, source_q[...], 0.0)
    inner = couple[1]
    inner_t = inner.T
    apq = jnp.where(forward, inner_t, inner)
    aqp = jnp.where(forward, inner, inner_t)

    def run(invert):
        xp, size_p = invert(sp, hold, 1 / 12, 4)
        inverse_p[...] = xp
        fp = dot3(xp, apq)
        yp = dot3(xp, rp)
        factor_p[...] = fp
        value_p[...] = yp
        sq = diag[1] + shifted - dot3(aqp, fp)
        source = rq - dot3(aqp, yp)
        matrix_q[...] = sq
        source_q[...] = source
        xq, size_q = invert(sq, hold, 1 / 12, 4)
        yq = dot3(xq, source)
        inverse_q[...] = xq
        value_q[...] = yq
        pack_symmetric(xq, out)
        out[width : 2 * width, :] = yq
        return jnp.maximum(size_p, size_q)

    guarded(run)


def pack_full(matrix, out):
    n = matrix.shape[0]
    lanes = out.shape[1]
    out[0:n, :] = matrix[:, 0:lanes]
    out[n : n + n // 2, :] = jnp.concatenate(
        [matrix[0 : n // 2, lanes:], matrix[n // 2 :, lanes:]], axis=1
    )


def unpack_full(packed, n):
    rest = packed[n : n + n // 2]
    lanes = packed.shape[1]
    tail = jnp.concatenate([rest[:, : n - lanes], rest[:, n - lanes :]], axis=0)
    return jnp.concatenate([packed[0:n], tail], axis=1)


def spots(index, rows_all, depth, pitch, across, first_z, first_x):
    plane = rows_all * across
    z = index // plane - first_z
    x = index // across % rows_all - first_x
    y = index % across
    inside = (z >= 0) & (z < depth) & (x >= 0) & (x < pitch)
    row = jnp.where(inside, z * pitch + x, -1)
    n = index.shape[1]
    pick_row = lax.broadcasted_iota(jnp.int32, (depth * pitch, n), 0) == row
    pick_y = lax.broadcasted_iota(jnp.int32, (across, n), 0) == y
    return pick_row.astype(F32).astype(BF16), pick_y.astype(F32)


def region_start(depth_here, rows_here):
    first_z = lax.axis_index("slab") * depth_here - SWEEPS
    return first_z, lax.axis_index("energy") * rows_here - SWEEPS


def ready_kernel(rows_all, energy, diag, couple, probes, probes_near, even, odd, dopants, potential, got_even,
                 got_odd, factor_p, value_p, inverse_p, matrix_q, source_q, matrix, source, link,
                 base, base_source, reach, out, wide, dopant):
    slab, left, distance = place()
    half = lax.axis_size("slab") // 2
    width = diag.shape[1]
    packed = width + width // 2

    @pl.when(slab == half - 1)
    def _():
        ahead = following((even, odd))
        across = dot3(inverse_p[...], ahead.T)
        reach[...] = across
        matrix[...] = matrix_q[...]
        source[...] = source_q[...]
        link[...] = dot3(couple[1].T, across)
        base[...] = dot3(ahead, across)
        base_source[...] = dot3(ahead, value_p[...])

    @pl.when(slab == half)
    def _():
        shift = sigma_base + sigma_step * energy[...].astype(F32)
        shifted = shift * eye(width)
        matrix[...] = diag[1] + shifted
        source[...] = probes[width : 2 * width, :]
        link[...] = couple[1]
        base[...] = diag[0] + shifted
        base_source[...] = probes[0:width, :]

    @pl.when(distance < half - 1)
    def _():
        pack_full(factor_p[...], out)
        out[packed : packed + width, :] = value_p[...]

    depth, rows_here, across = potential.shape
    even_e = lax.axis_index("energy") % 2 == 0
    below = jnp.where(even_e, got_odd[...], got_even[...])
    above = jnp.where(even_e, got_even[...], got_odd[...])
    spare = wide.shape[1] - rows_here - 2 * SWEEPS
    parts = [below, potential[...], above]
    if spare > 0:
        parts.append(jnp.zeros((depth, spare, across), F32))
    wide[...] = jnp.concatenate(parts, axis=1)
    put_planes(out, out.shape[0] - SWEEPS * wide.shape[1], wide, slab % 2 == 0)
    first_z, first_x = region_start(depth, rows_here)
    rows, ys = spots(dopants[...], rows_all, depth + 2 * SWEEPS, wide.shape[1], across, first_z,
                     first_x)
    dopant[...] = dopant_charge * one_pass(rows, ys.astype(BF16), NT)


def put_planes(out, start, wide, high):
    pitch = wide.shape[1]
    last = wide.shape[0] - SWEEPS
    for k in range(SWEEPS):
        plane = jnp.where(high, wide[last + k], wide[k])
        out[start + k * pitch : start + (k + 1) * pitch, :] = plane


def centre_kernel(couple, even, odd, message, matrix, source, link, base, base_source, wide,
                  factor, value, total, total_source, out, hold, block, column):
    slab, left, distance = place()
    half = lax.axis_size("slab") // 2
    width = matrix.shape[0]
    put_planes(out, 2 * width, wide, slab % 2 == 1)

    @pl.when(jnp.logical_or(slab == half - 1, slab == half))
    def _():
        take_message(message, couple, (even, odd), left, block, column)
        right_side = source[...] - column[...]
        near = link[...]
        near_t = near.T
        sign = jnp.where(left, 1.0, -1.0)

        def run(invert):
            solved, size = invert(matrix[...] - block[...], hold, 1 / 12, 4)
            reach = dot3(solved, near)
            found = dot3(solved, right_side)
            factor[...] = reach
            value[...] = found
            both = base[...] + sign * dot3(near_t, reach)
            both_source = base_source[...] - dot3(near_t, found)
            total[...] = both
            total_source[...] = both_source
            pack_symmetric(both, out)
            out[width : 2 * width, :] = both_source
            return size

        guarded(run)


def expand_kernel(couple, even, odd, probes, probes_near, letter, second, factor, value, factor_p,
                  value_p, reach, slope, offset, weights):
    slab, left, distance = place()
    half = lax.axis_size("slab") // 2
    width = value.shape[0]
    packed = width + width // 2

    def put(block, m, v):
        at = pl.ds(pl.multiple_of(block * width, width), width)
        slope[at, :] = m
        offset[at, :] = v

    @pl.when(jnp.logical_or(slab == half - 1, slab == half))
    def _():
        own = jnp.where(left, 0, 1)
        sign = jnp.where(left, 1.0, -1.0)
        m1 = sign * factor[...]
        v1 = value[...]
        put(own, m1, v1)

        @pl.when(left)
        def _():
            put(1, -(dot3(factor_p[...], m1) + reach[...]), value_p[...] - dot3(factor_p[...], v1))

        @pl.when(jnp.logical_not(left))
        def _():
            put(0, eye(width), jnp.zeros_like(v1))

        link = jnp.where(left, couple[0].T, following((even, odd)))
        carry = dot3(unpack_symmetric(letter[0:width, :]), link)
        mq = -dot3(carry, m1)
        vq = letter[width : 2 * width, :] - dot3(carry, v1)
        put(jnp.where(left, 3, 2), mq, vq)
        outer = unpack_full(second[0:packed, :], width)
        put(jnp.where(left, 2, 3), -dot3(outer, mq),
            second[packed : packed + width, :] - dot3(outer, vq))
        weights[0 : 2 * width, :] = probes[...]
        weights[2 * width :, :] = probes_near[...]


def join_middle(invert, message, total, total_source, hold, left):
    width = total.shape[0]
    sign = jnp.where(left, 1.0, -1.0)
    matrix = sign * (unpack_symmetric(message[0:width, :]) - total[...])
    right_side = sign * (message[width : 2 * width, :] - total_source[...])
    inverse, size = invert(matrix, hold, 1 / 48, 5)
    return dot3(inverse, right_side), size


def join_pair_kernel(message, total, total_source, slope, offset, weights, dens, hold):
    slab, left, distance = place()
    half = lax.axis_size("slab") // 2

    @pl.when(jnp.logical_or(slab == half - 1, slab == half))
    def _():
        def run(invert):
            middle, size = join_middle(invert, message, total, total_source, hold, left)
            terms = weights[...] * (offset[...] + dot3(slope[...], middle))
            dens[...] = dot6(jnp.ones((8, terms.shape[1]), F32), terms, NT)[0:1]
            return size

        guarded(run)


def join_kernel(message, total, total_source, factor, value, out_first, out_middle, hold):
    slab, left, distance = place()
    half = lax.axis_size("slab") // 2

    @pl.when(jnp.logical_or(slab == half - 1, slab == half))
    def _():
        def run(invert):
            middle, size = join_middle(invert, message, total, total_source, hold, left)
            sign = jnp.where(left, 1.0, -1.0)
            out_first[...] = value[...] + sign * dot3(factor[...], middle)
            out_middle[...] = middle
            return size

        guarded(run)


def back_kernel(step, couple, even, odd, probes, message, first, middle, known_p, known_q,
                factor_p, value_p, inverse_q, value_q, reach, out_p, out_q, dens):
    slab, left, distance = place()
    centre = lax.axis_size("slab") // 2 - 1
    width = couple.shape[1]

    @pl.when(jnp.logical_and(distance < centre, distance != step))
    def _():
        out_p[...] = known_p[...]
        out_q[...] = known_q[...]

    @pl.when(distance == step)
    def _():
        link = jnp.where(left, following((even, odd)).T, couple[0])
        xq = value_q[...] - dot3(inverse_q[...], dot3(link, message[...]))
        out_q[...] = xq
        out_p[...] = value_p[...] - dot3(factor_p[...], xq)

    @pl.when(jnp.logical_and(distance == centre, left))
    def _():
        xa = first[...]
        out_p[...] = xa
        out_q[...] = value_p[...] - dot3(factor_p[...], xa) - dot3(reach[...], middle[...])

    @pl.when(jnp.logical_and(distance == centre, jnp.logical_not(left)))
    def _():
        out_p[...] = first[...]
        out_q[...] = middle[...]

    xp = out_p[...]
    xq = out_q[...]
    xa = jnp.where(left, xp, xq)
    xb = jnp.where(left, xq, xp)
    terms = jnp.concatenate([probes[0:width, :] * xa, probes[width:, :] * xb], axis=0)
    dens[...] = dot6(jnp.ones((8, terms.shape[1]), F32), terms, NT)[0:1]


def total_kernel(scale, cells, *rest):
    parts, out = rest[:-1], rest[-1]
    total = parts[0][0:1, :]
    for part in parts[1:]:
        total = total + part[0:1, :]
    out[0:1, :] = total * scale
    out[1:2, 0 : cells.shape[1]] = cells[...].astype(F32)


def poisson_kernel(rows_all, planes, paired, packet, near, far, dopant_grid, wide, near_letter,
                   near_at, far_letter, far_at, out, density):
    slab, slabs = lax.axis_index("slab"), lax.axis_size("slab")
    depth, pitch, across = wide.shape
    depth = depth + 2 * SWEEPS
    first_z, first_x = region_start(out.shape[0], out.shape[1])
    n = density.shape[0]
    even = slab % 2 == 0
    alone = jnp.logical_or(slab == 0, slab == slabs - 1)
    own, beside, beyond = packet[0:1, 0:n], near[0:1, 0:n], far[0:1, 0:n]
    if paired:
        own = jnp.where(alone, near[0:1, n : 2 * n], own)
        beside = jnp.where(alone, beside, packet[0:1, n : 2 * n])
    density[...] = own.reshape(n)
    weights = jnp.concatenate([own, beside, jnp.where(alone, 0.0, beyond)], axis=1)
    orbitals = jnp.concatenate([packet[1:2, 0:n], near[1:2, 0:n], far[1:2, 0:n]], axis=1)
    orbitals = jnp.where(jnp.abs(orbitals) < 2.0**30, orbitals, -1.0).astype(jnp.int32)
    rows, ys = spots(orbitals, rows_all, depth, pitch, across, first_z, first_x)
    spread = ys * weights
    h = spread.astype(BF16)
    rest = spread - h.astype(F32)
    m = rest.astype(BF16)
    low = (rest - m.astype(F32)).astype(BF16)
    electron = one_pass(rows, h, NT) + (one_pass(rows, m, NT) + one_pass(rows, low, NT))
    electron = electron.reshape(depth, pitch, across)
    dopant = dopant_grid[...].reshape(depth, pitch, across)
    size = SWEEPS * pitch
    near_planes = near_letter[near_at : near_at + size, :].reshape(SWEEPS, pitch, across)
    far_planes = far_letter[far_at : far_at + size, :].reshape(SWEEPS, pitch, across)
    start = jnp.concatenate(
        [jnp.where(even, far_planes, near_planes), wide[...],
         jnp.where(even, near_planes, far_planes)],
        axis=0,
    )
    zs = lax.broadcasted_iota(jnp.int32, start.shape, 0) + first_z
    xs = lax.broadcasted_iota(jnp.int32, start.shape, 1) + first_x
    ys = lax.broadcasted_iota(jnp.int32, start.shape, 2)
    exists = (zs >= 0) & (zs < planes) & (xs >= 0) & (xs < rows_all)
    potential = jnp.where(exists, start, 0.0)
    start = potential
    strength = coupling_beta * jnp.abs(electron)
    for _ in range(SWEEPS):
        blank = jnp.zeros((1, pitch, across), F32)
        beside = jnp.concatenate([potential[1:], blank], axis=0)
        beside = beside + jnp.concatenate([blank, potential[:-1]], axis=0)
        beside = beside + pltpu.roll(potential, 1, 1) + pltpu.roll(potential, pitch - 1, 1)
        beside = beside + jnp.where(ys > 0, pltpu.roll(potential, 1, 2), 0.0)
        beside = beside + jnp.where(ys < across - 1, pltpu.roll(potential, across - 1, 2), 0.0)
        growth = jnp.exp(potential - start)
        residual = beside - 6.0 * potential + coupling_beta * (dopant - electron * growth)
        potential = potential + residual / (6.0 + strength * growth)
        potential = jnp.where(exists, potential, 0.0)
    halo = SWEEPS
    out[...] = potential[halo : halo + out.shape[0], halo : halo + out.shape[1], :]


VM = pl.BlockSpec(memory_space=pltpu.VMEM)
FAR = pl.BlockSpec(memory_space=pltpu.HBM)
GRANT = 16 << 20


def like(*shape, dtype=F32):
    return jax.ShapeDtypeStruct(shape, dtype)


def call(kernel, name, outs, args, scratch=(), distant=0, flops=10**8):
    args = list(args)
    for k in range(distant):
        args[k] = pltpu.with_memory_space_constraint(args[k], pltpu.HBM)
    own = [pltpu.VMEM(shape, F32) for shape in scratch]
    if distant:
        own += [pltpu.SemaphoreType.DMA((distant + 1,))]
    return pl.pallas_call(
        kernel,
        out_shape=outs,
        in_specs=[FAR] * distant + [VM] * (len(args) - distant),
        out_specs=jax.tree.map(lambda _: VM, outs),
        scratch_shapes=own,
        compiler_params=pltpu.CompilerParams(vmem_limit_bytes=GRANT),
        cost_estimate=pl.CostEstimate(flops=flops, bytes_accessed=10**6, transcendentals=0),
        name=name,
    )(*args)


def pairs_of(count, odd):
    found = []
    for first in range(1 if odd else 0, count - 1, 2):
        found += [(first, first + 1), (first + 1, first)]
    return found


def slab_exchange(value, odd):
    slabs, energies = lax.axis_size("slab"), lax.axis_size("energy")
    pairs = pairs_of(slabs, odd)
    busy = {a for a, _ in pairs}
    whole = [(a * energies + e, b * energies + e) for a, b in pairs for e in range(energies)]
    for a in range(slabs):
        if a not in busy:
            whole += [(a * energies + e, a * energies + (e ^ 1)) for e in range(energies)]
    return lax.ppermute(value, ("slab", "energy"), whole)


def energy_exchange(value, odd):
    energies = lax.axis_size("energy")
    pairs = pairs_of(energies, odd)
    if odd:
        pairs += [(energies - 1, 0), (0, energies - 1)]
    return lax.ppermute(value, "energy", pairs)


def body(energy_index, diag_blocks, couple, probes, orbital_cell, dopant_cells, initial_potential):
    width = diag_blocks.shape[1]
    probe_count = probes.shape[1]
    slab, slabs = lax.axis_index("slab"), lax.axis_size("slab")
    energy, energies = lax.axis_index("energy"), lax.axis_size("energy")
    half = slabs // 2
    square, column = like(width, width), like(width, probe_count)
    letter = like(2 * width, probe_count)
    sq, col = (width, width), (width, probe_count)

    even = slab_exchange(couple, False)
    odd = lax.ppermute(couple, "slab", [(s + 1, s) for s in range(1, slabs - 1, 2)])
    paired = half == 2
    probes_near = slab_exchange(probes, False) if paired else probes

    message = None
    for t in range(half - 1):
        args = [diag_blocks, couple, probes, energy_index.reshape(1, 1)]
        if t > 0:
            if t > 1:
                _, _, distance = place()
                message = jnp.where(distance == t, message, kept)
            kept = message
            args += [message, even, odd]
        state = call(
            functools.partial(stage_kernel, t), f"stage{t}",
            (square, column, square, square, column, square, column, letter),
            args, (sq, diag_blocks.shape, couple.shape, probes.shape), 3,
        )
        if t == 0:
            prepared = state
        message = slab_exchange(state[-1], t % 2 == 1)
    factor_p, value_p, _, _, _, inverse_q, value_q, _ = state

    depth, rows_here, across = initial_potential.shape
    halo = SWEEPS
    rows_all = rows_here * energies
    pitch = -(-(rows_here + 2 * halo) // 8) * 8
    strip = halo * pitch
    odd_e = lax.axis_index("energy") % 2 == 1
    low, high = initial_potential[:, :halo], initial_potential[:, rows_here - halo :]
    got_even = energy_exchange(jnp.where(odd_e, low, high), False)
    got_odd = energy_exchange(jnp.where(odd_e, high, low), True)
    packed = width + width // 2
    near_at, far_at = packed + width, 2 * width
    cells = (depth + 2 * halo) * pitch

    matrix, source, link, base, base_source, reach, second, wide, dopant_grid = call(
        functools.partial(ready_kernel, rows_all), "ready",
        (square, column, square, square, column, square, like(near_at + strip, probe_count),
         like(depth, pitch, across), like(cells, across)),
        [energy_index.reshape(1, 1), diag_blocks, couple, probes, probes_near, even, odd,
         dopant_cells.reshape(1, -1), initial_potential, got_even, got_odd, *prepared[:5]],
    )
    second = slab_exchange(second, False)
    factor, value, total, total_source, sent = call(
        centre_kernel, "centre",
        (square, column, square, column, like(far_at + strip, probe_count)),
        [couple, even, odd, message, matrix, source, link, base, base_source, wide],
        (sq, sq, col),
    )
    across_middle = slab_exchange(sent, half % 2 == 0)
    far_letter = across_middle if paired else slab_exchange(sent, True)
    if paired:
        slope, offset, weights = call(
            expand_kernel, "expand",
            (like(4 * width, width), like(4 * width, probe_count), like(4 * width, probe_count)),
            [couple, even, odd, probes, probes_near, message, second, factor, value,
             prepared[0], prepared[1], reach],
        )
        dens = call(
            join_pair_kernel, "join", like(1, 4 * width),
            [across_middle, total, total_source, slope, offset, weights], (sq,),
        )
    else:
        first, middle = call(
            join_kernel, "join", (column, column),
            [across_middle, total, total_source, factor, value], (sq,),
        )
        centred = lax.axis_index("slab") == half - 1
        factor_p = jnp.where(centred, prepared[0], factor_p)
        value_p = jnp.where(centred, prepared[1], value_p)
        known_p, known_q = first, middle
        for t in range(half - 2, -1, -1):
            known_p, known_q, dens = call(
                functools.partial(back_kernel, t), f"back{t}",
                (column, column, like(1, 2 * width)),
                [couple, even, odd, probes, slab_exchange(known_p, t % 2 == 1), first, middle,
                 known_p, known_q, factor_p, value_p, inverse_q, value_q, reach],
            )
    parts = [dens] + [
        lax.ppermute(dens, "energy", [(e, e ^ k) for e in range(energies)])
        for k in range(1, energies)
    ]
    packet = call(
        functools.partial(total_kernel, 1.0 / (probe_count * energies)), "total",
        like(2, dens.shape[1]), [orbital_cell.reshape(1, -1), *parts],
    )
    near = slab_exchange(packet, False)
    far = slab_exchange(packet, True)

    def poisson(packet, near, far, dopant_grid, wide, near_letter, far_letter, out, density):
        poisson_kernel(rows_all, depth * slabs, paired, packet, near, far, dopant_grid, wide,
                       near_letter, near_at, far_letter, far_at, out, density)

    potential, density = call(
        poisson, "poisson", (like(depth, rows_here, across), like(2 * width)),
        [packet, near, far, dopant_grid, wide, second, far_letter],
    )
    return (potential, density)


def solution(mesh):
    placed = (
        P("energy"),
        P(("cfg", "slab"), None, None),
        P(("cfg", "slab"), None, None),
        P("slab", None),
        P("slab"),
        P("cfg"),
        P(("cfg", "slab"), "energy", None),
    )
    return jax.shard_map(
        body,
        mesh=mesh,
        in_specs=placed,
        out_specs=(P(("cfg", "slab"), "energy", None), P(("cfg", "slab"))),
        check_vma=False,
    )
```

```python
import functools

import jax
import jax.numpy as jnp
from jax import lax
from jax.experimental import pallas as pl
from jax.experimental.pallas import tpu as pltpu
from jax.sharding import PartitionSpec as P


SWEEPS = 2

sigma_base = 0.02
sigma_step = 0.01
coupling_beta = 0.5
dopant_charge = 4.0

F32 = jnp.float32
BF16 = jnp.bfloat16
NT = (((1,), (1,)), ((), ()))
NN = (((1,), (0,)), ((), ()))


def split2(a):
    high = a.astype(BF16)
    return high, (a - high.astype(F32)).astype(BF16)


def one_pass(a, b, dims=NN):
    return lax.dot_general(a, b, dims, preferred_element_type=F32)


def dot3(a, b):
    ah, al = split2(a)
    bh, bl = split2(b)
    return one_pass(ah, bh) + (one_pass(ah, bl) + one_pass(al, bh))


def dot6(a, b, dims=NN):
    return lax.dot_general(
        a, b, dims, precision=lax.Precision.HIGHEST, preferred_element_type=F32
    )


def eye(n):
    return (
        lax.broadcasted_iota(jnp.int32, (n, n), 0) == lax.broadcasted_iota(jnp.int32, (n, n), 1)
    ).astype(F32)


def estimate(matrix, ratio, doublings):
    unit = eye(matrix.shape[0])
    square = dot3(matrix, matrix)
    sums = jnp.sum(jnp.abs(square), axis=0, keepdims=True)
    bound = jnp.sqrt(jnp.max(sums, axis=1, keepdims=True))
    first = 2.0 / (bound * (1.0 + ratio))
    tau = (1.0 + ratio) / (1.0 - ratio)
    for k in range(doublings):
        after = 2.0 * tau * tau - 1.0
        scale = (after + 1.0) / after
        if k == 0:
            grown = (2.0 * first) * unit - (first * first) * matrix
            squared = unit - (2.0 * first) * matrix + (first * first) * square
        else:
            grown = guess + dot3(guess, error)
            squared = dot3(error, error) if k + 1 < doublings else None
        guess = scale * grown
        if k + 1 < doublings:
            error = scale * squared - (scale - 1.0) * unit
        tau = after
    residual = unit - dot6(matrix, guess)
    return guess + dot3(guess, residual), jnp.sum(residual * residual), first


def fast(matrix, hold, ratio, doublings):
    found, size, _ = estimate(matrix, ratio, doublings)
    return found, size


def careful(matrix, hold, ratio, doublings):
    unit = eye(matrix.shape[0])
    found, size, first = estimate(matrix, ratio, doublings)
    hold[...] = found

    @pl.when(jnp.logical_not(size < 0.9))
    def _():
        hold[...] = first * unit

    def go_on(state):
        count, last = state
        return jnp.logical_and(count < 64, jnp.logical_not(last < 1e-6))

    def newton(state):
        count, _ = state
        now = hold[...]
        left = unit - dot6(matrix, now)
        hold[...] = now + dot6(now, left)
        return count + 1, jnp.sum(left * left)

    lax.while_loop(go_on, newton, (jnp.int32(0), size))
    return hold[...], size


def guarded(run):
    worst = run(fast)

    @pl.when(jnp.logical_not(worst < 4e-5))
    def _():
        run(careful)


def pack_symmetric(matrix, out):
    half = matrix.shape[0] // 3
    out[0:half, :] = matrix[half : 2 * half, 0 : 2 * half]
    out[half : 2 * half, :] = matrix[2 * half :, 0 : 2 * half]
    out[2 * half : 3 * half, :] = jnp.concatenate(
        [matrix[0:half, 0:half], matrix[2 * half :, 2 * half :]], axis=1
    )


def unpack_symmetric(packed):
    third = packed.shape[0] // 3
    row1 = packed[0:third]
    row2 = packed[third : 2 * third]
    ends = packed[2 * third :]
    b10, b11 = row1[:, :third], row1[:, third:]
    b20, b21 = row2[:, :third], row2[:, third:]
    b00, b22 = ends[:, :third], ends[:, third:]
    return jnp.concatenate(
        [
            jnp.concatenate([b00, b10.T, b20.T], axis=1),
            jnp.concatenate([b10, b11, b21.T], axis=1),
            jnp.concatenate([b20, b21, b22], axis=1),
        ],
        axis=0,
    )


def place():
    slab, slabs = lax.axis_index("slab"), lax.axis_size("slab")
    left = slab < slabs // 2
    return slab, left, jnp.where(left, slab, slabs - 1 - slab)


def following(ahead):
    even, odd = ahead
    return jnp.where(lax.axis_index("slab") % 2 == 0, even[0], odd[0])


def take_message(message, couple, ahead, left, block, column):
    width = block.shape[0]
    link_t = jnp.where(left, couple[0].T, following(ahead))
    link = jnp.where(left, couple[0], following(ahead).T)
    block[...] = dot3(link, dot3(unpack_symmetric(message[0:width, :]), link_t))
    column[...] = dot3(link, message[width : 2 * width, :])


def stage_kernel(step, diag_far, couple_far, probes_far, energy, *rest):
    if step > 0:
        message, even, odd, rest = rest[0], rest[1], rest[2], rest[3:]
    factor_p, value_p, inverse_p, matrix_q, source_q, inverse_q, value_q, out = rest[:8]
    hold, diag, couple, probes, sems = rest[8:]
    _, left, distance = place()
    forward = lax.axis_index("slab") <= lax.axis_size("slab") // 2
    first = jnp.where(forward, 0, 1)
    width = diag.shape[1]
    loads = [
        pltpu.make_async_copy(diag_far.at[first], diag.at[0], sems.at[0]),
        pltpu.make_async_copy(couple_far, couple, sems.at[1]),
        pltpu.make_async_copy(probes_far, probes, sems.at[2]),
        pltpu.make_async_copy(diag_far.at[1 - first], diag.at[1], sems.at[3]),
    ]
    for load in loads:
        load.start()
    loads[0].wait()
    if step > 0:
        loads[1].wait()
    shift = sigma_base + sigma_step * energy[...].astype(F32)
    shifted = shift * eye(width)
    sp = diag[0] + shifted
    if step > 0:
        taken = jnp.logical_and(distance >= 1, distance <= step)
        take_message(message, couple, (even, odd), left, matrix_q, source_q)
        sp = sp - jnp.where(taken, matrix_q[...], 0.0)
        extra = jnp.where(taken, source_q[...], 0.0)

    def run(invert):
        xp, size_p = invert(sp, hold, 1 / 12, 4)
        inverse_p[...] = xp
        if invert is fast:
            for load in loads[2 if step > 0 else 1 :]:
                load.wait()
        rp = probes[pl.ds(pl.multiple_of(first * width, width), width), :]
        rq = probes[pl.ds(pl.multiple_of((1 - first) * width, width), width), :]
        if step > 0:
            rp = rp - extra
        inner = couple[1]
        inner_t = inner.T
        apq = jnp.where(forward, inner_t, inner)
        aqp = jnp.where(forward, inner, inner_t)
        fp = dot3(xp, apq)
        yp = dot3(xp, rp)
        factor_p[...] = fp
        value_p[...] = yp
        sq = diag[1] + shifted - dot3(aqp, fp)
        source = rq - dot3(aqp, yp)
        matrix_q[...] = sq
        source_q[...] = source
        xq, size_q = invert(sq, hold, 1 / 12, 4)
        yq = dot3(xq, source)
        inverse_q[...] = xq
        value_q[...] = yq
        pack_symmetric(xq, out)
        out[width : 2 * width, :] = yq
        return jnp.maximum(size_p, size_q)

    guarded(run)


def pack_full(matrix, out):
    n = matrix.shape[0]
    lanes = out.shape[1]
    out[0:n, :] = matrix[:, 0:lanes]
    out[n : n + n // 2, :] = jnp.concatenate(
        [matrix[0 : n // 2, lanes:], matrix[n // 2 :, lanes:]], axis=1
    )


def unpack_full(packed, n):
    rest = packed[n : n + n // 2]
    lanes = packed.shape[1]
    tail = jnp.concatenate([rest[:, : n - lanes], rest[:, n - lanes :]], axis=0)
    return jnp.concatenate([packed[0:n], tail], axis=1)


def spots(index, rows_all, depth, pitch, across, first_z, first_x):
    plane = rows_all * across
    z = index // plane - first_z
    x = index // across % rows_all - first_x
    y = index % across
    inside = (z >= 0) & (z < depth) & (x >= 0) & (x < pitch)
    row = jnp.where(inside, z * pitch + x, -1)
    n = index.shape[1]
    pick_row = lax.broadcasted_iota(jnp.int32, (depth * pitch, n), 0) == row
    pick_y = lax.broadcasted_iota(jnp.int32, (across, n), 0) == y
    return pick_row.astype(F32).astype(BF16), pick_y.astype(F32)


def region_start(depth_here, rows_here):
    first_z = lax.axis_index("slab") * depth_here - SWEEPS
    return first_z, lax.axis_index("energy") * rows_here - SWEEPS


def ready_kernel(energy, diag, couple, probes, factor_p, value_p, inverse_p, matrix_q, source_q,
                 matrix, source, link, base, base_source, reach, out):
    slab, _, distance = place()
    half = lax.axis_size("slab") // 2
    width = diag.shape[1]
    packed = width + width // 2

    @pl.when(slab == half)
    def _():
        behind = couple[0]
        behind_t = behind.T
        across = dot3(inverse_p[...], behind)
        reach[...] = across
        matrix[...] = matrix_q[...]
        source[...] = source_q[...]
        link[...] = dot3(couple[1], across)
        base[...] = dot3(behind_t, across)
        base_source[...] = dot3(behind_t, value_p[...])

    @pl.when(slab == half - 1)
    def _():
        shift = sigma_base + sigma_step * energy[...].astype(F32)
        shifted = shift * eye(width)
        matrix[...] = diag[0] + shifted
        source[...] = probes[0:width, :]
        link[...] = couple[1].T
        base[...] = diag[1] + shifted
        base_source[...] = probes[width : 2 * width, :]

    @pl.when(distance < half - 1)
    def _():
        pack_full(factor_p[...], out)
        out[packed : packed + width, :] = value_p[...]


def halo_kernel(rows_all, dopants, potential, got_even, got_odd, wide, dopant, planes):
    depth, rows_here, across = potential.shape
    even_e = lax.axis_index("energy") % 2 == 0
    below = jnp.where(even_e, got_odd[...], got_even[...])
    above = jnp.where(even_e, got_even[...], got_odd[...])
    spare = wide.shape[1] - rows_here - 2 * SWEEPS
    parts = [below, potential[...], above]
    if spare > 0:
        parts.append(jnp.zeros((depth, spare, across), F32))
    wide[...] = jnp.concatenate(parts, axis=1)
    put_planes(planes, 0, wide, lax.axis_index("slab") % 2 == 0)
    first_z, first_x = region_start(depth, rows_here)
    rows, ys = spots(dopants[...], rows_all, depth + 2 * SWEEPS, wide.shape[1], across, first_z,
                     first_x)
    dopant[...] = dopant_charge * one_pass(rows, ys.astype(BF16), NT)


def put_planes(out, start, wide, high):
    pitch = wide.shape[1]
    last = wide.shape[0] - SWEEPS
    for k in range(SWEEPS):
        plane = jnp.where(high, wide[last + k], wide[k])
        out[start + k * pitch : start + (k + 1) * pitch, :] = plane


def centre_kernel(couple, even, odd, message, matrix, source, link, base, base_source, wide,
                  factor, value, total, total_source, out, hold, block, column):
    slab, left, _ = place()
    half = lax.axis_size("slab") // 2
    width = matrix.shape[0]
    put_planes(out, 2 * width, wide, slab % 2 == 1)

    @pl.when(jnp.logical_or(slab == half - 1, slab == half))
    def _():
        take_message(message, couple, (even, odd), left, block, column)
        right_side = source[...] - column[...]
        near = link[...]
        near_t = near.T
        sign = jnp.where(left, -1.0, 1.0)

        def run(invert):
            solved, size = invert(matrix[...] - block[...], hold, 1 / 12, 4)
            reach = dot3(solved, near)
            found = dot3(solved, right_side)
            factor[...] = reach
            value[...] = found
            both = base[...] + sign * dot3(near_t, reach)
            both_source = base_source[...] - dot3(near_t, found)
            total[...] = both
            total_source[...] = both_source
            pack_symmetric(both, out)
            out[width : 2 * width, :] = both_source
            return size

        guarded(run)


def expand_kernel(couple, even, odd, probes, probes_near, letter, second, factor, value, factor_p,
                  value_p, reach, slope, offset, weights):
    slab, left, _ = place()
    half = lax.axis_size("slab") // 2
    width = value.shape[0]
    packed = width + width // 2

    def put(block, m, v):
        at = pl.ds(pl.multiple_of(block * width, width), width)
        slope[at, :] = m
        offset[at, :] = v

    @pl.when(jnp.logical_or(slab == half - 1, slab == half))
    def _():
        own = jnp.where(left, 0, 1)
        m1 = jnp.where(left, -1.0, 1.0) * factor[...]
        v1 = value[...]
        put(own, m1, v1)

        @pl.when(left)
        def _():
            put(1, eye(width), jnp.zeros_like(v1))

        @pl.when(jnp.logical_not(left))
        def _():
            put(0, -(dot3(factor_p[...], m1) + reach[...]), value_p[...] - dot3(factor_p[...], v1))

        link = jnp.where(left, couple[0].T, following((even, odd)))
        carry = dot3(unpack_symmetric(letter[0:width, :]), link)
        mq = -dot3(carry, m1)
        vq = letter[width : 2 * width, :] - dot3(carry, v1)
        put(jnp.where(left, 3, 2), mq, vq)
        outer = unpack_full(second[0:packed, :], width)
        put(jnp.where(left, 2, 3), -dot3(outer, mq),
            second[packed : packed + width, :] - dot3(outer, vq))
        weights[0 : 2 * width, :] = probes[...]
        weights[2 * width :, :] = probes_near[...]


def join_middle(invert, message, total, total_source, hold, left):
    width = total.shape[0]
    sign = jnp.where(left, -1.0, 1.0)
    matrix = sign * (unpack_symmetric(message[0:width, :]) - total[...])
    right_side = sign * (message[width : 2 * width, :] - total_source[...])
    inverse, size = invert(matrix, hold, 1 / 48, 5)
    return dot3(inverse, right_side), size


def join_pair_kernel(message, total, total_source, slope, offset, weights, dens, hold):
    slab, left, _ = place()
    half = lax.axis_size("slab") // 2

    @pl.when(jnp.logical_or(slab == half - 1, slab == half))
    def _():
        def run(invert):
            middle, size = join_middle(invert, message, total, total_source, hold, left)
            terms = weights[...] * (offset[...] + dot3(slope[...], middle))
            dens[...] = dot6(jnp.ones((8, terms.shape[1]), F32), terms, NT)[0:1]
            return size

        guarded(run)


def join_kernel(message, total, total_source, factor, value, out_first, out_middle, hold):
    slab, left, _ = place()
    half = lax.axis_size("slab") // 2

    @pl.when(jnp.logical_or(slab == half - 1, slab == half))
    def _():
        def run(invert):
            middle, size = join_middle(invert, message, total, total_source, hold, left)
            sign = jnp.where(left, -1.0, 1.0)
            out_first[...] = value[...] + sign * dot3(factor[...], middle)
            out_middle[...] = middle
            return size

        guarded(run)


def back_kernel(step, couple, even, odd, probes, message, first, middle, known_p, known_q,
                factor_p, value_p, inverse_q, value_q, reach, out_p, out_q, dens):
    _, left, distance = place()
    centre = lax.axis_size("slab") // 2 - 1
    width = couple.shape[1]

    @pl.when(jnp.logical_and(distance < centre, distance != step))
    def _():
        out_p[...] = known_p[...]
        out_q[...] = known_q[...]

    @pl.when(distance == step)
    def _():
        link = jnp.where(left, following((even, odd)).T, couple[0])
        xq = value_q[...] - dot3(inverse_q[...], dot3(link, message[...]))
        out_q[...] = xq
        out_p[...] = value_p[...] - dot3(factor_p[...], xq)

    @pl.when(jnp.logical_and(distance == centre, left))
    def _():
        out_p[...] = first[...]
        out_q[...] = middle[...]

    @pl.when(jnp.logical_and(distance == centre, jnp.logical_not(left)))
    def _():
        xb = first[...]
        out_p[...] = xb
        out_q[...] = value_p[...] - dot3(factor_p[...], xb) - dot3(reach[...], middle[...])

    xp = out_p[...]
    xq = out_q[...]
    xa = jnp.where(left, xp, xq)
    xb = jnp.where(left, xq, xp)
    terms = jnp.concatenate([probes[0:width, :] * xa, probes[width:, :] * xb], axis=0)
    dens[...] = dot6(jnp.ones((8, terms.shape[1]), F32), terms, NT)[0:1]


def total_kernel(scale, cells, *rest):
    parts, out = rest[:-1], rest[-1]
    total = parts[0][0:1, :]
    for part in parts[1:]:
        total = total + part[0:1, :]
    out[0:1, :] = total * scale
    out[1:2, 0 : cells.shape[1]] = cells[...].astype(F32)


def poisson_kernel(rows_all, planes, paired, packet, near, far, dopant_grid, wide, near_letter,
                   far_letter, far_at, out, density):
    slab, slabs = lax.axis_index("slab"), lax.axis_size("slab")
    depth, pitch, across = wide.shape
    depth = depth + 2 * SWEEPS
    first_z, first_x = region_start(out.shape[0], out.shape[1])
    n = density.shape[0]
    even = slab % 2 == 0
    alone = jnp.logical_or(slab == 0, slab == slabs - 1)
    own, beside, beyond = packet[0:1, 0:n], near[0:1, 0:n], far[0:1, 0:n]
    if paired:
        own = jnp.where(alone, near[0:1, n : 2 * n], own)
        beside = jnp.where(alone, beside, packet[0:1, n : 2 * n])
    density[...] = own.reshape(n)
    weights = jnp.concatenate([own, beside, jnp.where(alone, 0.0, beyond)], axis=1)
    orbitals = jnp.concatenate([packet[1:2, 0:n], near[1:2, 0:n], far[1:2, 0:n]], axis=1)
    orbitals = jnp.where(jnp.abs(orbitals) < 2.0**30, orbitals, -1.0).astype(jnp.int32)
    rows, ys = spots(orbitals, rows_all, depth, pitch, across, first_z, first_x)
    spread = ys * weights
    h = spread.astype(BF16)
    rest = spread - h.astype(F32)
    m = rest.astype(BF16)
    low = (rest - m.astype(F32)).astype(BF16)
    electron = one_pass(rows, h, NT) + (one_pass(rows, m, NT) + one_pass(rows, low, NT))
    electron = electron.reshape(depth, pitch, across)
    dopant = dopant_grid[...].reshape(depth, pitch, across)
    size = SWEEPS * pitch
    near_planes = near_letter[...].reshape(SWEEPS, pitch, across)
    far_planes = far_letter[far_at : far_at + size, :].reshape(SWEEPS, pitch, across)
    start = jnp.concatenate(
        [jnp.where(even, far_planes, near_planes), wide[...],
         jnp.where(even, near_planes, far_planes)],
        axis=0,
    )
    zs = lax.broadcasted_iota(jnp.int32, start.shape, 0) + first_z
    xs = lax.broadcasted_iota(jnp.int32, start.shape, 1) + first_x
    ys = lax.broadcasted_iota(jnp.int32, start.shape, 2)
    exists = (zs >= 0) & (zs < planes) & (xs >= 0) & (xs < rows_all)
    potential = jnp.where(exists, start, 0.0)
    start = potential
    strength = coupling_beta * jnp.abs(electron)
    for _ in range(SWEEPS):
        blank = jnp.zeros((1, pitch, across), F32)
        beside = jnp.concatenate([potential[1:], blank], axis=0)
        beside = beside + jnp.concatenate([blank, potential[:-1]], axis=0)
        beside = beside + pltpu.roll(potential, 1, 1) + pltpu.roll(potential, pitch - 1, 1)
        beside = beside + jnp.where(ys > 0, pltpu.roll(potential, 1, 2), 0.0)
        beside = beside + jnp.where(ys < across - 1, pltpu.roll(potential, across - 1, 2), 0.0)
        growth = jnp.exp(potential - start)
        residual = beside - 6.0 * potential + coupling_beta * (dopant - electron * growth)
        potential = potential + residual / (6.0 + strength * growth)
        potential = jnp.where(exists, potential, 0.0)
    halo = SWEEPS
    out[...] = potential[halo : halo + out.shape[0], halo : halo + out.shape[1], :]


VM = pl.BlockSpec(memory_space=pltpu.VMEM)
FAR = pl.BlockSpec(memory_space=pltpu.HBM)
GRANT = 16 << 20


def like(*shape, dtype=F32):
    return jax.ShapeDtypeStruct(shape, dtype)


def call(kernel, outs, args, scratch=(), distant=0, flops=10**8):
    args = list(args)
    for k in range(distant):
        args[k] = pltpu.with_memory_space_constraint(args[k], pltpu.HBM)
    own = [pltpu.VMEM(shape, F32) for shape in scratch]
    if distant:
        own += [pltpu.SemaphoreType.DMA((distant + 1,))]
    return pl.pallas_call(
        kernel,
        out_shape=outs,
        in_specs=[FAR] * distant + [VM] * (len(args) - distant),
        out_specs=jax.tree.map(lambda _: VM, outs),
        scratch_shapes=own,
        compiler_params=pltpu.CompilerParams(vmem_limit_bytes=GRANT),
        cost_estimate=pl.CostEstimate(flops=flops, bytes_accessed=10**6, transcendentals=0),
    )(*args)


def pairs_of(count, odd):
    found = []
    for first in range(1 if odd else 0, count - 1, 2):
        found += [(first, first + 1), (first + 1, first)]
    return found


def slab_exchange(value, odd):
    slabs, energies = lax.axis_size("slab"), lax.axis_size("energy")
    pairs = pairs_of(slabs, odd)
    busy = {a for a, _ in pairs}
    whole = [(a * energies + e, b * energies + e) for a, b in pairs for e in range(energies)]
    for a in range(slabs):
        if a not in busy:
            whole += [(a * energies + e, a * energies + (e ^ 1)) for e in range(energies)]
    return lax.ppermute(value, ("slab", "energy"), whole)


def energy_exchange(value, odd):
    energies = lax.axis_size("energy")
    pairs = pairs_of(energies, odd)
    if odd:
        pairs += [(energies - 1, 0), (0, energies - 1)]
    return lax.ppermute(value, "energy", pairs)


def program(energy_index, diag_blocks, couple, probes, orbital_cell, dopant_cells, initial_potential):
    width = diag_blocks.shape[1]
    probe_count = probes.shape[1]
    slabs = lax.axis_size("slab")
    energies = lax.axis_size("energy")
    half = slabs // 2
    square, column = like(width, width), like(width, probe_count)
    letter = like(2 * width, probe_count)
    sq, col = (width, width), (width, probe_count)

    even = slab_exchange(couple, False)
    paired = half == 2
    odd = even
    if not paired:
        odd = lax.ppermute(couple, "slab", [(s + 1, s) for s in range(1, slabs - 1, 2)])

    message = None
    for t in range(half - 1):
        args = [diag_blocks, couple, probes, energy_index.reshape(1, 1)]
        if t > 0:
            if t > 1:
                _, _, distance = place()
                message = jnp.where(distance == t, message, kept)
            kept = message
            args += [message, even, odd]
        state = call(
            functools.partial(stage_kernel, t),
            (square, column, square, square, column, square, column, letter),
            args, (sq, diag_blocks.shape, couple.shape, probes.shape), 3,
        )
        if t == 0:
            prepared = state
        message = slab_exchange(state[-1], t % 2 == 1)
    factor_p, value_p, _, _, _, inverse_q, value_q, _ = state

    depth, rows_here, across = initial_potential.shape
    halo = SWEEPS
    rows_all = rows_here * energies
    pitch = -(-(rows_here + 2 * halo) // 8) * 8
    strip = halo * pitch
    odd_e = lax.axis_index("energy") % 2 == 1
    low, high = initial_potential[:, :halo], initial_potential[:, rows_here - halo :]
    got_even = energy_exchange(jnp.where(odd_e, low, high), False)
    got_odd = energy_exchange(jnp.where(odd_e, high, low), True)
    far_at = 2 * width
    cells = (depth + 2 * halo) * pitch
    matrix, source, link, base, base_source, reach, second = call(
        ready_kernel,
        (square, column, square, square, column, square,
         like(width + width // 2 + width, probe_count)),
        [energy_index.reshape(1, 1), diag_blocks, couple, probes, *prepared[:5]],
    )
    if paired:
        probes_near = slab_exchange(probes, False)
        second = slab_exchange(second, False)
    wide, dopant_grid, planes = call(
        functools.partial(halo_kernel, rows_all),
        (like(depth, pitch, across), like(cells, across), like(strip, across)),
        [dopant_cells.reshape(1, -1), initial_potential, got_even, got_odd],
    )
    factor, value, total, total_source, sent = call(
        centre_kernel,
        (square, column, square, column, like(far_at + strip, probe_count)),
        [couple, even, odd, message, matrix, source, link, base, base_source, wide],
        (sq, sq, col),
    )
    across_middle = slab_exchange(sent, half % 2 == 0)
    planes, _ = lax.optimization_barrier((planes, sent))
    near_planes = slab_exchange(planes, False)
    far_letter = across_middle if paired else slab_exchange(sent, True)
    if paired:
        slope, offset, weights = call(
            expand_kernel,
            (like(4 * width, width), like(4 * width, probe_count), like(4 * width, probe_count)),
            [couple, even, odd, probes, probes_near, message, second, factor, value,
             prepared[0], prepared[1], reach],
        )
        dens = call(
            join_pair_kernel, like(1, 4 * width),
            [across_middle, total, total_source, slope, offset, weights], (sq,),
        )
    else:
        first, middle = call(
            join_kernel, (column, column),
            [across_middle, total, total_source, factor, value], (sq,),
        )
        centred = lax.axis_index("slab") == half
        factor_p = jnp.where(centred, prepared[0], factor_p)
        value_p = jnp.where(centred, prepared[1], value_p)
        known_p, known_q = first, middle
        for t in range(half - 2, -1, -1):
            known_p, known_q, dens = call(
                functools.partial(back_kernel, t),
                (column, column, like(1, 2 * width)),
                [couple, even, odd, probes, slab_exchange(known_p, t % 2 == 1), first, middle,
                 known_p, known_q, factor_p, value_p, inverse_q, value_q, reach],
            )
    parts = [dens] + [
        lax.ppermute(dens, "energy", [(e, e ^ k) for e in range(energies)])
        for k in range(1, energies)
    ]
    packet = call(
        functools.partial(total_kernel, 1.0 / (probe_count * energies)),
        like(2, dens.shape[1]), [orbital_cell.reshape(1, -1), *parts],
    )
    near = slab_exchange(packet, False)
    far = slab_exchange(packet, True)

    def poisson(packet, near, far, dopant_grid, wide, near_letter, far_letter, out, density):
        poisson_kernel(rows_all, depth * slabs, paired, packet, near, far, dopant_grid, wide,
                       near_letter, far_letter, far_at, out, density)

    potential, density = call(
        poisson, (like(depth, rows_here, across), like(2 * width)),
        [packet, near, far, dopant_grid, wide, near_planes, far_letter],
    )
    return (potential, density)


def solution(mesh):
    placed = (
        P("energy"),
        P(("cfg", "slab"), None, None),
        P(("cfg", "slab"), None, None),
        P("slab", None),
        P("slab"),
        P("cfg"),
        P(("cfg", "slab"), "energy", None),
    )
    return jax.shard_map(
        program,
        mesh=mesh,
        in_specs=placed,
        out_specs=(P(("cfg", "slab"), "energy", None), P(("cfg", "slab"))),
        check_vma=False,
    )
```

```python
import functools

import jax
import jax.numpy as jnp
from jax import lax
from jax.experimental import pallas as pl
from jax.experimental.pallas import tpu as pltpu
from jax.sharding import PartitionSpec as P


SWEEPS = 2

sigma_base = 0.02
sigma_step = 0.01
coupling_beta = 0.5
dopant_charge = 4.0

F32 = jnp.float32
BF16 = jnp.bfloat16
NT = (((1,), (1,)), ((), ()))
NN = (((1,), (0,)), ((), ()))


def split2(a):
    high = a.astype(BF16)
    return high, (a - high.astype(F32)).astype(BF16)


def one_pass(a, b, dims=NN):
    return lax.dot_general(a, b, dims, preferred_element_type=F32)


def dot3(a, b):
    ah, al = split2(a)
    bh, bl = split2(b)
    return one_pass(ah, bh) + (one_pass(ah, bl) + one_pass(al, bh))


def dot6(a, b, dims=NN):
    return lax.dot_general(
        a, b, dims, precision=lax.Precision.HIGHEST, preferred_element_type=F32
    )


def eye(n):
    return (
        lax.broadcasted_iota(jnp.int32, (n, n), 0) == lax.broadcasted_iota(jnp.int32, (n, n), 1)
    ).astype(F32)


def estimate(matrix, ratio, doublings):
    unit = eye(matrix.shape[0])
    square = dot3(matrix, matrix)
    sums = jnp.sum(jnp.abs(square), axis=0, keepdims=True)
    bound = jnp.sqrt(jnp.max(sums, axis=1, keepdims=True))
    first = 2.0 / (bound * (1.0 + ratio))
    tau = (1.0 + ratio) / (1.0 - ratio)
    for k in range(doublings):
        after = 2.0 * tau * tau - 1.0
        scale = (after + 1.0) / after
        if k == 0:
            grown = (2.0 * first) * unit - (first * first) * matrix
            squared = unit - (2.0 * first) * matrix + (first * first) * square
        else:
            grown = guess + dot3(guess, error)
            squared = dot3(error, error) if k + 1 < doublings else None
        guess = scale * grown
        if k + 1 < doublings:
            error = scale * squared - (scale - 1.0) * unit
        tau = after
    residual = unit - dot6(matrix, guess)
    return guess + dot3(guess, residual), jnp.sum(residual * residual), first


def fast(matrix, hold, ratio, doublings):
    found, size, _ = estimate(matrix, ratio, doublings)
    return found, size


def careful(matrix, hold, ratio, doublings):
    unit = eye(matrix.shape[0])
    found, size, first = estimate(matrix, ratio, doublings)
    hold[...] = found

    @pl.when(jnp.logical_not(size < 0.9))
    def _():
        hold[...] = first * unit

    def go_on(state):
        count, last = state
        return jnp.logical_and(count < 64, jnp.logical_not(last < 1e-6))

    def newton(state):
        count, _ = state
        now = hold[...]
        left = unit - dot6(matrix, now)
        hold[...] = now + dot6(now, left)
        return count + 1, jnp.sum(left * left)

    lax.while_loop(go_on, newton, (jnp.int32(0), size))
    return hold[...], size


def guarded(run):
    worst = run(fast)

    @pl.when(jnp.logical_not(worst < 4e-5))
    def _():
        run(careful)


def pack_symmetric(matrix, out):
    half = matrix.shape[0] // 3
    out[0:half, :] = matrix[half : 2 * half, 0 : 2 * half]
    out[half : 2 * half, :] = matrix[2 * half :, 0 : 2 * half]
    out[2 * half : 3 * half, :] = jnp.concatenate(
        [matrix[0:half, 0:half], matrix[2 * half :, 2 * half :]], axis=1
    )


def unpack_symmetric(packed):
    third = packed.shape[0] // 3
    row1 = packed[0:third]
    row2 = packed[third : 2 * third]
    ends = packed[2 * third :]
    b10, b11 = row1[:, :third], row1[:, third:]
    b20, b21 = row2[:, :third], row2[:, third:]
    b00, b22 = ends[:, :third], ends[:, third:]
    return jnp.concatenate(
        [
            jnp.concatenate([b00, b10.T, b20.T], axis=1),
            jnp.concatenate([b10, b11, b21.T], axis=1),
            jnp.concatenate([b20, b21, b22], axis=1),
        ],
        axis=0,
    )


def place():
    slab, slabs = lax.axis_index("slab"), lax.axis_size("slab")
    left = slab < slabs // 2
    return slab, left, jnp.where(left, slab, slabs - 1 - slab)


def following(ahead):
    even, odd = ahead
    return jnp.where(lax.axis_index("slab") % 2 == 0, even[0], odd[0])


def take_block(message, couple, ahead, left):
    link_t = jnp.where(left, couple[0].T, following(ahead))
    link = jnp.where(left, couple[0], following(ahead).T)
    return dot3(link, dot3(unpack_symmetric(message[...]), link_t))


def take_column(message, couple, ahead, left):
    return dot3(jnp.where(left, couple[0], following(ahead).T), message[...])


def stage_kernel(step, diag_far, couple_far, probes_far, energy, *rest):
    if step > 0:
        message, sources, even, odd, rest = rest[0], rest[1], rest[2], rest[3], rest[4:]
    factor_p, value_p, inverse_p, matrix_q, source_q, inverse_q, value_q, out = rest[:8]
    hold, diag, couple, probes, sems = rest[8:]
    _, left, distance = place()
    forward = lax.axis_index("slab") <= lax.axis_size("slab") // 2
    first = jnp.where(forward, 0, 1)
    width = diag.shape[1]
    loads = [
        pltpu.make_async_copy(diag_far.at[first], diag.at[0], sems.at[0]),
        pltpu.make_async_copy(couple_far, couple, sems.at[1]),
        pltpu.make_async_copy(probes_far, probes, sems.at[2]),
        pltpu.make_async_copy(diag_far.at[1 - first], diag.at[1], sems.at[3]),
    ]
    for load in loads:
        load.start()
    loads[0].wait()
    if step > 0:
        loads[1].wait()
    shift = sigma_base + sigma_step * energy[...].astype(F32)
    shifted = shift * eye(width)
    sp = diag[0] + shifted
    if step > 0:
        taken = jnp.logical_and(distance >= 1, distance <= step)
        ahead = (even, odd)
        sp = sp - jnp.where(taken, take_block(message, couple, ahead, left), 0.0)
        extra = jnp.where(taken, take_column(sources, couple, ahead, left), 0.0)

    def run(invert):
        xp, size_p = invert(sp, hold, 1 / 12, 4)
        inverse_p[...] = xp
        if invert is fast:
            for load in loads[2 if step > 0 else 1 :]:
                load.wait()
        rp = probes[pl.ds(pl.multiple_of(first * width, width), width), :]
        rq = probes[pl.ds(pl.multiple_of((1 - first) * width, width), width), :]
        if step > 0:
            rp = rp - extra
        inner = couple[1]
        inner_t = inner.T
        apq = jnp.where(forward, inner_t, inner)
        aqp = jnp.where(forward, inner, inner_t)
        fp = dot3(xp, apq)
        yp = dot3(xp, rp)
        factor_p[...] = fp
        value_p[...] = yp
        sq = diag[1] + shifted - dot3(aqp, fp)
        source = rq - dot3(aqp, yp)
        matrix_q[...] = sq
        source_q[...] = source
        xq, size_q = invert(sq, hold, 1 / 12, 4)
        yq = dot3(xq, source)
        inverse_q[...] = xq
        value_q[...] = yq
        pack_symmetric(xq, out)
        return jnp.maximum(size_p, size_q)

    guarded(run)


def pack_full(matrix, out):
    n = matrix.shape[0]
    lanes = out.shape[1]
    out[0:n, :] = matrix[:, 0:lanes]
    out[n : n + n // 2, :] = jnp.concatenate(
        [matrix[0 : n // 2, lanes:], matrix[n // 2 :, lanes:]], axis=1
    )


def unpack_full(packed, n):
    rest = packed[n : n + n // 2]
    lanes = packed.shape[1]
    tail = jnp.concatenate([rest[:, : n - lanes], rest[:, n - lanes :]], axis=0)
    return jnp.concatenate([packed[0:n], tail], axis=1)


def spots(index, rows_all, depth, pitch, across, first_z, first_x):
    plane = rows_all * across
    z = index // plane - first_z
    x = index // across % rows_all - first_x
    y = index % across
    inside = (z >= 0) & (z < depth) & (x >= 0) & (x < pitch)
    row = jnp.where(inside, z * pitch + x, -1)
    n = index.shape[1]
    pick_row = lax.broadcasted_iota(jnp.int32, (depth * pitch, n), 0) == row
    pick_y = lax.broadcasted_iota(jnp.int32, (across, n), 0) == y
    return pick_row.astype(F32).astype(BF16), pick_y.astype(F32)


def region_start(depth_here, rows_here):
    first_z = lax.axis_index("slab") * depth_here - SWEEPS
    return first_z, lax.axis_index("energy") * rows_here - SWEEPS


def ready_kernel(energy, diag, couple, probes, factor_p, value_p, inverse_p, matrix_q, source_q,
                 matrix, source, link, base, base_source, reach, out):
    slab, _, distance = place()
    half = lax.axis_size("slab") // 2
    width = diag.shape[1]
    packed = width + width // 2

    @pl.when(slab == half)
    def _():
        behind = couple[0]
        behind_t = behind.T
        across = dot3(inverse_p[...], behind)
        reach[...] = across
        matrix[...] = matrix_q[...]
        source[...] = source_q[...]
        link[...] = dot3(couple[1], across)
        base[...] = dot3(behind_t, across)
        base_source[...] = dot3(behind_t, value_p[...])

    @pl.when(slab == half - 1)
    def _():
        shift = sigma_base + sigma_step * energy[...].astype(F32)
        shifted = shift * eye(width)
        matrix[...] = diag[0] + shifted
        source[...] = probes[0:width, :]
        link[...] = couple[1].T
        base[...] = diag[1] + shifted
        base_source[...] = probes[width : 2 * width, :]

    @pl.when(distance < half - 1)
    def _():
        pack_full(factor_p[...], out)
        out[packed : packed + width, :] = value_p[...]


def deposit_kernel(rows_all, pitch, depth, rows_here, dopants, dopant):
    first_z, first_x = region_start(depth, rows_here)
    rows, ys = spots(dopants[...], rows_all, depth + 2 * SWEEPS, pitch, dopant.shape[1], first_z,
                     first_x)
    dopant[...] = dopant_charge * one_pass(rows, ys.astype(BF16), NT)


def halo_kernel(potential, got_even, got_odd, wide, near_planes, far_planes):
    depth, rows_here, across = potential.shape
    even_e = lax.axis_index("energy") % 2 == 0
    below = jnp.where(even_e, got_odd[...], got_even[...])
    above = jnp.where(even_e, got_even[...], got_odd[...])
    spare = wide.shape[1] - rows_here - 2 * SWEEPS
    parts = [below, potential[...], above]
    if spare > 0:
        parts.append(jnp.zeros((depth, spare, across), F32))
    wide[...] = jnp.concatenate(parts, axis=1)
    even = lax.axis_index("slab") % 2 == 0
    put_planes(near_planes, 0, wide, even)
    put_planes(far_planes, 0, wide, jnp.logical_not(even))


def put_planes(out, start, wide, high):
    pitch = wide.shape[1]
    last = wide.shape[0] - SWEEPS
    for k in range(SWEEPS):
        plane = jnp.where(high, wide[last + k], wide[k])
        out[start + k * pitch : start + (k + 1) * pitch, :] = plane


def middle_slab():
    slab, left, _ = place()
    half = lax.axis_size("slab") // 2
    return jnp.logical_or(slab == half - 1, slab == half), left


def centre_kernel(couple, even, odd, message, matrix, link, base, solved, factor, total, out,
                  hold):
    here, left = middle_slab()

    @pl.when(here)
    def _():
        block = matrix[...] - take_block(message, couple, (even, odd), left)
        near = link[...]
        near_t = near.T
        sign = jnp.where(left, -1.0, 1.0)

        def run(invert):
            found, size = invert(block, hold, 1 / 12, 4)
            reach = dot3(found, near)
            both = base[...] + sign * dot3(near_t, reach)
            pack_symmetric(both, out)
            solved[...] = found
            factor[...] = reach
            total[...] = both
            return size

        guarded(run)


def source_kernel(couple, even, odd, message, source, link, base_source, solved, value, total):
    here, left = middle_slab()

    @pl.when(here)
    def _():
        right_side = source[...] - take_column(message, couple, (even, odd), left)
        found = dot3(solved[...], right_side)
        value[...] = found
        total[...] = base_source[...] - dot3(link[...].T, found)


def expand_kernel(couple, even, odd, letter, sources, second, factor, value, factor_p, value_p,
                  reach, slope, offset):
    slab, left, _ = place()
    half = lax.axis_size("slab") // 2
    width = value.shape[0]
    packed = width + width // 2

    def put(block, m, v):
        at = pl.ds(pl.multiple_of(block * width, width), width)
        slope[at, :] = m
        offset[at, :] = v

    @pl.when(jnp.logical_or(slab == half - 1, slab == half))
    def _():
        own = jnp.where(left, 0, 1)
        m1 = jnp.where(left, -1.0, 1.0) * factor[...]
        v1 = value[...]
        put(own, m1, v1)

        @pl.when(left)
        def _():
            put(1, eye(width), jnp.zeros_like(v1))

        @pl.when(jnp.logical_not(left))
        def _():
            put(0, -(dot3(factor_p[...], m1) + reach[...]), value_p[...] - dot3(factor_p[...], v1))

        link = jnp.where(left, couple[0].T, following((even, odd)))
        carry = dot3(unpack_symmetric(letter[...]), link)
        mq = -dot3(carry, m1)
        vq = sources[...] - dot3(carry, v1)
        put(jnp.where(left, 3, 2), mq, vq)
        outer = unpack_full(second[0:packed, :], width)
        put(jnp.where(left, 2, 3), -dot3(outer, mq),
            second[packed : packed + width, :] - dot3(outer, vq))


def join_kernel(message, total, inverse, hold):
    here, left = middle_slab()

    @pl.when(here)
    def _():
        sign = jnp.where(left, -1.0, 1.0)
        matrix = sign * (unpack_symmetric(message[...]) - total[...])

        def run(invert):
            found, size = invert(matrix, hold, 1 / 48, 5)
            inverse[...] = found
            return size

        guarded(run)


def join_solution(message, inverse, total, left):
    sign = jnp.where(left, -1.0, 1.0)
    return dot3(inverse[...], sign * (message[...] - total[...]))


def density_kernel(message, inverse, total, slope, offset, probes, probes_near, dens):
    here, left = middle_slab()

    @pl.when(here)
    def _():
        middle = join_solution(message, inverse, total, left)
        values = offset[...] + dot3(slope[...], middle)
        n = probes.shape[0]
        terms = jnp.concatenate([probes[...] * values[:n], probes_near[...] * values[n:]], axis=0)
        dens[...] = dot6(jnp.ones((8, terms.shape[1]), F32), terms, NT)[0:1]


def middle_kernel(message, inverse, total, factor, value, out_first, out_middle):
    here, left = middle_slab()

    @pl.when(here)
    def _():
        middle = join_solution(message, inverse, total, left)
        sign = jnp.where(left, -1.0, 1.0)
        out_first[...] = value[...] + sign * dot3(factor[...], middle)
        out_middle[...] = middle


def back_kernel(step, couple, even, odd, probes, message, first, middle, known_p, known_q,
                factor_p, value_p, inverse_q, value_q, reach, out_p, out_q, dens):
    _, left, distance = place()
    centre = lax.axis_size("slab") // 2 - 1
    width = couple.shape[1]

    @pl.when(jnp.logical_and(distance < centre, distance != step))
    def _():
        out_p[...] = known_p[...]
        out_q[...] = known_q[...]

    @pl.when(distance == step)
    def _():
        link = jnp.where(left, following((even, odd)).T, couple[0])
        xq = value_q[...] - dot3(inverse_q[...], dot3(link, message[...]))
        out_q[...] = xq
        out_p[...] = value_p[...] - dot3(factor_p[...], xq)

    @pl.when(jnp.logical_and(distance == centre, left))
    def _():
        out_p[...] = first[...]
        out_q[...] = middle[...]

    @pl.when(jnp.logical_and(distance == centre, jnp.logical_not(left)))
    def _():
        xb = first[...]
        out_p[...] = xb
        out_q[...] = value_p[...] - dot3(factor_p[...], xb) - dot3(reach[...], middle[...])

    xp = out_p[...]
    xq = out_q[...]
    xa = jnp.where(left, xp, xq)
    xb = jnp.where(left, xq, xp)
    terms = jnp.concatenate([probes[0:width, :] * xa, probes[width:, :] * xb], axis=0)
    dens[...] = dot6(jnp.ones((8, terms.shape[1]), F32), terms, NT)[0:1]


def total_kernel(scale, cells, *rest):
    parts, out = rest[:-1], rest[-1]
    total = parts[0][0:1, :]
    for part in parts[1:]:
        total = total + part[0:1, :]
    out[0:1, :] = total * scale
    out[1:2, 0 : cells.shape[1]] = cells[...].astype(F32)


def poisson_kernel(rows_all, planes, paired, packet, near, far, dopant_grid, wide, near_letter,
                   far_letter, out, density):
    slab, slabs = lax.axis_index("slab"), lax.axis_size("slab")
    depth, pitch, across = wide.shape
    depth = depth + 2 * SWEEPS
    first_z, first_x = region_start(out.shape[0], out.shape[1])
    n = density.shape[0]
    even = slab % 2 == 0
    alone = jnp.logical_or(slab == 0, slab == slabs - 1)
    own, beside, beyond = packet[0:1, 0:n], near[0:1, 0:n], far[0:1, 0:n]
    if paired:
        own = jnp.where(alone, near[0:1, n : 2 * n], own)
        beside = jnp.where(alone, beside, packet[0:1, n : 2 * n])
    density[...] = own.reshape(n)
    weights = jnp.concatenate([own, beside, jnp.where(alone, 0.0, beyond)], axis=1)
    orbitals = jnp.concatenate([packet[1:2, 0:n], near[1:2, 0:n], far[1:2, 0:n]], axis=1)
    orbitals = jnp.where(jnp.abs(orbitals) < 2.0**30, orbitals, -1.0).astype(jnp.int32)
    rows, ys = spots(orbitals, rows_all, depth, pitch, across, first_z, first_x)
    spread = ys * weights
    h = spread.astype(BF16)
    rest = spread - h.astype(F32)
    m = rest.astype(BF16)
    low = (rest - m.astype(F32)).astype(BF16)
    electron = one_pass(rows, h, NT) + (one_pass(rows, m, NT) + one_pass(rows, low, NT))
    electron = electron.reshape(depth, pitch, across)
    dopant = dopant_grid[...].reshape(depth, pitch, across)
    near_planes = near_letter[...].reshape(SWEEPS, pitch, across)
    far_planes = far_letter[...].reshape(SWEEPS, pitch, across)
    start = jnp.concatenate(
        [jnp.where(even, far_planes, near_planes), wide[...],
         jnp.where(even, near_planes, far_planes)],
        axis=0,
    )
    zs = lax.broadcasted_iota(jnp.int32, start.shape, 0) + first_z
    xs = lax.broadcasted_iota(jnp.int32, start.shape, 1) + first_x
    ys = lax.broadcasted_iota(jnp.int32, start.shape, 2)
    exists = (zs >= 0) & (zs < planes) & (xs >= 0) & (xs < rows_all)
    potential = jnp.where(exists, start, 0.0)
    start = potential
    strength = coupling_beta * jnp.abs(electron)
    for _ in range(SWEEPS):
        blank = jnp.zeros((1, pitch, across), F32)
        beside = jnp.concatenate([potential[1:], blank], axis=0)
        beside = beside + jnp.concatenate([blank, potential[:-1]], axis=0)
        beside = beside + pltpu.roll(potential, 1, 1) + pltpu.roll(potential, pitch - 1, 1)
        beside = beside + jnp.where(ys > 0, pltpu.roll(potential, 1, 2), 0.0)
        beside = beside + jnp.where(ys < across - 1, pltpu.roll(potential, across - 1, 2), 0.0)
        growth = jnp.exp(potential - start)
        residual = beside - 6.0 * potential + coupling_beta * (dopant - electron * growth)
        potential = potential + residual / (6.0 + strength * growth)
        potential = jnp.where(exists, potential, 0.0)
    halo = SWEEPS
    out[...] = potential[halo : halo + out.shape[0], halo : halo + out.shape[1], :]


VM = pl.BlockSpec(memory_space=pltpu.VMEM)
FAR = pl.BlockSpec(memory_space=pltpu.HBM)
GRANT = 16 << 20


def like(*shape, dtype=F32):
    return jax.ShapeDtypeStruct(shape, dtype)


def call(kernel, outs, args, scratch=(), distant=0, flops=10**8):
    args = list(args)
    for k in range(distant):
        args[k] = pltpu.with_memory_space_constraint(args[k], pltpu.HBM)
    own = [pltpu.VMEM(shape, F32) for shape in scratch]
    if distant:
        own += [pltpu.SemaphoreType.DMA((distant + 1,))]
    return pl.pallas_call(
        kernel,
        out_shape=outs,
        in_specs=[FAR] * distant + [VM] * (len(args) - distant),
        out_specs=jax.tree.map(lambda _: VM, outs),
        scratch_shapes=own,
        compiler_params=pltpu.CompilerParams(vmem_limit_bytes=GRANT),
        cost_estimate=pl.CostEstimate(flops=flops, bytes_accessed=10**6, transcendentals=0),
    )(*args)


def pairs_of(count, odd):
    found = []
    for first in range(1 if odd else 0, count - 1, 2):
        found += [(first, first + 1), (first + 1, first)]
    return found


def slab_exchange(value, odd):
    slabs, energies = lax.axis_size("slab"), lax.axis_size("energy")
    pairs = pairs_of(slabs, odd)
    busy = {a for a, _ in pairs}
    whole = [(a * energies + e, b * energies + e) for a, b in pairs for e in range(energies)]
    for a in range(slabs):
        if a not in busy:
            whole += [(a * energies + e, a * energies + (e ^ 1)) for e in range(energies)]
    return lax.ppermute(value, ("slab", "energy"), whole)


def energy_exchange(value, odd):
    energies = lax.axis_size("energy")
    pairs = pairs_of(energies, odd)
    if odd:
        pairs += [(energies - 1, 0), (0, energies - 1)]
    return lax.ppermute(value, "energy", pairs)


def program(energy_index, diag_blocks, couple, probes, orbital_cell, dopant_cells, initial_potential):
    width = diag_blocks.shape[1]
    probe_count = probes.shape[1]
    slabs = lax.axis_size("slab")
    energies = lax.axis_size("energy")
    half = slabs // 2
    square, column = like(width, width), like(width, probe_count)
    letter = like(width, probe_count)
    sq = (width, width)

    even = slab_exchange(couple, False)
    paired = half == 2
    odd = even
    if not paired:
        odd = lax.ppermute(couple, "slab", [(s + 1, s) for s in range(1, slabs - 1, 2)])

    message = None
    for t in range(half - 1):
        args = [diag_blocks, couple, probes, energy_index.reshape(1, 1)]
        if t > 0:
            if t > 1:
                _, _, distance = place()
                message = jnp.where(distance == t, message, kept[0])
                sources = jnp.where(distance == t, sources, kept[1])
            kept = message, sources
            args += [message, sources, even, odd]
        state = call(
            functools.partial(stage_kernel, t),
            (square, column, square, square, column, square, column, letter),
            args, (sq, diag_blocks.shape, couple.shape, probes.shape), 3,
        )
        if t == 0:
            prepared = state
        message = slab_exchange(state[-1], t % 2 == 1)
        sources = slab_exchange(state[-2], t % 2 == 1)
    factor_p, value_p, _, _, _, inverse_q, value_q, _ = state

    depth, rows_here, across = initial_potential.shape
    halo = SWEEPS
    rows_all = rows_here * energies
    pitch = -(-(rows_here + 2 * halo) // 8) * 8
    strip = halo * pitch
    odd_e = lax.axis_index("energy") % 2 == 1
    low, high = initial_potential[:, :halo], initial_potential[:, rows_here - halo :]
    got_even = energy_exchange(jnp.where(odd_e, low, high), False)
    got_odd = energy_exchange(jnp.where(odd_e, high, low), True)
    cells = (depth + 2 * halo) * pitch
    matrix, source, link, base, base_source, reach, second = call(
        ready_kernel,
        (square, column, square, square, column, square,
         like(width + width // 2 + width, probe_count)),
        [energy_index.reshape(1, 1), diag_blocks, couple, probes, *prepared[:5]],
    )
    if paired:
        probes_near = slab_exchange(probes, False)
        second = slab_exchange(second, False)
    dopant_grid = call(
        functools.partial(deposit_kernel, rows_all, pitch, depth, rows_here),
        like(cells, across), [dopant_cells.reshape(1, -1)],
    )
    solved, factor, total, sent = call(
        centre_kernel, (square, square, square, letter),
        [couple, even, odd, message, matrix, link, base], (sq,),
    )
    across_middle = slab_exchange(sent, half % 2 == 0)
    value, total_source = call(
        source_kernel, (column, column),
        [couple, even, odd, sources, source, link, base_source, solved],
    )
    sources_middle = slab_exchange(total_source, half % 2 == 0)
    wide, near_planes, far_planes = call(
        halo_kernel,
        (like(depth, pitch, across), like(strip, across), like(strip, across)),
        [initial_potential, *lax.optimization_barrier((got_even, got_odd, sent))[:2]],
    )
    near_planes = slab_exchange(near_planes, False)
    far_planes = slab_exchange(far_planes, True)
    inverse = call(join_kernel, square, [across_middle, total], (sq,))
    if paired:
        slope, offset = call(
            expand_kernel, (like(4 * width, width), like(4 * width, probe_count)),
            [couple, even, odd, message, sources, second, factor, value, prepared[0],
             prepared[1], reach],
        )
        dens = call(
            density_kernel, like(1, 4 * width),
            [sources_middle, inverse, total_source, slope, offset, probes, probes_near],
        )
    else:
        first, middle = call(
            middle_kernel, (column, column),
            [sources_middle, inverse, total_source, factor, value],
        )
        centred = lax.axis_index("slab") == half
        factor_p = jnp.where(centred, prepared[0], factor_p)
        value_p = jnp.where(centred, prepared[1], value_p)
        known_p, known_q = first, middle
        for t in range(half - 2, -1, -1):
            known_p, known_q, dens = call(
                functools.partial(back_kernel, t),
                (column, column, like(1, 2 * width)),
                [couple, even, odd, probes, slab_exchange(known_p, t % 2 == 1), first, middle,
                 known_p, known_q, factor_p, value_p, inverse_q, value_q, reach],
            )
    parts = [dens] + [
        lax.ppermute(dens, "energy", [(e, e ^ k) for e in range(energies)])
        for k in range(1, energies)
    ]
    packet = call(
        functools.partial(total_kernel, 1.0 / (probe_count * energies)),
        like(2, dens.shape[1]), [orbital_cell.reshape(1, -1), *parts],
    )
    near = slab_exchange(packet, False)
    far = slab_exchange(packet, True)

    def poisson(packet, near, far, dopant_grid, wide, near_letter, far_letter, out, density):
        poisson_kernel(rows_all, depth * slabs, paired, packet, near, far, dopant_grid, wide,
                       near_letter, far_letter, out, density)

    potential, density = call(
        poisson, (like(depth, rows_here, across), like(2 * width)),
        [packet, near, far, dopant_grid, wide, near_planes, far_planes],
    )
    return (potential, density)


def solution(mesh):
    placed = (
        P("energy"),
        P(("cfg", "slab"), None, None),
        P(("cfg", "slab"), None, None),
        P("slab", None),
        P("slab"),
        P("cfg"),
        P(("cfg", "slab"), "energy", None),
    )
    return jax.shard_map(
        program,
        mesh=mesh,
        in_specs=placed,
        out_specs=(P(("cfg", "slab"), "energy", None), P(("cfg", "slab"))),
        check_vma=False,
    )
```

```python
import functools

import jax
import jax.numpy as jnp
from jax import lax
from jax.experimental import pallas as pl
from jax.experimental.pallas import tpu as pltpu
from jax.sharding import PartitionSpec as P


SWEEPS = 2

sigma_base = 0.02
sigma_step = 0.01
coupling_beta = 0.5
dopant_charge = 4.0

F32 = jnp.float32
BF16 = jnp.bfloat16
NT = (((1,), (1,)), ((), ()))
NN = (((1,), (0,)), ((), ()))


def split2(a):
    high = a.astype(BF16)
    return high, (a - high.astype(F32)).astype(BF16)


def one_pass(a, b, dims=NN):
    return lax.dot_general(a, b, dims, preferred_element_type=F32)


def dot3(a, b):
    ah, al = split2(a)
    bh, bl = split2(b)
    return one_pass(ah, bh) + (one_pass(ah, bl) + one_pass(al, bh))


def dot6(a, b, dims=NN):
    return lax.dot_general(
        a, b, dims, precision=lax.Precision.HIGHEST, preferred_element_type=F32
    )


def eye(n):
    return (
        lax.broadcasted_iota(jnp.int32, (n, n), 0) == lax.broadcasted_iota(jnp.int32, (n, n), 1)
    ).astype(F32)


def estimate(matrix, ratio, doublings):
    unit = eye(matrix.shape[0])
    square = dot3(matrix, matrix)
    sums = jnp.sum(jnp.abs(square), axis=0, keepdims=True)
    bound = jnp.sqrt(jnp.max(sums, axis=1, keepdims=True))
    first = 2.0 / (bound * (1.0 + ratio))
    tau = (1.0 + ratio) / (1.0 - ratio)
    for k in range(doublings):
        after = 2.0 * tau * tau - 1.0
        scale = (after + 1.0) / after
        if k == 0:
            grown = (2.0 * first) * unit - (first * first) * matrix
            squared = unit - (2.0 * first) * matrix + (first * first) * square
        else:
            grown = guess + dot3(guess, error)
            squared = dot3(error, error) if k + 1 < doublings else None
        guess = scale * grown
        if k + 1 < doublings:
            error = scale * squared - (scale - 1.0) * unit
        tau = after
    residual = unit - dot6(matrix, guess)
    return guess + dot3(guess, residual), jnp.sum(residual * residual), first


def fast(matrix, hold, ratio, doublings):
    found, size, _ = estimate(matrix, ratio, doublings)
    return found, size


def careful(matrix, hold, ratio, doublings):
    unit = eye(matrix.shape[0])
    found, size, first = estimate(matrix, ratio, doublings)
    hold[...] = found

    @pl.when(jnp.logical_not(size < 0.9))
    def _():
        hold[...] = first * unit

    def go_on(state):
        count, last = state
        return jnp.logical_and(count < 64, jnp.logical_not(last < 1e-6))

    def newton(state):
        count, _ = state
        now = hold[...]
        left = unit - dot6(matrix, now)
        hold[...] = now + dot6(now, left)
        return count + 1, jnp.sum(left * left)

    lax.while_loop(go_on, newton, (jnp.int32(0), size))
    return hold[...], size


def guarded(run):
    worst = run(fast)

    @pl.when(jnp.logical_not(worst < 4e-5))
    def _():
        run(careful)


def pack_symmetric(matrix, out):
    half = matrix.shape[0] // 3
    out[0:half, :] = matrix[half : 2 * half, 0 : 2 * half]
    out[half : 2 * half, :] = matrix[2 * half :, 0 : 2 * half]
    out[2 * half : 3 * half, :] = jnp.concatenate(
        [matrix[0:half, 0:half], matrix[2 * half :, 2 * half :]], axis=1
    )


def unpack_symmetric(packed):
    third = packed.shape[0] // 3
    row1 = packed[0:third]
    row2 = packed[third : 2 * third]
    ends = packed[2 * third :]
    b10, b11 = row1[:, :third], row1[:, third:]
    b20, b21 = row2[:, :third], row2[:, third:]
    b00, b22 = ends[:, :third], ends[:, third:]
    return jnp.concatenate(
        [
            jnp.concatenate([b00, b10.T, b20.T], axis=1),
            jnp.concatenate([b10, b11, b21.T], axis=1),
            jnp.concatenate([b20, b21, b22], axis=1),
        ],
        axis=0,
    )


def place():
    slab, slabs = lax.axis_index("slab"), lax.axis_size("slab")
    left = slab < slabs // 2
    return slab, left, jnp.where(left, slab, slabs - 1 - slab)


def following(ahead):
    even, odd = ahead
    return jnp.where(lax.axis_index("slab") % 2 == 0, even[0], odd[0])


def take_block(message, couple, ahead, left):
    link_t = jnp.where(left, couple[0].T, following(ahead))
    link = jnp.where(left, couple[0], following(ahead).T)
    return dot3(link, dot3(unpack_symmetric(message[...]), link_t))


def take_column(message, couple, ahead, left):
    return dot3(jnp.where(left, couple[0], following(ahead).T), message[...])


def stage_kernel(step, diag_far, couple_far, probes_far, energy, *rest):
    if step > 0:
        message, sources, even, odd, rest = rest[0], rest[1], rest[2], rest[3], rest[4:]
    factor_p, value_p, inverse_p, matrix_q, source_q, inverse_q, value_q, out = rest[:8]
    hold, diag, couple, probes, sems = rest[8:]
    _, left, distance = place()
    forward = lax.axis_index("slab") <= lax.axis_size("slab") // 2
    first = jnp.where(forward, 0, 1)
    width = diag.shape[1]
    loads = [
        pltpu.make_async_copy(diag_far.at[first], diag.at[0], sems.at[0]),
        pltpu.make_async_copy(couple_far, couple, sems.at[1]),
        pltpu.make_async_copy(probes_far, probes, sems.at[2]),
        pltpu.make_async_copy(diag_far.at[1 - first], diag.at[1], sems.at[3]),
    ]
    for load in loads:
        load.start()
    loads[0].wait()
    if step > 0:
        loads[1].wait()
    shift = sigma_base + sigma_step * energy[...].astype(F32)
    shifted = shift * eye(width)
    sp = diag[0] + shifted
    if step > 0:
        taken = jnp.logical_and(distance >= 1, distance <= step)
        ahead = (even, odd)
        sp = sp - jnp.where(taken, take_block(message, couple, ahead, left), 0.0)
        extra = jnp.where(taken, take_column(sources, couple, ahead, left), 0.0)

    def run(invert):
        xp, size_p = invert(sp, hold, 1 / 12, 4)
        inverse_p[...] = xp
        if invert is fast:
            for load in loads[2 if step > 0 else 1 :]:
                load.wait()
        rp = probes[pl.ds(pl.multiple_of(first * width, width), width), :]
        rq = probes[pl.ds(pl.multiple_of((1 - first) * width, width), width), :]
        if step > 0:
            rp = rp - extra
        inner = couple[1]
        inner_t = inner.T
        apq = jnp.where(forward, inner_t, inner)
        aqp = jnp.where(forward, inner, inner_t)
        fp = dot3(xp, apq)
        yp = dot3(xp, rp)
        factor_p[...] = fp
        value_p[...] = yp
        sq = diag[1] + shifted - dot3(aqp, fp)
        source = rq - dot3(aqp, yp)
        matrix_q[...] = sq
        source_q[...] = source
        xq, size_q = invert(sq, hold, 1 / 12, 4)
        yq = dot3(xq, source)
        inverse_q[...] = xq
        value_q[...] = yq
        pack_symmetric(xq, out)
        return jnp.maximum(size_p, size_q)

    guarded(run)


def pack_full(matrix, out):
    n = matrix.shape[0]
    lanes = out.shape[1]
    out[0:n, :] = matrix[:, 0:lanes]
    out[n : n + n // 2, :] = jnp.concatenate(
        [matrix[0 : n // 2, lanes:], matrix[n // 2 :, lanes:]], axis=1
    )


def unpack_full(packed, n):
    rest = packed[n : n + n // 2]
    lanes = packed.shape[1]
    tail = jnp.concatenate([rest[:, : n - lanes], rest[:, n - lanes :]], axis=0)
    return jnp.concatenate([packed[0:n], tail], axis=1)


def spots(index, rows_all, depth, pitch, across, first_z, first_x):
    plane = rows_all * across
    z = index // plane - first_z
    x = index // across % rows_all - first_x
    y = index % across
    inside = (z >= 0) & (z < depth) & (x >= 0) & (x < pitch)
    row = jnp.where(inside, z * pitch + x, -1)
    n = index.shape[1]
    pick_row = lax.broadcasted_iota(jnp.int32, (depth * pitch, n), 0) == row
    pick_y = lax.broadcasted_iota(jnp.int32, (across, n), 0) == y
    return pick_row.astype(F32).astype(BF16), pick_y.astype(F32)


def region_start(depth_here, rows_here):
    first_z = lax.axis_index("slab") * depth_here - SWEEPS
    return first_z, lax.axis_index("energy") * rows_here - SWEEPS


def ready_kernel(energy, diag, couple, probes, factor_p, value_p, inverse_p, matrix_q, source_q,
                 matrix, source, link, base, base_source, reach, out):
    slab, _, distance = place()
    half = lax.axis_size("slab") // 2
    width = diag.shape[1]
    packed = width + width // 2

    @pl.when(slab == half)
    def _():
        behind = couple[0]
        behind_t = behind.T
        across = dot3(inverse_p[...], behind)
        reach[...] = across
        matrix[...] = matrix_q[...]
        source[...] = source_q[...]
        link[...] = dot3(couple[1], across)
        base[...] = dot3(behind_t, across)
        base_source[...] = dot3(behind_t, value_p[...])

    @pl.when(slab == half - 1)
    def _():
        shift = sigma_base + sigma_step * energy[...].astype(F32)
        shifted = shift * eye(width)
        matrix[...] = diag[0] + shifted
        source[...] = probes[0:width, :]
        link[...] = couple[1].T
        base[...] = diag[1] + shifted
        base_source[...] = probes[width : 2 * width, :]

    @pl.when(distance < half - 1)
    def _():
        pack_full(factor_p[...], out)
        out[packed : packed + width, :] = value_p[...]


def deposit_kernel(rows_all, pitch, depth, rows_here, dopants, dopant):
    first_z, first_x = region_start(depth, rows_here)
    rows, ys = spots(dopants[...], rows_all, depth + 2 * SWEEPS, pitch, dopant.shape[1], first_z,
                     first_x)
    dopant[...] = dopant_charge * one_pass(rows, ys.astype(BF16), NT)


def halo_kernel(potential, got_even, got_odd, wide):
    depth, rows_here, across = potential.shape
    even_e = lax.axis_index("energy") % 2 == 0
    below = jnp.where(even_e, got_odd[...], got_even[...])
    above = jnp.where(even_e, got_even[...], got_odd[...])
    spare = wide.shape[1] - rows_here - 2 * SWEEPS
    parts = [below, potential[...], above]
    if spare > 0:
        parts.append(jnp.zeros((depth, spare, across), F32))
    wide[...] = jnp.concatenate(parts, axis=1)


def put_planes(out, start, wide, high):
    pitch = wide.shape[1]
    last = wide.shape[0] - SWEEPS
    for k in range(SWEEPS):
        plane = jnp.where(high, wide[last + k], wide[k])
        out[start + k * pitch : start + (k + 1) * pitch, :] = plane


def middle_slab():
    slab, left, _ = place()
    half = lax.axis_size("slab") // 2
    return jnp.logical_or(slab == half - 1, slab == half), left


def centre_kernel(couple, even, odd, message, matrix, link, base, solved, factor, total, out,
                  hold):
    here, left = middle_slab()

    @pl.when(here)
    def _():
        block = matrix[...] - take_block(message, couple, (even, odd), left)
        near = link[...]
        near_t = near.T
        sign = jnp.where(left, -1.0, 1.0)

        def run(invert):
            found, size = invert(block, hold, 1 / 12, 4)
            reach = dot3(found, near)
            both = base[...] + sign * dot3(near_t, reach)
            pack_symmetric(both, out)
            solved[...] = found
            factor[...] = reach
            total[...] = both
            return size

        guarded(run)


def source_kernel(couple, even, odd, message, source, link, base_source, solved, value, total):
    here, left = middle_slab()

    @pl.when(here)
    def _():
        right_side = source[...] - take_column(message, couple, (even, odd), left)
        found = dot3(solved[...], right_side)
        value[...] = found
        total[...] = base_source[...] - dot3(link[...].T, found)


def expand_kernel(couple, even, odd, letter, sources, second, factor, value, factor_p, value_p,
                  reach, slope, offset):
    slab, left, _ = place()
    half = lax.axis_size("slab") // 2
    width = value.shape[0]
    packed = width + width // 2

    def put(block, m, v):
        at = pl.ds(pl.multiple_of(block * width, width), width)
        slope[at, :] = m
        offset[at, :] = v

    @pl.when(jnp.logical_or(slab == half - 1, slab == half))
    def _():
        own = jnp.where(left, 0, 1)
        m1 = jnp.where(left, -1.0, 1.0) * factor[...]
        v1 = value[...]
        put(own, m1, v1)

        @pl.when(left)
        def _():
            put(1, eye(width), jnp.zeros_like(v1))

        @pl.when(jnp.logical_not(left))
        def _():
            put(0, -(dot3(factor_p[...], m1) + reach[...]), value_p[...] - dot3(factor_p[...], v1))

        link = jnp.where(left, couple[0].T, following((even, odd)))
        carry = dot3(unpack_symmetric(letter[...]), link)
        mq = -dot3(carry, m1)
        vq = sources[...] - dot3(carry, v1)
        put(jnp.where(left, 3, 2), mq, vq)
        outer = unpack_full(second[0:packed, :], width)
        put(jnp.where(left, 2, 3), -dot3(outer, mq),
            second[packed : packed + width, :] - dot3(outer, vq))


def join_kernel(message, total, inverse, hold):
    here, left = middle_slab()

    @pl.when(here)
    def _():
        sign = jnp.where(left, -1.0, 1.0)
        matrix = sign * (unpack_symmetric(message[...]) - total[...])

        def run(invert):
            found, size = invert(matrix, hold, 1 / 48, 5)
            inverse[...] = found
            return size

        guarded(run)


def join_solution(message, inverse, total, left):
    sign = jnp.where(left, -1.0, 1.0)
    return dot3(inverse[...], sign * (message[...] - total[...]))


def density_kernel(message, inverse, total, slope, offset, probes, probes_near, dens):
    here, left = middle_slab()

    @pl.when(here)
    def _():
        middle = join_solution(message, inverse, total, left)
        values = offset[...] + dot3(slope[...], middle)
        n = probes.shape[0]
        terms = jnp.concatenate([probes[...] * values[:n], probes_near[...] * values[n:]], axis=0)
        dens[...] = dot6(jnp.ones((8, terms.shape[1]), F32), terms, NT)[0:1]


def middle_kernel(message, inverse, total, factor, value, out_first, out_middle):
    here, left = middle_slab()

    @pl.when(here)
    def _():
        middle = join_solution(message, inverse, total, left)
        sign = jnp.where(left, -1.0, 1.0)
        out_first[...] = value[...] + sign * dot3(factor[...], middle)
        out_middle[...] = middle


def back_kernel(step, couple, even, odd, probes, message, first, middle, known_p, known_q,
                factor_p, value_p, inverse_q, value_q, reach, out_p, out_q, dens):
    _, left, distance = place()
    centre = lax.axis_size("slab") // 2 - 1
    width = couple.shape[1]

    @pl.when(jnp.logical_and(distance < centre, distance != step))
    def _():
        out_p[...] = known_p[...]
        out_q[...] = known_q[...]

    @pl.when(distance == step)
    def _():
        link = jnp.where(left, following((even, odd)).T, couple[0])
        xq = value_q[...] - dot3(inverse_q[...], dot3(link, message[...]))
        out_q[...] = xq
        out_p[...] = value_p[...] - dot3(factor_p[...], xq)

    @pl.when(jnp.logical_and(distance == centre, left))
    def _():
        out_p[...] = first[...]
        out_q[...] = middle[...]

    @pl.when(jnp.logical_and(distance == centre, jnp.logical_not(left)))
    def _():
        xb = first[...]
        out_p[...] = xb
        out_q[...] = value_p[...] - dot3(factor_p[...], xb) - dot3(reach[...], middle[...])

    xp = out_p[...]
    xq = out_q[...]
    xa = jnp.where(left, xp, xq)
    xb = jnp.where(left, xq, xp)
    terms = jnp.concatenate([probes[0:width, :] * xa, probes[width:, :] * xb], axis=0)
    dens[...] = dot6(jnp.ones((8, terms.shape[1]), F32), terms, NT)[0:1]


def total_kernel(scale, cells, wide, *rest):
    parts, outs = rest[:-2], rest[-2:]
    total = parts[0][...]
    for part in parts[1:]:
        total = total + part[...]
    total = total * scale
    place_of = cells[...].astype(F32)
    lanes = wide.shape[2]
    values = total.shape[1] // lanes
    even = lax.axis_index("slab") % 2 == 0
    for out, high in zip(outs, (even, jnp.logical_not(even))):
        for k in range(values):
            out[k : k + 1, :] = total[:, k * lanes : (k + 1) * lanes]
        for k in range(cells.shape[1] // lanes):
            out[values + k : values + k + 1, :] = place_of[:, k * lanes : (k + 1) * lanes]
        put_planes(out, packet_planes(values, cells.shape[1] // lanes), wide, high)


def packet_planes(values, cells):
    return -(-(values + cells) // 8) * 8


def packet_row(packet, first, count):
    return jnp.concatenate([packet[first + k : first + k + 1, :] for k in range(count)], axis=1)


def poisson_kernel(rows_all, planes, paired, packet, near, far, dopant_grid, wide, out, density):
    slab, slabs = lax.axis_index("slab"), lax.axis_size("slab")
    depth, pitch, across = wide.shape
    depth = depth + 2 * SWEEPS
    first_z, first_x = region_start(out.shape[0], out.shape[1])
    n = density.shape[0]
    even = slab % 2 == 0
    alone = jnp.logical_or(slab == 0, slab == slabs - 1)
    count = n // across
    values = 2 * count if paired else count
    own, beside, beyond = [packet_row(p, 0, count) for p in (packet, near, far)]
    if paired:
        own = jnp.where(alone, packet_row(near, count, count), own)
        beside = jnp.where(alone, beside, packet_row(packet, count, count))
    density[...] = own.reshape(n)
    weights = jnp.concatenate([own, beside, jnp.where(alone, 0.0, beyond)], axis=1)
    orbitals = jnp.concatenate([packet_row(p, values, count) for p in (packet, near, far)], axis=1)
    orbitals = jnp.where(jnp.abs(orbitals) < 2.0**30, orbitals, -1.0).astype(jnp.int32)
    rows, ys = spots(orbitals, rows_all, depth, pitch, across, first_z, first_x)
    spread = ys * weights
    h = spread.astype(BF16)
    rest = spread - h.astype(F32)
    m = rest.astype(BF16)
    low = (rest - m.astype(F32)).astype(BF16)
    electron = one_pass(rows, h, NT) + (one_pass(rows, m, NT) + one_pass(rows, low, NT))
    electron = electron.reshape(depth, pitch, across)
    dopant = dopant_grid[...].reshape(depth, pitch, across)
    near_planes = near[packet_planes(values, count) :, :].reshape(SWEEPS, pitch, across)
    far_planes = far[packet_planes(values, count) :, :].reshape(SWEEPS, pitch, across)
    start = jnp.concatenate(
        [jnp.where(even, far_planes, near_planes), wide[...],
         jnp.where(even, near_planes, far_planes)],
        axis=0,
    )
    zs = lax.broadcasted_iota(jnp.int32, start.shape, 0) + first_z
    xs = lax.broadcasted_iota(jnp.int32, start.shape, 1) + first_x
    ys = lax.broadcasted_iota(jnp.int32, start.shape, 2)
    exists = (zs >= 0) & (zs < planes) & (xs >= 0) & (xs < rows_all)
    potential = jnp.where(exists, start, 0.0)
    start = potential
    strength = coupling_beta * jnp.abs(electron)
    for _ in range(SWEEPS):
        blank = jnp.zeros((1, pitch, across), F32)
        beside = jnp.concatenate([potential[1:], blank], axis=0)
        beside = beside + jnp.concatenate([blank, potential[:-1]], axis=0)
        beside = beside + pltpu.roll(potential, 1, 1) + pltpu.roll(potential, pitch - 1, 1)
        beside = beside + jnp.where(ys > 0, pltpu.roll(potential, 1, 2), 0.0)
        beside = beside + jnp.where(ys < across - 1, pltpu.roll(potential, across - 1, 2), 0.0)
        growth = jnp.exp(potential - start)
        residual = beside - 6.0 * potential + coupling_beta * (dopant - electron * growth)
        potential = potential + residual / (6.0 + strength * growth)
        potential = jnp.where(exists, potential, 0.0)
    halo = SWEEPS
    out[...] = potential[halo : halo + out.shape[0], halo : halo + out.shape[1], :]


VM = pl.BlockSpec(memory_space=pltpu.VMEM)
FAR = pl.BlockSpec(memory_space=pltpu.HBM)
GRANT = 16 << 20


def like(*shape, dtype=F32):
    return jax.ShapeDtypeStruct(shape, dtype)


def call(kernel, outs, args, scratch=(), distant=0, flops=10**8):
    args = list(args)
    for k in range(distant):
        args[k] = pltpu.with_memory_space_constraint(args[k], pltpu.HBM)
    own = [pltpu.VMEM(shape, F32) for shape in scratch]
    if distant:
        own += [pltpu.SemaphoreType.DMA((distant + 1,))]
    return pl.pallas_call(
        kernel,
        out_shape=outs,
        in_specs=[FAR] * distant + [VM] * (len(args) - distant),
        out_specs=jax.tree.map(lambda _: VM, outs),
        scratch_shapes=own,
        compiler_params=pltpu.CompilerParams(vmem_limit_bytes=GRANT),
        cost_estimate=pl.CostEstimate(flops=flops, bytes_accessed=10**6, transcendentals=0),
    )(*args)


def pairs_of(count, odd):
    found = []
    for first in range(1 if odd else 0, count - 1, 2):
        found += [(first, first + 1), (first + 1, first)]
    return found


def slab_exchange(value, odd):
    slabs, energies = lax.axis_size("slab"), lax.axis_size("energy")
    pairs = pairs_of(slabs, odd)
    busy = {a for a, _ in pairs}
    whole = [(a * energies + e, b * energies + e) for a, b in pairs for e in range(energies)]
    for a in range(slabs):
        if a not in busy:
            whole += [(a * energies + e, a * energies + (e ^ 1)) for e in range(energies)]
    return lax.ppermute(value, ("slab", "energy"), whole)


def energy_exchange(value, odd):
    energies = lax.axis_size("energy")
    pairs = pairs_of(energies, odd)
    if odd:
        pairs += [(energies - 1, 0), (0, energies - 1)]
    return lax.ppermute(value, "energy", pairs)


def program(energy_index, diag_blocks, couple, probes, orbital_cell, dopant_cells, initial_potential):
    width = diag_blocks.shape[1]
    probe_count = probes.shape[1]
    slabs = lax.axis_size("slab")
    energies = lax.axis_size("energy")
    half = slabs // 2
    square, column = like(width, width), like(width, probe_count)
    letter = like(width, probe_count)
    sq = (width, width)

    even = slab_exchange(couple, False)
    paired = half == 2
    odd = even
    if not paired:
        odd = lax.ppermute(couple, "slab", [(s + 1, s) for s in range(1, slabs - 1, 2)])

    message = None
    for t in range(half - 1):
        args = [diag_blocks, couple, probes, energy_index.reshape(1, 1)]
        if t > 0:
            if t > 1:
                _, _, distance = place()
                message = jnp.where(distance == t, message, kept[0])
                sources = jnp.where(distance == t, sources, kept[1])
            kept = message, sources
            args += [message, sources, even, odd]
        state = call(
            functools.partial(stage_kernel, t),
            (square, column, square, square, column, square, column, letter),
            args, (sq, diag_blocks.shape, couple.shape, probes.shape), 3,
        )
        if t == 0:
            prepared = state
        message = slab_exchange(state[-1], t % 2 == 1)
        sources = slab_exchange(state[-2], t % 2 == 1)
    factor_p, value_p, _, _, _, inverse_q, value_q, _ = state

    depth, rows_here, across = initial_potential.shape
    halo = SWEEPS
    rows_all = rows_here * energies
    pitch = -(-(rows_here + 2 * halo) // 8) * 8
    strip = halo * pitch
    odd_e = lax.axis_index("energy") % 2 == 1
    low, high = initial_potential[:, :halo], initial_potential[:, rows_here - halo :]
    got_even = energy_exchange(jnp.where(odd_e, low, high), False)
    got_odd = energy_exchange(jnp.where(odd_e, high, low), True)
    cells = (depth + 2 * halo) * pitch
    matrix, source, link, base, base_source, reach, second = call(
        ready_kernel,
        (square, column, square, square, column, square,
         like(width + width // 2 + width, probe_count)),
        [energy_index.reshape(1, 1), diag_blocks, couple, probes, *prepared[:5]],
    )
    if paired:
        probes_near = slab_exchange(probes, False)
        second = slab_exchange(second, False)
    dopant_grid = call(
        functools.partial(deposit_kernel, rows_all, pitch, depth, rows_here),
        like(cells, across), [dopant_cells.reshape(1, -1)],
    )
    solved, factor, total, sent = call(
        centre_kernel, (square, square, square, letter),
        [couple, even, odd, message, matrix, link, base], (sq,),
    )
    across_middle = slab_exchange(sent, half % 2 == 0)
    value, total_source = call(
        source_kernel, (column, column),
        [couple, even, odd, sources, source, link, base_source, solved],
    )
    sources_middle = slab_exchange(total_source, half % 2 == 0)
    wide = call(
        halo_kernel, like(depth, pitch, across),
        [initial_potential, *lax.optimization_barrier((got_even, got_odd, sent))[:2]],
    )
    inverse = call(join_kernel, square, [across_middle, total], (sq,))
    if paired:
        slope, offset = call(
            expand_kernel, (like(4 * width, width), like(4 * width, probe_count)),
            [couple, even, odd, message, sources, second, factor, value, prepared[0],
             prepared[1], reach],
        )
        dens = call(
            density_kernel, like(1, 4 * width),
            [sources_middle, inverse, total_source, slope, offset, probes, probes_near],
        )
    else:
        first, middle = call(
            middle_kernel, (column, column),
            [sources_middle, inverse, total_source, factor, value],
        )
        centred = lax.axis_index("slab") == half
        factor_p = jnp.where(centred, prepared[0], factor_p)
        value_p = jnp.where(centred, prepared[1], value_p)
        known_p, known_q = first, middle
        for t in range(half - 2, -1, -1):
            known_p, known_q, dens = call(
                functools.partial(back_kernel, t),
                (column, column, like(1, 2 * width)),
                [couple, even, odd, probes, slab_exchange(known_p, t % 2 == 1), first, middle,
                 known_p, known_q, factor_p, value_p, inverse_q, value_q, reach],
            )
    parts = [dens] + [
        lax.ppermute(dens, "energy", [(e, e ^ k) for e in range(energies)])
        for k in range(1, energies)
    ]
    spare = packet_planes(dens.shape[1] // across, orbital_cell.shape[0] // across)
    packet, packet_far = call(
        functools.partial(total_kernel, 1.0 / (probe_count * energies)),
        (like(spare + strip, across),) * 2, [orbital_cell.reshape(1, -1), wide, *parts],
    )
    near = slab_exchange(packet, False)
    far = slab_exchange(packet_far, True)

    def poisson(*refs):
        poisson_kernel(rows_all, depth * slabs, paired, *refs)

    potential, density = call(
        poisson, (like(depth, rows_here, across), like(2 * width)),
        [packet, near, far, dopant_grid, wide],
    )
    return (potential, density)


def solution(mesh):
    placed = (
        P("energy"),
        P(("cfg", "slab"), None, None),
        P(("cfg", "slab"), None, None),
        P("slab", None),
        P("slab"),
        P("cfg"),
        P(("cfg", "slab"), "energy", None),
    )
    return jax.shard_map(
        program,
        mesh=mesh,
        in_specs=placed,
        out_specs=(P(("cfg", "slab"), "energy", None), P(("cfg", "slab"))),
        check_vma=False,
    )
```

```python
import functools

import jax
import jax.numpy as jnp
from jax import lax
from jax.experimental import pallas as pl
from jax.experimental.pallas import tpu as pltpu
from jax.sharding import PartitionSpec as P


SWEEPS = 2

sigma_base = 0.02
sigma_step = 0.01
coupling_beta = 0.5
dopant_charge = 4.0

F32 = jnp.float32
BF16 = jnp.bfloat16
NT = (((1,), (1,)), ((), ()))
NN = (((1,), (0,)), ((), ()))


def split2(a):
    high = a.astype(BF16)
    return high, (a - high.astype(F32)).astype(BF16)


def one_pass(a, b, dims=NN):
    return lax.dot_general(a, b, dims, preferred_element_type=F32)


def dot3(a, b):
    ah, al = split2(a)
    bh, bl = split2(b)
    return one_pass(ah, bh) + (one_pass(ah, bl) + one_pass(al, bh))


def dot6(a, b, dims=NN):
    return lax.dot_general(
        a, b, dims, precision=lax.Precision.HIGHEST, preferred_element_type=F32
    )


def eye(n):
    return (
        lax.broadcasted_iota(jnp.int32, (n, n), 0) == lax.broadcasted_iota(jnp.int32, (n, n), 1)
    ).astype(F32)


def estimate(matrix, ratio, doublings):
    unit = eye(matrix.shape[0])
    square = dot3(matrix, matrix)
    sums = jnp.sum(jnp.abs(square), axis=0, keepdims=True)
    bound = jnp.sqrt(jnp.max(sums, axis=1, keepdims=True))
    first = 2.0 / (bound * (1.0 + ratio))
    tau = (1.0 + ratio) / (1.0 - ratio)
    for k in range(doublings):
        after = 2.0 * tau * tau - 1.0
        scale = (after + 1.0) / after
        if k == 0:
            grown = (2.0 * first) * unit - (first * first) * matrix
            squared = unit - (2.0 * first) * matrix + (first * first) * square
        else:
            grown = guess + dot3(guess, error)
            squared = dot3(error, error) if k + 1 < doublings else None
        guess = scale * grown
        if k + 1 < doublings:
            error = scale * squared - (scale - 1.0) * unit
        tau = after
    residual = unit - dot6(matrix, guess)
    step = one_pass(guess.astype(BF16), residual.astype(BF16))
    return guess + step, jnp.sum(residual * residual), first


def fast(matrix, hold, ratio, doublings):
    found, size, _ = estimate(matrix, ratio, doublings)
    return found, size


def careful(matrix, hold, ratio, doublings):
    unit = eye(matrix.shape[0])
    found, size, first = estimate(matrix, ratio, doublings)
    hold[...] = found

    @pl.when(jnp.logical_not(size < 0.9))
    def _():
        hold[...] = first * unit

    def go_on(state):
        count, last = state
        return jnp.logical_and(count < 64, jnp.logical_not(last < 1e-6))

    def newton(state):
        count, _ = state
        now = hold[...]
        left = unit - dot6(matrix, now)
        hold[...] = now + dot6(now, left)
        return count + 1, jnp.sum(left * left)

    lax.while_loop(go_on, newton, (jnp.int32(0), size))
    return hold[...], size


def guarded(run):
    worst = run(fast)

    @pl.when(jnp.logical_not(worst < 4e-5))
    def _():
        run(careful)


def pack_symmetric(matrix, out):
    half = matrix.shape[0] // 3
    out[0:half, :] = matrix[half : 2 * half, 0 : 2 * half]
    out[half : 2 * half, :] = matrix[2 * half :, 0 : 2 * half]
    out[2 * half : 3 * half, :] = jnp.concatenate(
        [matrix[0:half, 0:half], matrix[2 * half :, 2 * half :]], axis=1
    )


def unpack_symmetric(packed):
    third = packed.shape[0] // 3
    row1 = packed[0:third]
    row2 = packed[third : 2 * third]
    ends = packed[2 * third :]
    b10, b11 = row1[:, :third], row1[:, third:]
    b20, b21 = row2[:, :third], row2[:, third:]
    b00, b22 = ends[:, :third], ends[:, third:]
    return jnp.concatenate(
        [
            jnp.concatenate([b00, b10.T, b20.T], axis=1),
            jnp.concatenate([b10, b11, b21.T], axis=1),
            jnp.concatenate([b20, b21, b22], axis=1),
        ],
        axis=0,
    )


def place():
    slab, slabs = lax.axis_index("slab"), lax.axis_size("slab")
    left = slab < slabs // 2
    return slab, left, jnp.where(left, slab, slabs - 1 - slab)


def following(ahead):
    even, odd = ahead
    return jnp.where(lax.axis_index("slab") % 2 == 0, even[0], odd[0])


def take_block(message, couple, ahead, left):
    link_t = jnp.where(left, couple[0].T, following(ahead))
    link = jnp.where(left, couple[0], following(ahead).T)
    return dot3(link, dot3(unpack_symmetric(message[...]), link_t))


def take_column(message, couple, ahead, left):
    return dot3(jnp.where(left, couple[0], following(ahead).T), message[...])


def stage_kernel(step, inner_too, diag_far, couple_far, probes_far, energy, *rest):
    if step > 0:
        message, sources, even, odd, rest = rest[0], rest[1], rest[2], rest[3], rest[4:]
    factor_p, value_p, inverse_p, matrix_q, source_q, out = rest[:6]
    rest = rest[6:]
    if inner_too:
        inverse_q, value_q, out_inverse = rest[:3]
        rest = rest[3:]
    hold, diag, couple, probes, sems = rest
    _, left, distance = place()
    forward = lax.axis_index("slab") <= lax.axis_size("slab") // 2
    first = jnp.where(forward, 0, 1)
    width = diag.shape[1]
    loads = [
        pltpu.make_async_copy(diag_far.at[first], diag.at[0], sems.at[0]),
        pltpu.make_async_copy(couple_far, couple, sems.at[1]),
        pltpu.make_async_copy(probes_far, probes, sems.at[2]),
        pltpu.make_async_copy(diag_far.at[1 - first], diag.at[1], sems.at[3]),
    ]
    for load in loads:
        load.start()
    loads[0].wait()
    if step > 0:
        loads[1].wait()
    shift = sigma_base + sigma_step * energy[...].astype(F32)
    shifted = shift * eye(width)
    sp = diag[0] + shifted
    if step > 0:
        taken = jnp.logical_and(distance >= 1, distance <= step)
        ahead = (even, odd)
        sp = sp - jnp.where(taken, take_block(message, couple, ahead, left), 0.0)
        extra = jnp.where(taken, take_column(sources, couple, ahead, left), 0.0)

    def await_loads():
        for load in loads[2 if step > 0 else 1 :]:
            load.wait()

    def outer_block(invert):
        xp, size = invert(sp, hold, 1 / 12, 4)
        if invert is fast:
            await_loads()
        rp = probes[pl.ds(pl.multiple_of(first * width, width), width), :]
        rq = probes[pl.ds(pl.multiple_of((1 - first) * width, width), width), :]
        if step > 0:
            rp = rp - extra
        inner = couple[1]
        inner_t = inner.T
        apq = jnp.where(forward, inner_t, inner)
        aqp = jnp.where(forward, inner, inner_t)
        fp = dot3(xp, apq)
        yp = dot3(xp, rp)
        factor_p[...] = fp
        value_p[...] = yp
        sq = diag[1] + shifted - dot3(aqp, fp)
        return xp, yp, sq, rq - dot3(aqp, yp), size

    def run(invert):
        xp, _, sq, reduced, size = outer_block(invert)
        inverse_p[...] = xp
        matrix_q[...] = sq
        source_q[...] = reduced
        pack_symmetric(sq, out)
        if inner_too:
            xq, size_q = invert(sq, hold, 1 / 12, 4)
            inverse_q[...] = xq
            value_q[...] = dot3(xq, reduced)
            pack_symmetric(xq, out_inverse)
            size = jnp.maximum(size, size_q)
        return size

    guarded(run)


def pack_full(matrix, out):
    n = matrix.shape[0]
    lanes = out.shape[1]
    out[0:n, :] = matrix[:, 0:lanes]
    out[n : n + n // 2, :] = jnp.concatenate(
        [matrix[0 : n // 2, lanes:], matrix[n // 2 :, lanes:]], axis=1
    )


def unpack_full(packed, n):
    rest = packed[n : n + n // 2]
    lanes = packed.shape[1]
    tail = jnp.concatenate([rest[:, : n - lanes], rest[:, n - lanes :]], axis=0)
    return jnp.concatenate([packed[0:n], tail], axis=1)


def spots(index, rows_all, depth, pitch, across, first_z, first_x):
    plane = rows_all * across
    z = index // plane - first_z
    x = index // across % rows_all - first_x
    y = index % across
    inside = (z >= 0) & (z < depth) & (x >= 0) & (x < pitch)
    row = jnp.where(inside, z * pitch + x, -1)
    n = index.shape[1]
    pick_row = lax.broadcasted_iota(jnp.int32, (depth * pitch, n), 0) == row
    pick_y = lax.broadcasted_iota(jnp.int32, (across, n), 0) == y
    return pick_row.astype(F32).astype(BF16), pick_y.astype(F32)


def region_start(depth_here, rows_here):
    first_z = lax.axis_index("slab") * depth_here - SWEEPS
    return first_z, lax.axis_index("energy") * rows_here - SWEEPS


def pack_kernel(factor_p, value_p, out):
    _, _, distance = place()
    width = value_p.shape[0]
    packed = width + width // 2

    @pl.when(distance < lax.axis_size("slab") // 2 - 1)
    def _():
        pack_full(factor_p[...], out)
        out[packed : packed + width, :] = value_p[...]


def ready_kernel(couple, even, odd, factor_p, value_p, inverse_p, matrix_q, source_q, matrix,
                 source, link, base, base_source, near, far, inner, reach, hold):
    slab, _, _ = place()
    half = lax.axis_size("slab") // 2

    @pl.when(slab == half - 1)
    def _():
        behind = couple[0]
        behind_t = behind.T
        across = dot3(inverse_p[...], behind)
        near[...] = across
        far[...] = factor_p[...]
        inner[...] = value_p[...]
        matrix[...] = dot3(behind_t, across)
        source[...] = dot3(behind_t, value_p[...])
        link[...] = -dot3(behind_t, factor_p[...])
        base[...] = matrix_q[...]
        base_source[...] = source_q[...]

    @pl.when(slab == half)
    def _():
        behind = couple[0]
        behind_t = behind.T
        ahead = following((even, odd))
        ahead_t = ahead.T
        back = dot3(inverse_p[...], behind)
        reach[...] = back
        side = dot3(couple[1], back)
        side_t = side.T

        def run(invert):
            solved, size = invert(matrix_q[...], hold, 1 / 12, 4)
            found = dot3(solved, source_q[...])
            across = dot3(solved, ahead_t)
            aside = dot3(solved, side)
            near[...] = across
            far[...] = -aside
            inner[...] = found
            matrix[...] = dot3(ahead, across)
            source[...] = dot3(ahead, found)
            link[...] = -dot3(ahead, aside)
            base[...] = dot3(behind_t, back) + dot3(side_t, aside)
            base_source[...] = dot3(behind_t, value_p[...]) - dot3(side_t, found)
            return size

        guarded(run)


def rows_kernel(potential, even_out, odd_out):
    halo = even_out.shape[1]
    low, high = potential[:, :halo], potential[:, potential.shape[1] - halo :]
    odd = lax.axis_index("energy") % 2 == 1
    even_out[...] = jnp.where(odd, low, high)
    odd_out[...] = jnp.where(odd, high, low)


def deposit_kernel(rows_all, pitch, depth, rows_here, dopants, dopant):
    first_z, first_x = region_start(depth, rows_here)
    rows, ys = spots(dopants[...], rows_all, depth + 2 * SWEEPS, pitch, dopant.shape[1], first_z,
                     first_x)
    dopant[...] = dopant_charge * one_pass(rows, ys.astype(BF16), NT)


def halo_kernel(potential, got_even, got_odd, wide):
    depth, rows_here, across = potential.shape
    even_e = lax.axis_index("energy") % 2 == 0
    below = jnp.where(even_e, got_odd[...], got_even[...])
    above = jnp.where(even_e, got_even[...], got_odd[...])
    spare = wide.shape[1] - rows_here - 2 * SWEEPS
    parts = [below, potential[...], above]
    if spare > 0:
        parts.append(jnp.zeros((depth, spare, across), F32))
    wide[...] = jnp.concatenate(parts, axis=1)


def put_planes(out, start, wide, high):
    pitch = wide.shape[1]
    last = wide.shape[0] - SWEEPS
    for k in range(SWEEPS):
        plane = jnp.where(high, wide[last + k], wide[k])
        out[start + k * pitch : start + (k + 1) * pitch, :] = plane


def middle_slab():
    slab, left, _ = place()
    half = lax.axis_size("slab") // 2
    return jnp.logical_or(slab == half - 1, slab == half), left


def centre_kernel(message, matrix, link, base, solved, factor, total, out, hold):
    here, left = middle_slab()

    @pl.when(here)
    def _():
        block = unpack_symmetric(message[...]) - matrix[...]
        near = link[...]
        near_t = near.T
        sign = jnp.where(left, -1.0, 1.0)

        def run(invert):
            found, size = invert(block, hold, 1 / 12, 4)
            reach = dot3(found, near)
            both = base[...] + sign * dot3(near_t, reach)
            pack_symmetric(both, out)
            solved[...] = found
            factor[...] = reach
            total[...] = both
            return size

        guarded(run)


def source_kernel(message, source, link, base_source, solved, value, total):
    here, _ = middle_slab()

    @pl.when(here)
    def _():
        found = dot3(solved[...], message[...] - source[...])
        value[...] = found
        total[...] = base_source[...] - dot3(link[...].T, found)


def expand_kernel(second, factor, value, factor_p, value_p, near, far, inner, reach, slope,
                  offset):
    here, left = middle_slab()
    width = value.shape[0]
    packed = width + width // 2

    def put(block, m, v):
        at = pl.ds(pl.multiple_of(block * width, width), width)
        slope[at, :] = m
        offset[at, :] = v

    @pl.when(here)
    def _():
        m1 = jnp.where(left, -1.0, 1.0) * factor[...]
        v1 = value[...]
        put(jnp.where(left, 3, 2), m1, v1)
        m2 = -(dot3(near[...], m1) + far[...])
        v2 = inner[...] - dot3(near[...], v1)
        put(jnp.where(left, 0, 1), m2, v2)

        @pl.when(left)
        def _():
            put(1, eye(width), jnp.zeros_like(v1))

        @pl.when(jnp.logical_not(left))
        def _():
            put(0, -(dot3(factor_p[...], m2) + reach[...]), value_p[...] - dot3(factor_p[...], v2))

        outer = unpack_full(second[0:packed, :], width)
        put(jnp.where(left, 2, 3), -dot3(outer, m1),
            second[packed : packed + width, :] - dot3(outer, v1))


def join_kernel(message, total, inverse, hold):
    here, left = middle_slab()

    @pl.when(here)
    def _():
        sign = jnp.where(left, -1.0, 1.0)
        matrix = sign * (unpack_symmetric(message[...]) - total[...])

        def run(invert):
            found, size = invert(matrix, hold, 1 / 48, 5)
            inverse[...] = found
            return size

        guarded(run)


def join_solution(message, inverse, total, left):
    sign = jnp.where(left, -1.0, 1.0)
    return dot3(inverse[...], sign * (message[...] - total[...]))


def values_kernel(message, inverse, total, slope, offset, values):
    here, left = middle_slab()

    @pl.when(here)
    def _():
        middle = join_solution(message, inverse, total, left)
        values[...] = offset[...] + dot3(slope[...], middle)


def density_kernel(values, probes, probes_near, dens):
    here, _ = middle_slab()

    @pl.when(here)
    def _():
        n = probes.shape[0]
        terms = jnp.concatenate(
            [probes[...] * values[0:n, :], probes_near[...] * values[n:, :]], axis=0
        )
        dens[...] = dot6(jnp.ones((8, terms.shape[1]), F32), terms, NT)[0:1]


def middle_kernel(message, inverse, total, factor, value, out_first, out_middle):
    here, left = middle_slab()

    @pl.when(here)
    def _():
        middle = join_solution(message, inverse, total, left)
        sign = jnp.where(left, -1.0, 1.0)
        out_first[...] = value[...] + sign * dot3(factor[...], middle)
        out_middle[...] = middle


def back_kernel(step, couple, even, odd, probes, message, first, middle, known_p, known_q,
                factor_p, value_p, inverse_q, value_q, near, far, inner, reach, out_p, out_q,
                dens):
    _, left, distance = place()
    centre = lax.axis_size("slab") // 2 - 1
    width = couple.shape[1]

    @pl.when(jnp.logical_and(distance < centre, distance != step))
    def _():
        out_p[...] = known_p[...]
        out_q[...] = known_q[...]

    @pl.when(jnp.logical_and(distance == step, step == centre - 1))
    def _():
        xq = message[...]
        out_q[...] = xq
        out_p[...] = value_p[...] - dot3(factor_p[...], xq)

    @pl.when(jnp.logical_and(distance == step, step < centre - 1))
    def _():
        link = jnp.where(left, following((even, odd)).T, couple[0])
        xq = value_q[...] - dot3(inverse_q[...], dot3(link, message[...]))
        out_q[...] = xq
        out_p[...] = value_p[...] - dot3(factor_p[...], xq)

    @pl.when(distance == centre)
    def _():
        xi = inner[...] - dot3(near[...], first[...]) - dot3(far[...], middle[...])
        out_p[...] = xi
        out_q[...] = middle[...]

        @pl.when(jnp.logical_not(left))
        def _():
            out_q[...] = value_p[...] - dot3(factor_p[...], xi) - dot3(reach[...], middle[...])

    xp = out_p[...]
    xq = out_q[...]
    xa = jnp.where(left, xp, xq)
    xb = jnp.where(left, xq, xp)
    terms = jnp.concatenate([probes[0:width, :] * xa, probes[width:, :] * xb], axis=0)
    dens[...] = dot6(jnp.ones((8, terms.shape[1]), F32), terms, NT)[0:1]


def total_kernel(scale, cells, wide, *rest):
    parts, outs = rest[:-2], rest[-2:]
    total = parts[0][...]
    for part in parts[1:]:
        total = total + part[...]
    total = total * scale
    place_of = cells[...].astype(F32)
    lanes = wide.shape[2]
    values = total.shape[1] // lanes
    even = lax.axis_index("slab") % 2 == 0
    for out, high in zip(outs, (even, jnp.logical_not(even))):
        for k in range(values):
            out[k : k + 1, :] = total[:, k * lanes : (k + 1) * lanes]
        for k in range(cells.shape[1] // lanes):
            out[values + k : values + k + 1, :] = place_of[:, k * lanes : (k + 1) * lanes]
        put_planes(out, packet_planes(values, cells.shape[1] // lanes), wide, high)


def packet_planes(values, cells):
    return -(-(values + cells) // 8) * 8


def packet_row(packet, first, count):
    return jnp.concatenate([packet[first + k : first + k + 1, :] for k in range(count)], axis=1)


def poisson_kernel(rows_all, planes, paired, packet, near, far, dopant_grid, wide, out, density):
    slab, slabs = lax.axis_index("slab"), lax.axis_size("slab")
    depth, pitch, across = wide.shape
    depth = depth + 2 * SWEEPS
    first_z, first_x = region_start(out.shape[0], out.shape[1])
    n = density.shape[0]
    even = slab % 2 == 0
    alone = jnp.logical_or(slab == 0, slab == slabs - 1)
    count = n // across
    values = 2 * count if paired else count
    own, beside, beyond = [packet_row(p, 0, count) for p in (packet, near, far)]
    if paired:
        own = jnp.where(alone, packet_row(near, count, count), own)
        beside = jnp.where(alone, beside, packet_row(packet, count, count))
    density[...] = own.reshape(n)
    weights = jnp.concatenate([own, beside, jnp.where(alone, 0.0, beyond)], axis=1)
    orbitals = jnp.concatenate([packet_row(p, values, count) for p in (packet, near, far)], axis=1)
    orbitals = jnp.where(jnp.abs(orbitals) < 2.0**30, orbitals, -1.0).astype(jnp.int32)
    rows, ys = spots(orbitals, rows_all, depth, pitch, across, first_z, first_x)
    spread = ys * weights
    h = spread.astype(BF16)
    rest = spread - h.astype(F32)
    m = rest.astype(BF16)
    low = (rest - m.astype(F32)).astype(BF16)
    electron = one_pass(rows, h, NT) + (one_pass(rows, m, NT) + one_pass(rows, low, NT))
    electron = electron.reshape(depth, pitch, across)
    dopant = dopant_grid[...].reshape(depth, pitch, across)
    near_planes = near[packet_planes(values, count) :, :].reshape(SWEEPS, pitch, across)
    far_planes = far[packet_planes(values, count) :, :].reshape(SWEEPS, pitch, across)
    start = jnp.concatenate(
        [jnp.where(even, far_planes, near_planes), wide[...],
         jnp.where(even, near_planes, far_planes)],
        axis=0,
    )
    zs = lax.broadcasted_iota(jnp.int32, start.shape, 0) + first_z
    xs = lax.broadcasted_iota(jnp.int32, start.shape, 1) + first_x
    ys = lax.broadcasted_iota(jnp.int32, start.shape, 2)
    exists = (zs >= 0) & (zs < planes) & (xs >= 0) & (xs < rows_all)
    potential = jnp.where(exists, start, 0.0)
    start = potential
    strength = coupling_beta * jnp.abs(electron)
    for _ in range(SWEEPS):
        blank = jnp.zeros((1, pitch, across), F32)
        beside = jnp.concatenate([potential[1:], blank], axis=0)
        beside = beside + jnp.concatenate([blank, potential[:-1]], axis=0)
        beside = beside + pltpu.roll(potential, 1, 1) + pltpu.roll(potential, pitch - 1, 1)
        beside = beside + jnp.where(ys > 0, pltpu.roll(potential, 1, 2), 0.0)
        beside = beside + jnp.where(ys < across - 1, pltpu.roll(potential, across - 1, 2), 0.0)
        growth = jnp.exp(potential - start)
        residual = beside - 6.0 * potential + coupling_beta * (dopant - electron * growth)
        potential = potential + residual / (6.0 + strength * growth)
        potential = jnp.where(exists, potential, 0.0)
    halo = SWEEPS
    out[...] = potential[halo : halo + out.shape[0], halo : halo + out.shape[1], :]


VM = pl.BlockSpec(memory_space=pltpu.VMEM)
FAR = pl.BlockSpec(memory_space=pltpu.HBM)
GRANT = 16 << 20


def like(*shape, dtype=F32):
    return jax.ShapeDtypeStruct(shape, dtype)


def call(kernel, outs, args, scratch=(), distant=0, flops=10**8):
    args = list(args)
    for k in range(distant):
        args[k] = pltpu.with_memory_space_constraint(args[k], pltpu.HBM)
    own = [pltpu.VMEM(shape, F32) for shape in scratch]
    if distant:
        own += [pltpu.SemaphoreType.DMA((distant + 1,))]
    return pl.pallas_call(
        kernel,
        out_shape=outs,
        in_specs=[FAR] * distant + [VM] * (len(args) - distant),
        out_specs=jax.tree.map(lambda _: VM, outs),
        scratch_shapes=own,
        compiler_params=pltpu.CompilerParams(vmem_limit_bytes=GRANT),
        cost_estimate=pl.CostEstimate(flops=flops, bytes_accessed=10**6, transcendentals=0),
    )(*args)


def pairs_of(count, odd):
    found = []
    for first in range(1 if odd else 0, count - 1, 2):
        found += [(first, first + 1), (first + 1, first)]
    return found


def slab_exchange(value, odd):
    slabs, energies = lax.axis_size("slab"), lax.axis_size("energy")
    pairs = pairs_of(slabs, odd)
    busy = {a for a, _ in pairs}
    whole = [(a * energies + e, b * energies + e) for a, b in pairs for e in range(energies)]
    for a in range(slabs):
        if a not in busy:
            whole += [(a * energies + e, a * energies + (e ^ 1)) for e in range(energies)]
    return lax.ppermute(value, ("slab", "energy"), whole)


def energy_exchange(value, odd):
    energies = lax.axis_size("energy")
    pairs = pairs_of(energies, odd)
    if odd:
        pairs += [(energies - 1, 0), (0, energies - 1)]
    return lax.ppermute(value, "energy", pairs)


def program(energy_index, diag_blocks, couple, probes, orbital_cell, dopant_cells, initial_potential):
    width = diag_blocks.shape[1]
    probe_count = probes.shape[1]
    slabs = lax.axis_size("slab")
    energies = lax.axis_size("energy")
    half = slabs // 2
    square, column = like(width, width), like(width, probe_count)
    letter = like(width, probe_count)
    sq = (width, width)

    even = slab_exchange(couple, False)
    paired = half == 2
    odd = even
    if not paired:
        odd = lax.ppermute(couple, "slab", [(s + 1, s) for s in range(1, slabs - 1, 2)])

    message = None
    for t in range(half - 1):
        args = [diag_blocks, couple, probes, energy_index.reshape(1, 1)]
        if t > 0:
            if t > 1:
                _, _, distance = place()
                message = jnp.where(distance == t, message, kept[0])
                sources = jnp.where(distance == t, sources, kept[1])
            kept = message, sources
            args += [message, sources, even, odd]
        outs = (square, column, square, square, column, letter)
        if not paired:
            outs += (square, column, letter)
        state = call(
            functools.partial(stage_kernel, t, not paired), outs,
            args, (sq, diag_blocks.shape, couple.shape, probes.shape), 3,
        )
        if t == 0:
            prepared = state
        last = t == half - 2
        message = slab_exchange(state[5] if last else state[8], t % 2 == 1)
        if not last:
            sources = slab_exchange(state[7], t % 2 == 1)
    factor_p, value_p = state[:2]
    matrix, source, link, base, base_source, near_map, far_map, inner, reach = call(
        ready_kernel,
        (square, column, square, square, column, square, square, column, square),
        [couple, even, odd, *prepared[:5]], (sq,),
    )
    reduced, first_factor, reach = lax.optimization_barrier((state[4], prepared[0], reach))
    sources = slab_exchange(reduced, half % 2 == 1)

    depth, rows_here, across = initial_potential.shape
    halo = SWEEPS
    rows_all = rows_here * energies
    pitch = -(-(rows_here + 2 * halo) // 8) * 8
    strip = halo * pitch
    even_rows, odd_rows = call(rows_kernel, (like(depth, halo, across),) * 2, [initial_potential])
    got_even = energy_exchange(even_rows, False)
    got_odd = energy_exchange(odd_rows, True)
    cells = (depth + 2 * halo) * pitch
    second = call(
        pack_kernel, like(width + width // 2 + width, probe_count),
        [first_factor, prepared[1]],
    )
    if paired:
        probes_near = slab_exchange(probes, False)
        second = slab_exchange(second, False)
    dopant_grid = call(
        functools.partial(deposit_kernel, rows_all, pitch, depth, rows_here),
        like(cells, across), [dopant_cells.reshape(1, -1)],
    )
    solved, factor, total, sent = call(
        centre_kernel, (square, square, square, letter),
        [message, matrix, link, base], (sq,),
    )
    across_middle = slab_exchange(sent, half % 2 == 0)
    value, total_source = call(
        source_kernel, (column, column),
        [sources, source, link, base_source, solved],
    )
    sources_middle = slab_exchange(total_source, half % 2 == 0)
    wide = call(
        halo_kernel, like(depth, pitch, across),
        [initial_potential, *lax.optimization_barrier((got_even, got_odd, sent))[:2]],
    )
    inverse = call(join_kernel, square, [across_middle, total], (sq,))
    if paired:
        slope, offset = call(
            expand_kernel, (like(4 * width, width), like(4 * width, probe_count)),
            [second, factor, value, *prepared[:2], near_map, far_map, inner, reach],
        )
        values = call(
            values_kernel, like(4 * width, probe_count),
            [sources_middle, inverse, total_source, slope, offset],
        )
        dens = call(density_kernel, like(1, 4 * width), [values, probes, probes_near])
    else:
        first, middle = call(
            middle_kernel, (column, column),
            [sources_middle, inverse, total_source, factor, value],
        )
        centred = (lax.axis_index("slab") == half) | (lax.axis_index("slab") == half - 1)
        factor_p = jnp.where(centred, prepared[0], factor_p)
        value_p = jnp.where(centred, prepared[1], value_p)
        known_p, known_q = first, middle
        for t in range(half - 2, -1, -1):
            known_p, known_q, dens = call(
                functools.partial(back_kernel, t),
                (column, column, like(1, 2 * width)),
                [couple, even, odd, probes, slab_exchange(first if t == half - 2 else known_p, t % 2 == 1),
                 first, middle,
                 known_p, known_q, factor_p, value_p, state[6], state[7], near_map, far_map, inner,
                 reach],
            )
    parts = [dens] + [
        lax.ppermute(dens, "energy", [(e, e ^ k) for e in range(energies)])
        for k in range(1, energies)
    ]
    spare = packet_planes(dens.shape[1] // across, orbital_cell.shape[0] // across)
    packet, packet_far = call(
        functools.partial(total_kernel, 1.0 / (probe_count * energies)),
        (like(spare + strip, across),) * 2, [orbital_cell.reshape(1, -1), wide, *parts],
    )
    near = slab_exchange(packet, False)
    far = slab_exchange(packet_far, True)

    def poisson(*refs):
        poisson_kernel(rows_all, depth * slabs, paired, *refs)

    potential, density = call(
        poisson, (like(depth, rows_here, across), like(2 * width)),
        [packet, near, far, dopant_grid, wide],
    )
    return (potential, density)


def solution(mesh):
    placed = (
        P("energy"),
        P(("cfg", "slab"), None, None),
        P(("cfg", "slab"), None, None),
        P("slab", None),
        P("slab"),
        P("cfg"),
        P(("cfg", "slab"), "energy", None),
    )
    return jax.shard_map(
        program,
        mesh=mesh,
        in_specs=placed,
        out_specs=(P(("cfg", "slab"), "energy", None), P(("cfg", "slab"))),
        check_vma=False,
    )
```

```python
import functools

import jax
import jax.numpy as jnp
from jax import lax
from jax.experimental import pallas as pl
from jax.experimental.pallas import tpu as pltpu
from jax.sharding import PartitionSpec as P


SWEEPS = 2

sigma_base = 0.02
sigma_step = 0.01
coupling_beta = 0.5
dopant_charge = 4.0

F32 = jnp.float32
BF16 = jnp.bfloat16
NT = (((1,), (1,)), ((), ()))
NN = (((1,), (0,)), ((), ()))


def split2(a):
    high = a.astype(BF16)
    return high, (a - high.astype(F32)).astype(BF16)


def one_pass(a, b, dims=NN):
    return lax.dot_general(a, b, dims, preferred_element_type=F32)


def dot3(a, b):
    ah, al = split2(a)
    bh, bl = split2(b)
    return one_pass(ah, bh) + (one_pass(ah, bl) + one_pass(al, bh))


def dot6(a, b, dims=NN):
    return lax.dot_general(
        a, b, dims, precision=lax.Precision.HIGHEST, preferred_element_type=F32
    )


def eye(n):
    return (
        lax.broadcasted_iota(jnp.int32, (n, n), 0) == lax.broadcasted_iota(jnp.int32, (n, n), 1)
    ).astype(F32)


def estimate(matrix, ratio, doublings):
    unit = eye(matrix.shape[0])
    square = dot3(matrix, matrix)
    sums = jnp.sum(jnp.abs(square), axis=0, keepdims=True)
    bound = jnp.sqrt(jnp.max(sums, axis=1, keepdims=True))
    first = 2.0 / (bound * (1.0 + ratio))
    tau = (1.0 + ratio) / (1.0 - ratio)
    for k in range(doublings):
        after = 2.0 * tau * tau - 1.0
        scale = (after + 1.0) / after
        if k == 0:
            grown = (2.0 * first) * unit - (first * first) * matrix
            squared = unit - (2.0 * first) * matrix + (first * first) * square
        else:
            grown = guess + dot3(guess, error)
            squared = dot3(error, error) if k + 1 < doublings else None
        guess = scale * grown
        if k + 1 < doublings:
            error = scale * squared - (scale - 1.0) * unit
        tau = after
    residual = unit - dot6(matrix, guess)
    step = one_pass(guess.astype(BF16), residual.astype(BF16))
    return guess + step, jnp.sum(residual * residual), first


def fast(matrix, hold, ratio, doublings):
    found, size, _ = estimate(matrix, ratio, doublings)
    return found, size


def careful(matrix, hold, ratio, doublings):
    unit = eye(matrix.shape[0])
    found, size, first = estimate(matrix, ratio, doublings)
    hold[...] = found

    @pl.when(jnp.logical_not(size < 0.9))
    def _():
        hold[...] = first * unit

    def go_on(state):
        count, last = state
        return jnp.logical_and(count < 64, jnp.logical_not(last < 1e-6))

    def newton(state):
        count, _ = state
        now = hold[...]
        left = unit - dot6(matrix, now)
        hold[...] = now + dot6(now, left)
        return count + 1, jnp.sum(left * left)

    lax.while_loop(go_on, newton, (jnp.int32(0), size))
    return hold[...], size


def guarded(run):
    worst = run(fast)

    @pl.when(jnp.logical_not(worst < 4e-5))
    def _():
        run(careful)


def pack_symmetric(matrix, out):
    half = matrix.shape[0] // 3
    out[0:half, :] = matrix[half : 2 * half, 0 : 2 * half]
    out[half : 2 * half, :] = matrix[2 * half :, 0 : 2 * half]
    out[2 * half : 3 * half, :] = jnp.concatenate(
        [matrix[0:half, 0:half], matrix[2 * half :, 2 * half :]], axis=1
    )


def unpack_symmetric(packed):
    third = packed.shape[0] // 3
    row1 = packed[0:third]
    row2 = packed[third : 2 * third]
    ends = packed[2 * third :]
    b10, b11 = row1[:, :third], row1[:, third:]
    b20, b21 = row2[:, :third], row2[:, third:]
    b00, b22 = ends[:, :third], ends[:, third:]
    return jnp.concatenate(
        [
            jnp.concatenate([b00, b10.T, b20.T], axis=1),
            jnp.concatenate([b10, b11, b21.T], axis=1),
            jnp.concatenate([b20, b21, b22], axis=1),
        ],
        axis=0,
    )


def place():
    slab, slabs = lax.axis_index("slab"), lax.axis_size("slab")
    left = slab < slabs // 2
    return slab, left, jnp.where(left, slab, slabs - 1 - slab)


def following(ahead):
    even, odd = ahead
    return jnp.where(lax.axis_index("slab") % 2 == 0, even[...], odd[...])


def take_block(message, couple, ahead, left):
    link_t = jnp.where(left, couple[0].T, following(ahead))
    link = jnp.where(left, couple[0], following(ahead).T)
    return dot3(link, dot3(unpack_symmetric(message[...]), link_t))


def take_column(message, couple, ahead, left):
    return dot3(jnp.where(left, couple[0], following(ahead).T), message[...])


def stage_kernel(step, inner_too, diag_far, couple_far, probes_far, energy, *rest):
    if step > 0:
        message, sources, even, odd, rest = rest[0], rest[1], rest[2], rest[3], rest[4:]
    factor_p, value_p, inverse_p, matrix_q, source_q, out = rest[:6]
    rest = rest[6:]
    if inner_too:
        inverse_q, value_q, out_inverse = rest[:3]
        rest = rest[3:]
    hold, diag, couple, probes, sems = rest
    _, left, distance = place()
    forward = lax.axis_index("slab") <= lax.axis_size("slab") // 2
    first = jnp.where(forward, 0, 1)
    width = diag.shape[1]
    loads = [
        pltpu.make_async_copy(diag_far.at[first], diag.at[0], sems.at[0]),
        pltpu.make_async_copy(couple_far, couple, sems.at[1]),
        pltpu.make_async_copy(probes_far, probes, sems.at[2]),
        pltpu.make_async_copy(diag_far.at[1 - first], diag.at[1], sems.at[3]),
    ]
    for load in loads:
        load.start()
    loads[0].wait()
    if step > 0:
        loads[1].wait()
    shift = sigma_base + sigma_step * energy[...].astype(F32)
    shifted = shift * eye(width)
    sp = diag[0] + shifted
    if step > 0:
        taken = jnp.logical_and(distance >= 1, distance <= step)
        ahead = (even, odd)
        sp = sp - jnp.where(taken, take_block(message, couple, ahead, left), 0.0)
        extra = jnp.where(taken, take_column(sources, couple, ahead, left), 0.0)

    def await_loads():
        for load in loads[2 if step > 0 else 1 :]:
            load.wait()

    def outer_block(invert):
        xp, size = invert(sp, hold, 1 / 12, 4)
        if invert is fast:
            await_loads()
        rp = probes[pl.ds(pl.multiple_of(first * width, width), width), :]
        rq = probes[pl.ds(pl.multiple_of((1 - first) * width, width), width), :]
        if step > 0:
            rp = rp - extra
        inner = couple[1]
        inner_t = inner.T
        apq = jnp.where(forward, inner_t, inner)
        aqp = jnp.where(forward, inner, inner_t)
        fp = dot3(xp, apq)
        yp = dot3(xp, rp)
        factor_p[...] = fp
        value_p[...] = yp
        sq = diag[1] + shifted - dot3(aqp, fp)
        return xp, yp, sq, rq - dot3(aqp, yp), size

    def run(invert):
        xp, _, sq, reduced, size = outer_block(invert)
        inverse_p[...] = xp
        matrix_q[...] = sq
        source_q[...] = reduced
        pack_symmetric(sq, out)
        if inner_too:
            xq, size_q = invert(sq, hold, 1 / 12, 4)
            inverse_q[...] = xq
            value_q[...] = dot3(xq, reduced)
            pack_symmetric(xq, out_inverse)
            size = jnp.maximum(size, size_q)
        return size

    guarded(run)


def pack_full(matrix, out):
    n = matrix.shape[0]
    lanes = out.shape[1]
    out[0:n, :] = matrix[:, 0:lanes]
    out[n : n + n // 2, :] = jnp.concatenate(
        [matrix[0 : n // 2, lanes:], matrix[n // 2 :, lanes:]], axis=1
    )


def unpack_full(packed, n):
    rest = packed[n : n + n // 2]
    lanes = packed.shape[1]
    tail = jnp.concatenate([rest[:, : n - lanes], rest[:, n - lanes :]], axis=0)
    return jnp.concatenate([packed[0:n], tail], axis=1)


def spots(index, rows_all, depth, pitch, across, first_z, first_x):
    plane = rows_all * across
    z = index // plane - first_z
    x = index // across % rows_all - first_x
    y = index % across
    inside = (z >= 0) & (z < depth) & (x >= 0) & (x < pitch)
    row = jnp.where(inside, z * pitch + x, -1)
    n = index.shape[1]
    pick_row = lax.broadcasted_iota(jnp.int32, (depth * pitch, n), 0) == row
    pick_y = lax.broadcasted_iota(jnp.int32, (across, n), 0) == y
    return pick_row.astype(F32).astype(BF16), pick_y.astype(F32)


def region_start(depth_here, rows_here):
    first_z = lax.axis_index("slab") * depth_here - SWEEPS
    return first_z, lax.axis_index("energy") * rows_here - SWEEPS


def pack_kernel(factor_p, value_p, out):
    _, _, distance = place()
    width = value_p.shape[0]
    packed = width + width // 2

    @pl.when(distance < lax.axis_size("slab") // 2 - 1)
    def _():
        pack_full(factor_p[...], out)
        out[packed : packed + width, :] = value_p[...]


def ready_kernel(couple, even, odd, factor_p, value_p, inverse_p, matrix_q, source_q, matrix,
                 source, link, base, base_source, near, far, inner, reach, hold):
    slab, _, _ = place()
    half = lax.axis_size("slab") // 2

    @pl.when(slab == half - 1)
    def _():
        behind = couple[0]
        behind_t = behind.T
        across = dot3(inverse_p[...], behind)
        near[...] = across
        far[...] = factor_p[...]
        inner[...] = value_p[...]
        matrix[...] = dot3(behind_t, across)
        source[...] = dot3(behind_t, value_p[...])
        link[...] = -dot3(behind_t, factor_p[...])
        base[...] = matrix_q[...]
        base_source[...] = source_q[...]

    @pl.when(slab == half)
    def _():
        behind = couple[0]
        behind_t = behind.T
        ahead = following((even, odd))
        ahead_t = ahead.T
        back = dot3(inverse_p[...], behind)
        reach[...] = back
        side = dot3(couple[1], back)
        side_t = side.T

        def run(invert):
            solved, size = invert(matrix_q[...], hold, 1 / 12, 4)
            found = dot3(solved, source_q[...])
            across = dot3(solved, ahead_t)
            aside = dot3(solved, side)
            near[...] = across
            far[...] = -aside
            inner[...] = found
            matrix[...] = dot3(ahead, across)
            source[...] = dot3(ahead, found)
            link[...] = -dot3(ahead, aside)
            base[...] = dot3(behind_t, back) + dot3(side_t, aside)
            base_source[...] = dot3(behind_t, value_p[...]) - dot3(side_t, found)
            return size

        guarded(run)


def rows_kernel(potential, even_out, odd_out):
    halo = even_out.shape[1]
    low, high = potential[:, :halo], potential[:, potential.shape[1] - halo :]
    odd = lax.axis_index("energy") % 2 == 1
    even_out[...] = jnp.where(odd, low, high)
    odd_out[...] = jnp.where(odd, high, low)


def deposit_kernel(rows_all, pitch, depth, rows_here, dopants, dopant):
    first_z, first_x = region_start(depth, rows_here)
    rows, ys = spots(dopants[...], rows_all, depth + 2 * SWEEPS, pitch, dopant.shape[1], first_z,
                     first_x)
    dopant[...] = dopant_charge * one_pass(rows, ys.astype(BF16), NT)


def halo_kernel(potential, got_even, got_odd, wide):
    depth, rows_here, across = potential.shape
    even_e = lax.axis_index("energy") % 2 == 0
    below = jnp.where(even_e, got_odd[...], got_even[...])
    above = jnp.where(even_e, got_even[...], got_odd[...])
    spare = wide.shape[1] - rows_here - 2 * SWEEPS
    parts = [below, potential[...], above]
    if spare > 0:
        parts.append(jnp.zeros((depth, spare, across), F32))
    wide[...] = jnp.concatenate(parts, axis=1)


def put_planes(out, start, wide, high):
    pitch = wide.shape[1]
    last = wide.shape[0] - SWEEPS
    for k in range(SWEEPS):
        plane = jnp.where(high, wide[last + k], wide[k])
        out[start + k * pitch : start + (k + 1) * pitch, :] = plane


def middle_slab():
    slab, left, _ = place()
    half = lax.axis_size("slab") // 2
    return jnp.logical_or(slab == half - 1, slab == half), left


def centre_kernel(message, matrix, link, base, solved, factor, total, out, hold):
    here, left = middle_slab()

    @pl.when(here)
    def _():
        block = unpack_symmetric(message[...]) - matrix[...]
        near = link[...]
        near_t = near.T
        sign = jnp.where(left, -1.0, 1.0)

        def run(invert):
            found, size = invert(block, hold, 1 / 12, 4)
            reach = dot3(found, near)
            both = base[...] + sign * dot3(near_t, reach)
            pack_symmetric(both, out)
            solved[...] = found
            factor[...] = reach
            total[...] = both
            return size

        guarded(run)


def source_kernel(message, source, link, base_source, solved, value, total):
    here, _ = middle_slab()

    @pl.when(here)
    def _():
        found = dot3(solved[...], message[...] - source[...])
        value[...] = found
        total[...] = base_source[...] - dot3(link[...].T, found)


def expand_kernel(second, factor, value, factor_p, value_p, near, far, inner, reach, slope,
                  offset):
    here, left = middle_slab()
    width = value.shape[0]
    packed = width + width // 2

    def put(block, m, v):
        at = pl.ds(pl.multiple_of(block * width, width), width)
        slope[at, :] = m
        offset[at, :] = v

    @pl.when(here)
    def _():
        m1 = jnp.where(left, -1.0, 1.0) * factor[...]
        v1 = value[...]
        put(jnp.where(left, 3, 2), m1, v1)
        m2 = -(dot3(near[...], m1) + far[...])
        v2 = inner[...] - dot3(near[...], v1)
        put(jnp.where(left, 0, 1), m2, v2)

        @pl.when(left)
        def _():
            put(1, eye(width), jnp.zeros_like(v1))

        @pl.when(jnp.logical_not(left))
        def _():
            put(0, -(dot3(factor_p[...], m2) + reach[...]), value_p[...] - dot3(factor_p[...], v2))

        outer = unpack_full(second[0:packed, :], width)
        put(jnp.where(left, 2, 3), -dot3(outer, m1),
            second[packed : packed + width, :] - dot3(outer, v1))


def join_kernel(message, total, inverse, hold):
    here, left = middle_slab()

    @pl.when(here)
    def _():
        sign = jnp.where(left, -1.0, 1.0)
        matrix = sign * (unpack_symmetric(message[...]) - total[...])

        def run(invert):
            found, size = invert(matrix, hold, 1 / 48, 5)
            inverse[...] = found
            return size

        guarded(run)


def join_solution(message, inverse, total, left):
    sign = jnp.where(left, -1.0, 1.0)
    return dot3(inverse[...], sign * (message[...] - total[...]))


def values_kernel(message, inverse, total, slope, offset, values):
    here, left = middle_slab()

    @pl.when(here)
    def _():
        middle = join_solution(message, inverse, total, left)
        values[...] = offset[...] + dot3(slope[...], middle)


def density_kernel(values, probes, probes_near, dens):
    here, _ = middle_slab()

    @pl.when(here)
    def _():
        n = probes.shape[0]
        terms = jnp.concatenate(
            [probes[...] * values[0:n, :], probes_near[...] * values[n:, :]], axis=0
        )
        dens[...] = dot6(jnp.ones((8, terms.shape[1]), F32), terms, NT)[0:1]


def middle_kernel(message, inverse, total, factor, value, out_first, out_middle):
    here, left = middle_slab()

    @pl.when(here)
    def _():
        middle = join_solution(message, inverse, total, left)
        sign = jnp.where(left, -1.0, 1.0)
        out_first[...] = value[...] + sign * dot3(factor[...], middle)
        out_middle[...] = middle


def back_kernel(step, couple, even, odd, probes, message, first, middle, known_p, known_q,
                factor_p, value_p, inverse_q, value_q, near, far, inner, reach, out_p, out_q,
                dens):
    _, left, distance = place()
    centre = lax.axis_size("slab") // 2 - 1
    width = couple.shape[1]

    @pl.when(jnp.logical_and(distance < centre, distance != step))
    def _():
        out_p[...] = known_p[...]
        out_q[...] = known_q[...]

    @pl.when(jnp.logical_and(distance == step, step == centre - 1))
    def _():
        xq = message[...]
        out_q[...] = xq
        out_p[...] = value_p[...] - dot3(factor_p[...], xq)

    @pl.when(jnp.logical_and(distance == step, step < centre - 1))
    def _():
        link = jnp.where(left, following((even, odd)).T, couple[0])
        xq = value_q[...] - dot3(inverse_q[...], dot3(link, message[...]))
        out_q[...] = xq
        out_p[...] = value_p[...] - dot3(factor_p[...], xq)

    @pl.when(distance == centre)
    def _():
        xi = inner[...] - dot3(near[...], first[...]) - dot3(far[...], middle[...])
        out_p[...] = xi
        out_q[...] = middle[...]

        @pl.when(jnp.logical_not(left))
        def _():
            out_q[...] = value_p[...] - dot3(factor_p[...], xi) - dot3(reach[...], middle[...])

    xp = out_p[...]
    xq = out_q[...]
    xa = jnp.where(left, xp, xq)
    xb = jnp.where(left, xq, xp)
    terms = jnp.concatenate([probes[0:width, :] * xa, probes[width:, :] * xb], axis=0)
    dens[...] = dot6(jnp.ones((8, terms.shape[1]), F32), terms, NT)[0:1]


def total_kernel(scale, cells, wide, *rest):
    parts, outs = rest[:-2], rest[-2:]
    total = parts[0][...]
    for part in parts[1:]:
        total = total + part[...]
    total = total * scale
    place_of = cells[...].astype(F32)
    lanes = wide.shape[2]
    values = total.shape[1] // lanes
    even = lax.axis_index("slab") % 2 == 0
    for out, high in zip(outs, (even, jnp.logical_not(even))):
        for k in range(values):
            out[k : k + 1, :] = total[:, k * lanes : (k + 1) * lanes]
        for k in range(cells.shape[1] // lanes):
            out[values + k : values + k + 1, :] = place_of[:, k * lanes : (k + 1) * lanes]
        put_planes(out, packet_planes(values, cells.shape[1] // lanes), wide, high)


def packet_planes(values, cells):
    return -(-(values + cells) // 8) * 8


def packet_row(packet, first, count):
    return jnp.concatenate([packet[first + k : first + k + 1, :] for k in range(count)], axis=1)


def poisson_kernel(rows_all, planes, paired, packet, near, far, dopant_grid, wide, out, density):
    slab, slabs = lax.axis_index("slab"), lax.axis_size("slab")
    depth, pitch, across = wide.shape
    depth = depth + 2 * SWEEPS
    first_z, first_x = region_start(out.shape[0], out.shape[1])
    n = density.shape[0]
    even = slab % 2 == 0
    alone = jnp.logical_or(slab == 0, slab == slabs - 1)
    count = n // across
    values = 2 * count if paired else count
    own, beside, beyond = [packet_row(p, 0, count) for p in (packet, near, far)]
    if paired:
        own = jnp.where(alone, packet_row(near, count, count), own)
        beside = jnp.where(alone, beside, packet_row(packet, count, count))
    density[...] = own.reshape(n)
    weights = jnp.concatenate([own, beside, jnp.where(alone, 0.0, beyond)], axis=1)
    orbitals = jnp.concatenate([packet_row(p, values, count) for p in (packet, near, far)], axis=1)
    orbitals = jnp.where(jnp.abs(orbitals) < 2.0**30, orbitals, -1.0).astype(jnp.int32)
    rows, ys = spots(orbitals, rows_all, depth, pitch, across, first_z, first_x)
    spread = ys * weights
    h = spread.astype(BF16)
    rest = spread - h.astype(F32)
    m = rest.astype(BF16)
    low = (rest - m.astype(F32)).astype(BF16)
    electron = one_pass(rows, h, NT) + (one_pass(rows, m, NT) + one_pass(rows, low, NT))
    electron = electron.reshape(depth, pitch, across)
    dopant = dopant_grid[...].reshape(depth, pitch, across)
    near_planes = near[packet_planes(values, count) :, :].reshape(SWEEPS, pitch, across)
    far_planes = far[packet_planes(values, count) :, :].reshape(SWEEPS, pitch, across)
    start = jnp.concatenate(
        [jnp.where(even, far_planes, near_planes), wide[...],
         jnp.where(even, near_planes, far_planes)],
        axis=0,
    )
    zs = lax.broadcasted_iota(jnp.int32, start.shape, 0) + first_z
    xs = lax.broadcasted_iota(jnp.int32, start.shape, 1) + first_x
    ys = lax.broadcasted_iota(jnp.int32, start.shape, 2)
    exists = (zs >= 0) & (zs < planes) & (xs >= 0) & (xs < rows_all)
    potential = jnp.where(exists, start, 0.0)
    start = potential
    strength = coupling_beta * jnp.abs(electron)
    for _ in range(SWEEPS):
        blank = jnp.zeros((1, pitch, across), F32)
        beside = jnp.concatenate([potential[1:], blank], axis=0)
        beside = beside + jnp.concatenate([blank, potential[:-1]], axis=0)
        beside = beside + pltpu.roll(potential, 1, 1) + pltpu.roll(potential, pitch - 1, 1)
        beside = beside + jnp.where(ys > 0, pltpu.roll(potential, 1, 2), 0.0)
        beside = beside + jnp.where(ys < across - 1, pltpu.roll(potential, across - 1, 2), 0.0)
        growth = jnp.exp(potential - start)
        residual = beside - 6.0 * potential + coupling_beta * (dopant - electron * growth)
        potential = potential + residual / (6.0 + strength * growth)
        potential = jnp.where(exists, potential, 0.0)
    halo = SWEEPS
    out[...] = potential[halo : halo + out.shape[0], halo : halo + out.shape[1], :]


VM = pl.BlockSpec(memory_space=pltpu.VMEM)
FAR = pl.BlockSpec(memory_space=pltpu.HBM)
GRANT = 16 << 20


def like(*shape, dtype=F32):
    return jax.ShapeDtypeStruct(shape, dtype)


def call(kernel, outs, args, scratch=(), distant=0, flops=10**8):
    args = list(args)
    for k in range(distant):
        args[k] = pltpu.with_memory_space_constraint(args[k], pltpu.HBM)
    own = [pltpu.VMEM(shape, F32) for shape in scratch]
    if distant:
        own += [pltpu.SemaphoreType.DMA((distant + 1,))]
    return pl.pallas_call(
        kernel,
        out_shape=outs,
        in_specs=[FAR] * distant + [VM] * (len(args) - distant),
        out_specs=jax.tree.map(lambda _: VM, outs),
        scratch_shapes=own,
        compiler_params=pltpu.CompilerParams(vmem_limit_bytes=GRANT),
        cost_estimate=pl.CostEstimate(flops=flops, bytes_accessed=10**6, transcendentals=0),
    )(*args)


def pairs_of(count, odd):
    found = []
    for first in range(1 if odd else 0, count - 1, 2):
        found += [(first, first + 1), (first + 1, first)]
    return found


def slab_exchange(value, odd):
    slabs, energies = lax.axis_size("slab"), lax.axis_size("energy")
    pairs = pairs_of(slabs, odd)
    busy = {a for a, _ in pairs}
    whole = [(a * energies + e, b * energies + e) for a, b in pairs for e in range(energies)]
    for a in range(slabs):
        if a not in busy:
            whole += [(a * energies + e, a * energies + (e ^ 1)) for e in range(energies)]
    return lax.ppermute(value, ("slab", "energy"), whole)


def energy_exchange(value, odd):
    energies = lax.axis_size("energy")
    pairs = pairs_of(energies, odd)
    if odd:
        pairs += [(energies - 1, 0), (0, energies - 1)]
    return lax.ppermute(value, "energy", pairs)


def program(energy_index, diag_blocks, couple, probes, orbital_cell, dopant_cells, initial_potential):
    width = diag_blocks.shape[1]
    probe_count = probes.shape[1]
    slabs = lax.axis_size("slab")
    energies = lax.axis_size("energy")
    half = slabs // 2
    square, column = like(width, width), like(width, probe_count)
    letter = like(width, probe_count)
    sq = (width, width)

    even = slab_exchange(couple[0], False)
    paired = half == 2
    odd = even
    if not paired:
        odd = lax.ppermute(couple[0], "slab", [(s + 1, s) for s in range(1, slabs - 1, 2)])

    message = None
    for t in range(half - 1):
        args = [diag_blocks, couple, probes, energy_index.reshape(1, 1)]
        if t > 0:
            if t > 1:
                _, _, distance = place()
                message = jnp.where(distance == t, message, kept[0])
                sources = jnp.where(distance == t, sources, kept[1])
            kept = message, sources
            args += [message, sources, even, odd]
        outs = (square, column, square, square, column, letter)
        if not paired:
            outs += (square, column, letter)
        state = call(
            functools.partial(stage_kernel, t, not paired), outs,
            args, (sq, diag_blocks.shape, couple.shape, probes.shape), 3,
        )
        if t == 0:
            prepared = state
        last = t == half - 2
        message = slab_exchange(state[5] if last else state[8], t % 2 == 1)
        if not last:
            sources = slab_exchange(state[7], t % 2 == 1)
    factor_p, value_p = state[:2]
    matrix, source, link, base, base_source, near_map, far_map, inner, reach = call(
        ready_kernel,
        (square, column, square, square, column, square, square, column, square),
        [couple, even, odd, *prepared[:5]], (sq,),
    )
    reduced, first_factor, reach = lax.optimization_barrier((state[4], prepared[0], reach))
    sources = slab_exchange(reduced, half % 2 == 1)

    depth, rows_here, across = initial_potential.shape
    halo = SWEEPS
    rows_all = rows_here * energies
    pitch = -(-(rows_here + 2 * halo) // 8) * 8
    strip = halo * pitch
    even_rows, odd_rows = call(rows_kernel, (like(depth, halo, across),) * 2, [initial_potential])
    got_even = energy_exchange(even_rows, False)
    got_odd = energy_exchange(odd_rows, True)
    cells = (depth + 2 * halo) * pitch
    second = call(
        pack_kernel, like(width + width // 2 + width, probe_count),
        [first_factor, prepared[1]],
    )
    if paired:
        probes_near = slab_exchange(probes, False)
        second = slab_exchange(second, False)
    dopant_grid = call(
        functools.partial(deposit_kernel, rows_all, pitch, depth, rows_here),
        like(cells, across), [dopant_cells.reshape(1, -1)],
    )
    solved, factor, total, sent = call(
        centre_kernel, (square, square, square, letter),
        [message, matrix, link, base], (sq,),
    )
    across_middle = slab_exchange(sent, half % 2 == 0)
    value, total_source = call(
        source_kernel, (column, column),
        [sources, source, link, base_source, solved],
    )
    sources_middle = slab_exchange(total_source, half % 2 == 0)
    wide = call(
        halo_kernel, like(depth, pitch, across),
        [initial_potential, *lax.optimization_barrier((got_even, got_odd, sent))[:2]],
    )
    inverse = call(join_kernel, square, [across_middle, total], (sq,))
    if paired:
        slope, offset = call(
            expand_kernel, (like(4 * width, width), like(4 * width, probe_count)),
            [second, factor, value, *prepared[:2], near_map, far_map, inner, reach],
        )
        values = call(
            values_kernel, like(4 * width, probe_count),
            [sources_middle, inverse, total_source, slope, offset],
        )
        dens = call(density_kernel, like(1, 4 * width), [values, probes, probes_near])
    else:
        first, middle = call(
            middle_kernel, (column, column),
            [sources_middle, inverse, total_source, factor, value],
        )
        centred = (lax.axis_index("slab") == half) | (lax.axis_index("slab") == half - 1)
        factor_p = jnp.where(centred, prepared[0], factor_p)
        value_p = jnp.where(centred, prepared[1], value_p)
        known_p, known_q = first, middle
        for t in range(half - 2, -1, -1):
            known_p, known_q, dens = call(
                functools.partial(back_kernel, t),
                (column, column, like(1, 2 * width)),
                [couple, even, odd, probes, slab_exchange(first if t == half - 2 else known_p, t % 2 == 1),
                 first, middle,
                 known_p, known_q, factor_p, value_p, state[6], state[7], near_map, far_map, inner,
                 reach],
            )
    parts = [dens] + [
        lax.ppermute(dens, "energy", [(e, e ^ k) for e in range(energies)])
        for k in range(1, energies)
    ]
    spare = packet_planes(dens.shape[1] // across, orbital_cell.shape[0] // across)
    packet, packet_far = call(
        functools.partial(total_kernel, 1.0 / (probe_count * energies)),
        (like(spare + strip, across),) * 2, [orbital_cell.reshape(1, -1), wide, *parts],
    )
    near = slab_exchange(packet, False)
    far = slab_exchange(packet_far, True)

    def poisson(*refs):
        poisson_kernel(rows_all, depth * slabs, paired, *refs)

    potential, density = call(
        poisson, (like(depth, rows_here, across), like(2 * width)),
        [packet, near, far, dopant_grid, wide],
    )
    return (potential, density)


def solution(mesh):
    placed = (
        P("energy"),
        P(("cfg", "slab"), None, None),
        P(("cfg", "slab"), None, None),
        P("slab", None),
        P("slab"),
        P("cfg"),
        P(("cfg", "slab"), "energy", None),
    )
    return jax.shard_map(
        program,
        mesh=mesh,
        in_specs=placed,
        out_specs=(P(("cfg", "slab"), "energy", None), P(("cfg", "slab"))),
        check_vma=False,
    )
```

```python
import functools

import jax
import jax.numpy as jnp
from jax import lax
from jax.experimental import pallas as pl
from jax.experimental.pallas import tpu as pltpu
from jax.sharding import PartitionSpec as P


SWEEPS = 2

sigma_base = 0.02
sigma_step = 0.01
coupling_beta = 0.5
dopant_charge = 4.0

F32 = jnp.float32
BF16 = jnp.bfloat16
NT = (((1,), (1,)), ((), ()))
NN = (((1,), (0,)), ((), ()))


def split2(a):
    high = a.astype(BF16)
    return high, (a - high.astype(F32)).astype(BF16)


def one_pass(a, b, dims=NN):
    return lax.dot_general(a, b, dims, preferred_element_type=F32)


def dot3(a, b):
    ah, al = split2(a)
    bh, bl = split2(b)
    return one_pass(ah, bh) + (one_pass(ah, bl) + one_pass(al, bh))


def dot6(a, b, dims=NN):
    return lax.dot_general(
        a, b, dims, precision=lax.Precision.HIGHEST, preferred_element_type=F32
    )


def eye(n):
    return (
        lax.broadcasted_iota(jnp.int32, (n, n), 0) == lax.broadcasted_iota(jnp.int32, (n, n), 1)
    ).astype(F32)


def estimate(matrix, ratio, doublings):
    unit = eye(matrix.shape[0])
    square = dot3(matrix, matrix)
    sums = jnp.sum(jnp.abs(square), axis=0, keepdims=True)
    bound = jnp.sqrt(jnp.max(sums, axis=1, keepdims=True))
    first = 2.0 / (bound * (1.0 + ratio))
    tau = (1.0 + ratio) / (1.0 - ratio)
    for k in range(doublings):
        after = 2.0 * tau * tau - 1.0
        scale = (after + 1.0) / after
        if k == 0:
            grown = (2.0 * first) * unit - (first * first) * matrix
            squared = unit - (2.0 * first) * matrix + (first * first) * square
        else:
            grown = guess + dot3(guess, error)
            squared = dot3(error, error) if k + 1 < doublings else None
        guess = scale * grown
        if k + 1 < doublings:
            error = scale * squared - (scale - 1.0) * unit
        tau = after
    residual = unit - dot6(matrix, guess)
    step = one_pass(guess.astype(BF16), residual.astype(BF16))
    return guess + step, jnp.sum(residual * residual), first


def fast(matrix, hold, ratio, doublings):
    found, size, _ = estimate(matrix, ratio, doublings)
    return found, size


def careful(matrix, hold, ratio, doublings):
    unit = eye(matrix.shape[0])
    found, size, first = estimate(matrix, ratio, doublings)
    hold[...] = found

    @pl.when(jnp.logical_not(size < 0.9))
    def _():
        hold[...] = first * unit

    def go_on(state):
        count, last = state
        return jnp.logical_and(count < 64, jnp.logical_not(last < 1e-6))

    def newton(state):
        count, _ = state
        now = hold[...]
        left = unit - dot6(matrix, now)
        hold[...] = now + dot6(now, left)
        return count + 1, jnp.sum(left * left)

    lax.while_loop(go_on, newton, (jnp.int32(0), size))
    return hold[...], size


def guarded(run):
    worst = run(fast)

    @pl.when(jnp.logical_not(worst < 4e-5))
    def _():
        run(careful)


def pack_symmetric(matrix, out):
    half = matrix.shape[0] // 3
    out[0:half, :] = matrix[half : 2 * half, 0 : 2 * half]
    out[half : 2 * half, :] = matrix[2 * half :, 0 : 2 * half]
    out[2 * half : 3 * half, :] = jnp.concatenate(
        [matrix[0:half, 0:half], matrix[2 * half :, 2 * half :]], axis=1
    )


def unpack_symmetric(packed):
    third = packed.shape[0] // 3
    row1 = packed[0:third]
    row2 = packed[third : 2 * third]
    ends = packed[2 * third :]
    b10, b11 = row1[:, :third], row1[:, third:]
    b20, b21 = row2[:, :third], row2[:, third:]
    b00, b22 = ends[:, :third], ends[:, third:]
    return jnp.concatenate(
        [
            jnp.concatenate([b00, b10.T, b20.T], axis=1),
            jnp.concatenate([b10, b11, b21.T], axis=1),
            jnp.concatenate([b20, b21, b22], axis=1),
        ],
        axis=0,
    )


def place():
    slab, slabs = lax.axis_index("slab"), lax.axis_size("slab")
    left = slab < slabs // 2
    return slab, left, jnp.where(left, slab, slabs - 1 - slab)


def following(ahead):
    even, odd = ahead
    return jnp.where(lax.axis_index("slab") % 2 == 0, even[...], odd[...])


def take_block(message, couple, ahead, left):
    link_t = jnp.where(left, couple[0].T, following(ahead))
    link = jnp.where(left, couple[0], following(ahead).T)
    return dot3(link, dot3(unpack_symmetric(message[...]), link_t))


def take_column(message, couple, ahead, left):
    return dot3(jnp.where(left, couple[0], following(ahead).T), message[...])


def stage_kernel(step, inner_too, diag_far, couple_far, probes_far, energy, *rest):
    if step > 0:
        message, sources, even, odd, rest = rest[0], rest[1], rest[2], rest[3], rest[4:]
    factor_p, value_p, inverse_p, matrix_q, source_q, out = rest[:6]
    rest = rest[6:]
    if inner_too:
        inverse_q, value_q, out_inverse = rest[:3]
        rest = rest[3:]
    hold, diag, couple, probes, sems = rest
    _, left, distance = place()
    forward = lax.axis_index("slab") <= lax.axis_size("slab") // 2
    first = jnp.where(forward, 0, 1)
    width = diag.shape[1]
    loads = [
        pltpu.make_async_copy(diag_far.at[first], diag.at[0], sems.at[0]),
        pltpu.make_async_copy(couple_far, couple, sems.at[1]),
        pltpu.make_async_copy(probes_far, probes, sems.at[2]),
        pltpu.make_async_copy(diag_far.at[1 - first], diag.at[1], sems.at[3]),
    ]
    for load in loads:
        load.start()
    loads[0].wait()
    if step > 0:
        loads[1].wait()
    shift = sigma_base + sigma_step * energy[...].astype(F32)
    shifted = shift * eye(width)
    sp = diag[0] + shifted
    if step > 0:
        taken = jnp.logical_and(distance >= 1, distance <= step)
        ahead = (even, odd)
        sp = sp - jnp.where(taken, take_block(message, couple, ahead, left), 0.0)
        extra = jnp.where(taken, take_column(sources, couple, ahead, left), 0.0)

    def await_loads():
        for load in loads[2 if step > 0 else 1 :]:
            load.wait()

    def outer_block(invert):
        xp, size = invert(sp, hold, 1 / 12, 4)
        if invert is fast:
            await_loads()
        rp = probes[pl.ds(pl.multiple_of(first * width, width), width), :]
        rq = probes[pl.ds(pl.multiple_of((1 - first) * width, width), width), :]
        if step > 0:
            rp = rp - extra
        inner = couple[1]
        inner_t = inner.T
        apq = jnp.where(forward, inner_t, inner)
        aqp = jnp.where(forward, inner, inner_t)
        fp = dot3(xp, apq)
        yp = dot3(xp, rp)
        factor_p[...] = fp
        value_p[...] = yp
        sq = diag[1] + shifted - dot3(aqp, fp)
        return xp, yp, sq, rq - dot3(aqp, yp), size

    def run(invert):
        xp, _, sq, reduced, size = outer_block(invert)
        inverse_p[...] = xp
        matrix_q[...] = sq
        source_q[...] = reduced
        pack_symmetric(sq, out)
        if inner_too:
            xq, size_q = invert(sq, hold, 1 / 12, 4)
            inverse_q[...] = xq
            value_q[...] = dot3(xq, reduced)
            pack_symmetric(xq, out_inverse)
            size = jnp.maximum(size, size_q)
        return size

    guarded(run)


def pack_full(matrix, out):
    n = matrix.shape[0]
    lanes = out.shape[1]
    out[0:n, :] = matrix[:, 0:lanes]
    out[n : n + n // 2, :] = jnp.concatenate(
        [matrix[0 : n // 2, lanes:], matrix[n // 2 :, lanes:]], axis=1
    )


def unpack_full(packed, n):
    rest = packed[n : n + n // 2]
    lanes = packed.shape[1]
    tail = jnp.concatenate([rest[:, : n - lanes], rest[:, n - lanes :]], axis=0)
    return jnp.concatenate([packed[0:n], tail], axis=1)


def spots(index, rows_all, depth, pitch, across, first_z, first_x):
    plane = rows_all * across
    z = index // plane - first_z
    x = index // across % rows_all - first_x
    y = index % across
    inside = (z >= 0) & (z < depth) & (x >= 0) & (x < pitch)
    row = jnp.where(inside, z * pitch + x, -1)
    n = index.shape[1]
    pick_row = lax.broadcasted_iota(jnp.int32, (depth * pitch, n), 0) == row
    pick_y = lax.broadcasted_iota(jnp.int32, (across, n), 0) == y
    return pick_row.astype(F32).astype(BF16), pick_y.astype(F32)


def region_start(depth_here, rows_here):
    first_z = lax.axis_index("slab") * depth_here - SWEEPS
    return first_z, lax.axis_index("energy") * rows_here - SWEEPS


def pack_kernel(factor_p, value_p, probes, out):
    _, _, distance = place()
    width = value_p.shape[0]
    packed = width + width // 2

    @pl.when(distance < lax.axis_size("slab") // 2 - 1)
    def _():
        pack_full(factor_p[...], out)
        out[packed : packed + width, :] = value_p[...]
        out[packed + width :, :] = probes[...]


def ready_kernel(couple, even, odd, factor_p, value_p, inverse_p, matrix_q, source_q, matrix,
                 source, link, base, base_source, near, far, inner, reach, hold):
    slab, _, _ = place()
    half = lax.axis_size("slab") // 2

    @pl.when(slab == half - 1)
    def _():
        behind = couple[0]
        behind_t = behind.T
        across = dot3(inverse_p[...], behind)
        near[...] = across
        far[...] = factor_p[...]
        inner[...] = value_p[...]
        matrix[...] = dot3(behind_t, across)
        source[...] = dot3(behind_t, value_p[...])
        link[...] = -dot3(behind_t, factor_p[...])
        base[...] = matrix_q[...]
        base_source[...] = source_q[...]

    @pl.when(slab == half)
    def _():
        behind = couple[0]
        behind_t = behind.T
        ahead = following((even, odd))
        ahead_t = ahead.T
        back = dot3(inverse_p[...], behind)
        reach[...] = back
        side = dot3(couple[1], back)
        side_t = side.T

        def run(invert):
            solved, size = invert(matrix_q[...], hold, 1 / 12, 4)
            found = dot3(solved, source_q[...])
            across = dot3(solved, ahead_t)
            aside = dot3(solved, side)
            near[...] = across
            far[...] = -aside
            inner[...] = found
            matrix[...] = dot3(ahead, across)
            source[...] = dot3(ahead, found)
            link[...] = -dot3(ahead, aside)
            base[...] = dot3(behind_t, back) + dot3(side_t, aside)
            base_source[...] = dot3(behind_t, value_p[...]) - dot3(side_t, found)
            return size

        guarded(run)


ROWS_AT = 8


def put_message(out, total, potential, high):
    depth, rows_here, lanes = potential.shape
    for k in range(total.shape[1] // lanes):
        out[k : k + 1, :] = total[:, k * lanes : (k + 1) * lanes]
    for k in range(depth):
        at = ROWS_AT + k * SWEEPS
        low, top = potential[k, 0:SWEEPS, :], potential[k, rows_here - SWEEPS :, :]
        out[at : at + SWEEPS, :] = jnp.where(high, top, low)


def put_messages(total, potential, even_out, odd_out):
    odd = lax.axis_index("energy") % 2 == 1
    put_message(even_out, total, potential, jnp.logical_not(odd))
    put_message(odd_out, total, potential, odd)


def message_kernel(dens, potential, even_out, odd_out):
    put_messages(dens[...], potential, even_out, odd_out)


def deposit_kernel(rows_all, pitch, depth, rows_here, dopants, dopant):
    first_z, first_x = region_start(depth, rows_here)
    rows, ys = spots(dopants[...], rows_all, depth + 2 * SWEEPS, pitch, dopant.shape[1], first_z,
                     first_x)
    dopant[...] = dopant_charge * one_pass(rows, ys.astype(BF16), NT)


def put_wide(potential, got_even, got_odd, wide):
    depth, rows_here, across = potential.shape
    even = lax.axis_index("energy") % 2 == 0
    spare = wide.shape[1] - rows_here - 2 * SWEEPS
    for k in range(depth):
        at = ROWS_AT + k * SWEEPS
        one, two = got_even[at : at + SWEEPS, :], got_odd[at : at + SWEEPS, :]
        parts = [jnp.where(even, two, one), potential[k], jnp.where(even, one, two)]
        if spare > 0:
            parts.append(jnp.zeros((spare, across), F32))
        wide[k] = jnp.concatenate(parts, axis=0)


def put_planes(out, start, wide, high):
    pitch = wide.shape[1]
    last = wide.shape[0] - SWEEPS
    for k in range(SWEEPS):
        plane = jnp.where(high, wide[last + k], wide[k])
        out[start + k * pitch : start + (k + 1) * pitch, :] = plane


def middle_slab():
    slab, left, _ = place()
    half = lax.axis_size("slab") // 2
    return jnp.logical_or(slab == half - 1, slab == half), left


def centre_kernel(message, matrix, link, base, solved, factor, total, out, hold):
    here, left = middle_slab()

    @pl.when(here)
    def _():
        block = unpack_symmetric(message[...]) - matrix[...]
        near = link[...]
        near_t = near.T
        sign = jnp.where(left, -1.0, 1.0)

        def run(invert):
            found, size = invert(block, hold, 1 / 12, 4)
            reach = dot3(found, near)
            both = base[...] + sign * dot3(near_t, reach)
            pack_symmetric(both, out)
            solved[...] = found
            factor[...] = reach
            total[...] = both
            return size

        guarded(run)


def source_kernel(message, source, link, base_source, solved, value, total):
    here, _ = middle_slab()

    @pl.when(here)
    def _():
        found = dot3(solved[...], message[...] - source[...])
        value[...] = found
        total[...] = base_source[...] - dot3(link[...].T, found)


def expand_kernel(second, factor, value, factor_p, value_p, near, far, inner, reach, slope,
                  offset):
    here, left = middle_slab()
    width = value.shape[0]
    packed = width + width // 2

    def put(block, m, v):
        at = pl.ds(pl.multiple_of(block * width, width), width)
        slope[at, :] = m
        offset[at, :] = v

    @pl.when(here)
    def _():
        m1 = jnp.where(left, -1.0, 1.0) * factor[...]
        v1 = value[...]
        put(jnp.where(left, 3, 2), m1, v1)
        m2 = -(dot3(near[...], m1) + far[...])
        v2 = inner[...] - dot3(near[...], v1)
        put(jnp.where(left, 0, 1), m2, v2)

        @pl.when(left)
        def _():
            put(1, eye(width), jnp.zeros_like(v1))

        @pl.when(jnp.logical_not(left))
        def _():
            put(0, -(dot3(factor_p[...], m2) + reach[...]), value_p[...] - dot3(factor_p[...], v2))

        outer = unpack_full(second[0:packed, :], width)
        put(jnp.where(left, 2, 3), -dot3(outer, m1),
            second[packed : packed + width, :] - dot3(outer, v1))


def join_kernel(message, total, inverse, hold):
    here, left = middle_slab()

    @pl.when(here)
    def _():
        sign = jnp.where(left, -1.0, 1.0)
        matrix = sign * (unpack_symmetric(message[...]) - total[...])

        def run(invert):
            found, size = invert(matrix, hold, 1 / 48, 5)
            inverse[...] = found
            return size

        guarded(run)


def join_solution(message, inverse, total, left):
    sign = jnp.where(left, -1.0, 1.0)
    return dot3(inverse[...], sign * (message[...] - total[...]))


def values_kernel(message, inverse, total, slope, offset, values):
    here, left = middle_slab()

    @pl.when(here)
    def _():
        middle = join_solution(message, inverse, total, left)
        values[...] = offset[...] + dot3(slope[...], middle)


def density_kernel(values, probes, second, potential, even_out, odd_out, dens):
    here, _ = middle_slab()

    @pl.when(here)
    def _():
        n = probes.shape[0]
        outer = second[second.shape[0] - n :, :]
        terms = jnp.concatenate([probes[...] * values[0:n, :], outer * values[n:, :]], axis=0)
        dens[...] = dot6(jnp.ones((8, terms.shape[1]), F32), terms, NT)

    put_messages(dens[0:1, :], potential, even_out, odd_out)


def middle_kernel(message, inverse, total, factor, value, out_first, out_middle):
    here, left = middle_slab()

    @pl.when(here)
    def _():
        middle = join_solution(message, inverse, total, left)
        sign = jnp.where(left, -1.0, 1.0)
        out_first[...] = value[...] + sign * dot3(factor[...], middle)
        out_middle[...] = middle


def back_kernel(step, couple, even, odd, probes, message, first, middle, known_p, known_q,
                factor_p, value_p, inverse_q, value_q, near, far, inner, reach, out_p, out_q,
                dens):
    _, left, distance = place()
    centre = lax.axis_size("slab") // 2 - 1
    width = couple.shape[1]

    @pl.when(jnp.logical_and(distance < centre, distance != step))
    def _():
        out_p[...] = known_p[...]
        out_q[...] = known_q[...]

    @pl.when(jnp.logical_and(distance == step, step == centre - 1))
    def _():
        xq = message[...]
        out_q[...] = xq
        out_p[...] = value_p[...] - dot3(factor_p[...], xq)

    @pl.when(jnp.logical_and(distance == step, step < centre - 1))
    def _():
        link = jnp.where(left, following((even, odd)).T, couple[0])
        xq = value_q[...] - dot3(inverse_q[...], dot3(link, message[...]))
        out_q[...] = xq
        out_p[...] = value_p[...] - dot3(factor_p[...], xq)

    @pl.when(distance == centre)
    def _():
        xi = inner[...] - dot3(near[...], first[...]) - dot3(far[...], middle[...])
        out_p[...] = xi
        out_q[...] = middle[...]

        @pl.when(jnp.logical_not(left))
        def _():
            out_q[...] = value_p[...] - dot3(factor_p[...], xi) - dot3(reach[...], middle[...])

    xp = out_p[...]
    xq = out_q[...]
    xa = jnp.where(left, xp, xq)
    xb = jnp.where(left, xq, xp)
    terms = jnp.concatenate([probes[0:width, :] * xa, probes[width:, :] * xb], axis=0)
    dens[...] = dot6(jnp.ones((8, terms.shape[1]), F32), terms, NT)[0:1]


def total_kernel(scale, values, cells, potential, got_odd, *rest):
    parts, wide, outs = rest[:-3], rest[-3], rest[-2:]
    total = parts[0][0:values, :]
    for part in parts[1:]:
        total = total + part[0:values, :]
    total = total * scale
    place_of = cells[...].astype(F32)
    lanes = wide.shape[2]
    put_wide(potential, parts[1], got_odd, wide)
    even = lax.axis_index("slab") % 2 == 0
    for out, high in zip(outs, (even, jnp.logical_not(even))):
        out[0:values, :] = total
        for k in range(cells.shape[1] // lanes):
            out[values + k : values + k + 1, :] = place_of[:, k * lanes : (k + 1) * lanes]
        put_planes(out, packet_planes(values, cells.shape[1] // lanes), wide, high)


def packet_planes(values, cells):
    return -(-(values + cells) // 8) * 8


def packet_row(packet, first, count):
    return jnp.concatenate([packet[first + k : first + k + 1, :] for k in range(count)], axis=1)


def poisson_kernel(rows_all, planes, paired, packet, near, far, dopant_grid, wide, out, density):
    slab, slabs = lax.axis_index("slab"), lax.axis_size("slab")
    depth, pitch, across = wide.shape
    depth = depth + 2 * SWEEPS
    first_z, first_x = region_start(out.shape[0], out.shape[1])
    n = density.shape[0]
    even = slab % 2 == 0
    alone = jnp.logical_or(slab == 0, slab == slabs - 1)
    count = n // across
    values = 2 * count if paired else count
    own, beside, beyond = [packet_row(p, 0, count) for p in (packet, near, far)]
    if paired:
        own = jnp.where(alone, packet_row(near, count, count), own)
        beside = jnp.where(alone, beside, packet_row(packet, count, count))
    density[...] = own.reshape(n)
    weights = jnp.concatenate([own, beside, jnp.where(alone, 0.0, beyond)], axis=1)
    orbitals = jnp.concatenate([packet_row(p, values, count) for p in (packet, near, far)], axis=1)
    orbitals = jnp.where(jnp.abs(orbitals) < 2.0**30, orbitals, -1.0).astype(jnp.int32)
    rows, ys = spots(orbitals, rows_all, depth, pitch, across, first_z, first_x)
    spread = ys * weights
    h = spread.astype(BF16)
    rest = spread - h.astype(F32)
    m = rest.astype(BF16)
    low = (rest - m.astype(F32)).astype(BF16)
    electron = one_pass(rows, h, NT) + (one_pass(rows, m, NT) + one_pass(rows, low, NT))
    electron = electron.reshape(depth, pitch, across)
    dopant = dopant_grid[...].reshape(depth, pitch, across)
    near_planes = near[packet_planes(values, count) :, :].reshape(SWEEPS, pitch, across)
    far_planes = far[packet_planes(values, count) :, :].reshape(SWEEPS, pitch, across)
    start = jnp.concatenate(
        [jnp.where(even, far_planes, near_planes), wide[...],
         jnp.where(even, near_planes, far_planes)],
        axis=0,
    )
    zs = lax.broadcasted_iota(jnp.int32, start.shape, 0) + first_z
    xs = lax.broadcasted_iota(jnp.int32, start.shape, 1) + first_x
    ys = lax.broadcasted_iota(jnp.int32, start.shape, 2)
    exists = (zs >= 0) & (zs < planes) & (xs >= 0) & (xs < rows_all)
    potential = jnp.where(exists, start, 0.0)
    start = potential
    strength = coupling_beta * jnp.abs(electron)
    for _ in range(SWEEPS):
        blank = jnp.zeros((1, pitch, across), F32)
        beside = jnp.concatenate([potential[1:], blank], axis=0)
        beside = beside + jnp.concatenate([blank, potential[:-1]], axis=0)
        beside = beside + pltpu.roll(potential, 1, 1) + pltpu.roll(potential, pitch - 1, 1)
        beside = beside + jnp.where(ys > 0, pltpu.roll(potential, 1, 2), 0.0)
        beside = beside + jnp.where(ys < across - 1, pltpu.roll(potential, across - 1, 2), 0.0)
        growth = jnp.exp(potential - start)
        residual = beside - 6.0 * potential + coupling_beta * (dopant - electron * growth)
        potential = potential + residual / (6.0 + strength * growth)
        potential = jnp.where(exists, potential, 0.0)
    halo = SWEEPS
    out[...] = potential[halo : halo + out.shape[0], halo : halo + out.shape[1], :]


VM = pl.BlockSpec(memory_space=pltpu.VMEM)
FAR = pl.BlockSpec(memory_space=pltpu.HBM)
GRANT = 16 << 20


def like(*shape, dtype=F32):
    return jax.ShapeDtypeStruct(shape, dtype)


def call(kernel, outs, args, scratch=(), distant=0, flops=10**8):
    args = list(args)
    for k in range(distant):
        args[k] = pltpu.with_memory_space_constraint(args[k], pltpu.HBM)
    own = [pltpu.VMEM(shape, F32) for shape in scratch]
    if distant:
        own += [pltpu.SemaphoreType.DMA((distant + 1,))]
    return pl.pallas_call(
        kernel,
        out_shape=outs,
        in_specs=[FAR] * distant + [VM] * (len(args) - distant),
        out_specs=jax.tree.map(lambda _: VM, outs),
        scratch_shapes=own,
        compiler_params=pltpu.CompilerParams(vmem_limit_bytes=GRANT),
        cost_estimate=pl.CostEstimate(flops=flops, bytes_accessed=10**6, transcendentals=0),
    )(*args)


def pairs_of(count, odd):
    found = []
    for first in range(1 if odd else 0, count - 1, 2):
        found += [(first, first + 1), (first + 1, first)]
    return found


def slab_exchange(value, odd):
    slabs, energies = lax.axis_size("slab"), lax.axis_size("energy")
    pairs = pairs_of(slabs, odd)
    busy = {a for a, _ in pairs}
    whole = [(a * energies + e, b * energies + e) for a, b in pairs for e in range(energies)]
    for a in range(slabs):
        if a not in busy:
            whole += [(a * energies + e, a * energies + (e ^ 1)) for e in range(energies)]
    return lax.ppermute(value, ("slab", "energy"), whole)


def energy_exchange(value, odd):
    energies = lax.axis_size("energy")
    pairs = pairs_of(energies, odd)
    if odd:
        pairs += [(energies - 1, 0), (0, energies - 1)]
    return lax.ppermute(value, "energy", pairs)


def program(energy_index, diag_blocks, couple, probes, orbital_cell, dopant_cells, initial_potential):
    width = diag_blocks.shape[1]
    probe_count = probes.shape[1]
    slabs = lax.axis_size("slab")
    energies = lax.axis_size("energy")
    half = slabs // 2
    square, column = like(width, width), like(width, probe_count)
    letter = like(width, probe_count)
    sq = (width, width)

    even = slab_exchange(couple[0], False)
    paired = half == 2
    odd = even
    if not paired:
        odd = lax.ppermute(couple[0], "slab", [(s + 1, s) for s in range(1, slabs - 1, 2)])

    message = None
    for t in range(half - 1):
        args = [diag_blocks, couple, probes, energy_index.reshape(1, 1)]
        if t > 0:
            if t > 1:
                _, _, distance = place()
                message = jnp.where(distance == t, message, kept[0])
                sources = jnp.where(distance == t, sources, kept[1])
            kept = message, sources
            args += [message, sources, even, odd]
        outs = (square, column, square, square, column, letter)
        if not paired:
            outs += (square, column, letter)
        state = call(
            functools.partial(stage_kernel, t, not paired), outs,
            args, (sq, diag_blocks.shape, couple.shape, probes.shape), 3,
        )
        if t == 0:
            prepared = state
        last = t == half - 2
        message = slab_exchange(state[5] if last else state[8], t % 2 == 1)
        if not last:
            sources = slab_exchange(state[7], t % 2 == 1)
    factor_p, value_p = state[:2]
    matrix, source, link, base, base_source, near_map, far_map, inner, reach = call(
        ready_kernel,
        (square, column, square, square, column, square, square, column, square),
        [couple, even, odd, *prepared[:5]], (sq,),
    )
    reduced, first_factor, reach = lax.optimization_barrier((state[4], prepared[0], reach))
    sources = slab_exchange(reduced, half % 2 == 1)

    depth, rows_here, across = initial_potential.shape
    halo = SWEEPS
    rows_all = rows_here * energies
    pitch = -(-(rows_here + 2 * halo) // 8) * 8
    strip = halo * pitch
    cells = (depth + 2 * halo) * pitch
    second = call(
        pack_kernel, like(width + width // 2 + 3 * width, probe_count),
        [first_factor, prepared[1], probes],
    )
    if paired:
        second = slab_exchange(second, False)
    dopant_grid = call(
        functools.partial(deposit_kernel, rows_all, pitch, depth, rows_here),
        like(cells, across), [dopant_cells.reshape(1, -1)],
    )
    solved, factor, total, sent = call(
        centre_kernel, (square, square, square, letter),
        [message, matrix, link, base], (sq,),
    )
    across_middle = slab_exchange(sent, half % 2 == 0)
    value, total_source = call(
        source_kernel, (column, column),
        [sources, source, link, base_source, solved],
    )
    sources_middle = slab_exchange(total_source, half % 2 == 0)
    inverse = call(join_kernel, square, [across_middle, total], (sq,))
    if paired:
        slope, offset = call(
            expand_kernel, (like(4 * width, width), like(4 * width, probe_count)),
            [second, factor, value, *prepared[:2], near_map, far_map, inner, reach],
        )
        values = call(
            values_kernel, like(4 * width, probe_count),
            [sources_middle, inverse, total_source, slope, offset],
        )
        even_message, odd_message = call(
            density_kernel, (like(ROWS_AT + depth * halo, across),) * 2,
            [values, probes, second, initial_potential], ((8, 4 * width),),
        )
    else:
        first, middle = call(
            middle_kernel, (column, column),
            [sources_middle, inverse, total_source, factor, value],
        )
        centred = (lax.axis_index("slab") == half) | (lax.axis_index("slab") == half - 1)
        factor_p = jnp.where(centred, prepared[0], factor_p)
        value_p = jnp.where(centred, prepared[1], value_p)
        known_p, known_q = first, middle
        for t in range(half - 2, -1, -1):
            known_p, known_q, dens = call(
                functools.partial(back_kernel, t),
                (column, column, like(1, 2 * width)),
                [couple, even, odd, probes, slab_exchange(first if t == half - 2 else known_p, t % 2 == 1),
                 first, middle,
                 known_p, known_q, factor_p, value_p, state[6], state[7], near_map, far_map, inner,
                 reach],
            )
    if not paired:
        even_message, odd_message = call(
            message_kernel, (like(ROWS_AT + depth * halo, across),) * 2,
            [dens, initial_potential],
        )
    got_even = energy_exchange(even_message, False)
    got_odd = energy_exchange(odd_message, True)
    parts = [even_message, got_even]
    for k in range(2, energies):
        if energies == 4 and k == 3:
            parts.append(got_odd)
        else:
            partners = [(e, e ^ k) for e in range(energies)]
            parts.append(lax.ppermute(even_message, "energy", partners))
    values_rows = (4 if paired else 2) * width // across
    spare = packet_planes(values_rows, orbital_cell.shape[0] // across)
    wide, packet, packet_far = call(
        functools.partial(total_kernel, 1.0 / (probe_count * energies), values_rows),
        (like(depth, pitch, across),) + (like(spare + strip, across),) * 2,
        [orbital_cell.reshape(1, -1), initial_potential, got_odd, *parts],
    )
    near = slab_exchange(packet, False)
    far = slab_exchange(packet_far, True)

    def poisson(*refs):
        poisson_kernel(rows_all, depth * slabs, paired, *refs)

    potential, density = call(
        poisson, (like(depth, rows_here, across), like(2 * width)),
        [packet, near, far, dopant_grid, wide],
    )
    return (potential, density)


def solution(mesh):
    placed = (
        P("energy"),
        P(("cfg", "slab"), None, None),
        P(("cfg", "slab"), None, None),
        P("slab", None),
        P("slab"),
        P("cfg"),
        P(("cfg", "slab"), "energy", None),
    )
    return jax.shard_map(
        program,
        mesh=mesh,
        in_specs=placed,
        out_specs=(P(("cfg", "slab"), "energy", None), P(("cfg", "slab"))),
        check_vma=False,
    )
```

```python
import functools

import jax
import jax.numpy as jnp
from jax import lax
from jax.experimental import pallas as pl
from jax.experimental.pallas import tpu as pltpu
from jax.sharding import PartitionSpec as P


SWEEPS = 2

sigma_base = 0.02
sigma_step = 0.01
coupling_beta = 0.5
dopant_charge = 4.0

F32 = jnp.float32
BF16 = jnp.bfloat16
NT = (((1,), (1,)), ((), ()))
NN = (((1,), (0,)), ((), ()))


def split2(a):
    high = a.astype(BF16)
    return high, (a - high.astype(F32)).astype(BF16)


def one_pass(a, b, dims=NN):
    return lax.dot_general(a, b, dims, preferred_element_type=F32)


def dot3(a, b):
    ah, al = split2(a)
    bh, bl = split2(b)
    return one_pass(ah, bh) + (one_pass(ah, bl) + one_pass(al, bh))


def dot6(a, b, dims=NN):
    return lax.dot_general(
        a, b, dims, precision=lax.Precision.HIGHEST, preferred_element_type=F32
    )


def eye(n):
    return (
        lax.broadcasted_iota(jnp.int32, (n, n), 0) == lax.broadcasted_iota(jnp.int32, (n, n), 1)
    ).astype(F32)


def estimate(matrix, ratio, doublings):
    unit = eye(matrix.shape[0])
    square = dot3(matrix, matrix)
    sums = jnp.sum(jnp.abs(square), axis=0, keepdims=True)
    bound = jnp.sqrt(jnp.max(sums, axis=1, keepdims=True))
    first = 2.0 / (bound * (1.0 + ratio))
    tau = (1.0 + ratio) / (1.0 - ratio)
    for k in range(doublings):
        after = 2.0 * tau * tau - 1.0
        scale = (after + 1.0) / after
        if k == 0:
            grown = (2.0 * first) * unit - (first * first) * matrix
            squared = unit - (2.0 * first) * matrix + (first * first) * square
        else:
            grown = guess + dot3(guess, error)
            squared = dot3(error, error) if k + 1 < doublings else None
        guess = scale * grown
        if k + 1 < doublings:
            error = scale * squared - (scale - 1.0) * unit
        tau = after
    residual = unit - dot6(matrix, guess)
    step = one_pass(guess.astype(BF16), residual.astype(BF16))
    return guess + step, jnp.sum(residual * residual), first


def fast(matrix, hold, ratio, doublings):
    found, size, _ = estimate(matrix, ratio, doublings)
    return found, size


def careful(matrix, hold, ratio, doublings):
    unit = eye(matrix.shape[0])
    found, size, first = estimate(matrix, ratio, doublings)
    hold[...] = found

    @pl.when(jnp.logical_not(size < 0.9))
    def _():
        hold[...] = first * unit

    def go_on(state):
        count, last = state
        return jnp.logical_and(count < 64, jnp.logical_not(last < 1e-6))

    def newton(state):
        count, _ = state
        now = hold[...]
        left = unit - dot6(matrix, now)
        hold[...] = now + dot6(now, left)
        return count + 1, jnp.sum(left * left)

    lax.while_loop(go_on, newton, (jnp.int32(0), size))
    return hold[...], size


def guarded(run):
    worst = run(fast)

    @pl.when(jnp.logical_not(worst < 1e-4))
    def _():
        run(careful)


def pack_symmetric(matrix, out):
    half = matrix.shape[0] // 3
    out[0:half, :] = matrix[half : 2 * half, 0 : 2 * half]
    out[half : 2 * half, :] = matrix[2 * half :, 0 : 2 * half]
    out[2 * half : 3 * half, :] = jnp.concatenate(
        [matrix[0:half, 0:half], matrix[2 * half :, 2 * half :]], axis=1
    )


def unpack_symmetric(packed):
    third = packed.shape[0] // 3
    row1 = packed[0:third]
    row2 = packed[third : 2 * third]
    ends = packed[2 * third :]
    b10, b11 = row1[:, :third], row1[:, third:]
    b20, b21 = row2[:, :third], row2[:, third:]
    b00, b22 = ends[:, :third], ends[:, third:]
    return jnp.concatenate(
        [
            jnp.concatenate([b00, b10.T, b20.T], axis=1),
            jnp.concatenate([b10, b11, b21.T], axis=1),
            jnp.concatenate([b20, b21, b22], axis=1),
        ],
        axis=0,
    )


def place():
    slab, slabs = lax.axis_index("slab"), lax.axis_size("slab")
    left = slab < slabs // 2
    return slab, left, jnp.where(left, slab, slabs - 1 - slab)


def following(ahead):
    even, odd = ahead
    return jnp.where(lax.axis_index("slab") % 2 == 0, even[...], odd[...])


def take_block(message, couple, ahead, left):
    link_t = jnp.where(left, couple[0].T, following(ahead))
    link = jnp.where(left, couple[0], following(ahead).T)
    return dot3(link, dot3(unpack_symmetric(message[...]), link_t))


def take_column(message, couple, ahead, left):
    return dot3(jnp.where(left, couple[0], following(ahead).T), message[...])


def stage_kernel(step, inner_too, diag_far, couple_far, probes_far, energy, *rest):
    if step > 0:
        message, sources, even, odd, rest = rest[0], rest[1], rest[2], rest[3], rest[4:]
    factor_p, value_p, inverse_p, matrix_q, source_q, out = rest[:6]
    rest = rest[6:]
    if inner_too:
        inverse_q, value_q, out_inverse = rest[:3]
        rest = rest[3:]
    hold, diag, couple, probes, sems = rest
    _, left, distance = place()
    forward = lax.axis_index("slab") <= lax.axis_size("slab") // 2
    first = jnp.where(forward, 0, 1)
    width = diag.shape[1]
    loads = [
        pltpu.make_async_copy(diag_far.at[first], diag.at[0], sems.at[0]),
        pltpu.make_async_copy(couple_far, couple, sems.at[1]),
        pltpu.make_async_copy(probes_far, probes, sems.at[2]),
        pltpu.make_async_copy(diag_far.at[1 - first], diag.at[1], sems.at[3]),
    ]
    for load in loads:
        load.start()
    loads[0].wait()
    if step > 0:
        loads[1].wait()
    shift = sigma_base + sigma_step * energy[...].astype(F32)
    shifted = shift * eye(width)
    sp = diag[0] + shifted
    if step > 0:
        taken = jnp.logical_and(distance >= 1, distance <= step)
        ahead = (even, odd)
        sp = sp - jnp.where(taken, take_block(message, couple, ahead, left), 0.0)
        extra = jnp.where(taken, take_column(sources, couple, ahead, left), 0.0)

    def await_loads():
        for load in loads[2 if step > 0 else 1 :]:
            load.wait()

    def outer_block(invert):
        xp, size = invert(sp, hold, 1 / 16, 4)
        if invert is fast:
            await_loads()
        rp = probes[pl.ds(pl.multiple_of(first * width, width), width), :]
        rq = probes[pl.ds(pl.multiple_of((1 - first) * width, width), width), :]
        if step > 0:
            rp = rp - extra
        inner = couple[1]
        inner_t = inner.T
        apq = jnp.where(forward, inner_t, inner)
        aqp = jnp.where(forward, inner, inner_t)
        fp = dot3(xp, apq)
        yp = dot3(xp, rp)
        factor_p[...] = fp
        value_p[...] = yp
        sq = diag[1] + shifted - dot3(aqp, fp)
        return xp, yp, sq, rq - dot3(aqp, yp), size

    def run(invert):
        xp, _, sq, reduced, size = outer_block(invert)
        inverse_p[...] = xp
        matrix_q[...] = sq
        source_q[...] = reduced
        pack_symmetric(sq, out)
        if inner_too:
            xq, size_q = invert(sq, hold, 1 / 16, 4)
            inverse_q[...] = xq
            value_q[...] = dot3(xq, reduced)
            pack_symmetric(xq, out_inverse)
            size = jnp.maximum(size, size_q)
        return size

    guarded(run)


def pack_full(matrix, out):
    n = matrix.shape[0]
    lanes = out.shape[1]
    out[0:n, :] = matrix[:, 0:lanes]
    out[n : n + n // 2, :] = jnp.concatenate(
        [matrix[0 : n // 2, lanes:], matrix[n // 2 :, lanes:]], axis=1
    )


def unpack_full(packed, n):
    rest = packed[n : n + n // 2]
    lanes = packed.shape[1]
    tail = jnp.concatenate([rest[:, : n - lanes], rest[:, n - lanes :]], axis=0)
    return jnp.concatenate([packed[0:n], tail], axis=1)


def spots(index, rows_all, depth, pitch, across, first_z, first_x):
    plane = rows_all * across
    z = index // plane - first_z
    x = index // across % rows_all - first_x
    y = index % across
    inside = (z >= 0) & (z < depth) & (x >= 0) & (x < pitch)
    row = jnp.where(inside, z * pitch + x, -1)
    n = index.shape[1]
    pick_row = lax.broadcasted_iota(jnp.int32, (depth * pitch, n), 0) == row
    pick_y = lax.broadcasted_iota(jnp.int32, (across, n), 0) == y
    return pick_row.astype(F32).astype(BF16), pick_y.astype(F32)


def region_start(depth_here, rows_here):
    first_z = lax.axis_index("slab") * depth_here - SWEEPS
    return first_z, lax.axis_index("energy") * rows_here - SWEEPS


def pack_kernel(factor_p, value_p, out):
    _, _, distance = place()
    width = value_p.shape[0]
    packed = width + width // 2

    @pl.when(distance < lax.axis_size("slab") // 2 - 1)
    def _():
        pack_full(factor_p[...], out)
        out[packed : packed + width, :] = value_p[...]


def ready_kernel(couple, even, odd, factor_p, value_p, inverse_p, matrix_q, source_q, matrix,
                 source, link, base, base_source, near, far, inner, reach, hold):
    slab, _, _ = place()
    half = lax.axis_size("slab") // 2

    @pl.when(slab == half - 1)
    def _():
        behind = couple[0]
        behind_t = behind.T
        across = dot3(inverse_p[...], behind)
        near[...] = across
        far[...] = factor_p[...]
        inner[...] = value_p[...]
        matrix[...] = dot3(behind_t, across)
        source[...] = dot3(behind_t, value_p[...])
        link[...] = -dot3(behind_t, factor_p[...])
        base[...] = matrix_q[...]
        base_source[...] = source_q[...]

    @pl.when(slab == half)
    def _():
        behind = couple[0]
        behind_t = behind.T
        ahead = following((even, odd))
        ahead_t = ahead.T
        back = dot3(inverse_p[...], behind)
        reach[...] = back
        side = dot3(couple[1], back)
        side_t = side.T

        def run(invert):
            solved, size = invert(matrix_q[...], hold, 1 / 16, 4)
            found = dot3(solved, source_q[...])
            across = dot3(solved, ahead_t)
            aside = dot3(solved, side)
            near[...] = across
            far[...] = -aside
            inner[...] = found
            matrix[...] = dot3(ahead, across)
            source[...] = dot3(ahead, found)
            link[...] = -dot3(ahead, aside)
            base[...] = dot3(behind_t, back) + dot3(side_t, aside)
            base_source[...] = dot3(behind_t, value_p[...]) - dot3(side_t, found)
            return size

        guarded(run)


def rows_kernel(potential, even_out, odd_out):
    halo = even_out.shape[1]
    low, high = potential[:, :halo], potential[:, potential.shape[1] - halo :]
    odd = lax.axis_index("energy") % 2 == 1
    even_out[...] = jnp.where(odd, low, high)
    odd_out[...] = jnp.where(odd, high, low)


def deposit_kernel(rows_all, pitch, depth, rows_here, dopants, dopant):
    first_z, first_x = region_start(depth, rows_here)
    rows, ys = spots(dopants[...], rows_all, depth + 2 * SWEEPS, pitch, dopant.shape[1], first_z,
                     first_x)
    dopant[...] = dopant_charge * one_pass(rows, ys.astype(BF16), NT)


def halo_kernel(potential, got_even, got_odd, wide):
    depth, rows_here, across = potential.shape
    even_e = lax.axis_index("energy") % 2 == 0
    below = jnp.where(even_e, got_odd[...], got_even[...])
    above = jnp.where(even_e, got_even[...], got_odd[...])
    spare = wide.shape[1] - rows_here - 2 * SWEEPS
    parts = [below, potential[...], above]
    if spare > 0:
        parts.append(jnp.zeros((depth, spare, across), F32))
    wide[...] = jnp.concatenate(parts, axis=1)


def put_planes(out, start, wide, high):
    pitch = wide.shape[1]
    last = wide.shape[0] - SWEEPS
    for k in range(SWEEPS):
        plane = jnp.where(high, wide[last + k], wide[k])
        out[start + k * pitch : start + (k + 1) * pitch, :] = plane


def middle_slab():
    slab, left, _ = place()
    half = lax.axis_size("slab") // 2
    return jnp.logical_or(slab == half - 1, slab == half), left


def centre_kernel(message, matrix, link, base, solved, factor, total, out, hold):
    here, left = middle_slab()

    @pl.when(here)
    def _():
        block = unpack_symmetric(message[...]) - matrix[...]
        near = link[...]
        near_t = near.T
        sign = jnp.where(left, -1.0, 1.0)

        def run(invert):
            found, size = invert(block, hold, 1 / 16, 4)
            reach = dot3(found, near)
            both = base[...] + sign * dot3(near_t, reach)
            pack_symmetric(both, out)
            solved[...] = found
            factor[...] = reach
            total[...] = both
            return size

        guarded(run)


def source_kernel(message, source, link, base_source, solved, value, total):
    here, _ = middle_slab()

    @pl.when(here)
    def _():
        found = dot3(solved[...], message[...] - source[...])
        value[...] = found
        total[...] = base_source[...] - dot3(link[...].T, found)


def expand_kernel(second, factor, value, factor_p, value_p, near, far, inner, reach, slope,
                  offset):
    here, left = middle_slab()
    width = value.shape[0]
    packed = width + width // 2

    def put(block, m, v):
        at = pl.ds(pl.multiple_of(block * width, width), width)
        slope[at, :] = m
        offset[at, :] = v

    @pl.when(here)
    def _():
        m1 = jnp.where(left, -1.0, 1.0) * factor[...]
        v1 = value[...]
        put(jnp.where(left, 3, 2), m1, v1)
        m2 = -(dot3(near[...], m1) + far[...])
        v2 = inner[...] - dot3(near[...], v1)
        put(jnp.where(left, 0, 1), m2, v2)

        @pl.when(left)
        def _():
            put(1, eye(width), jnp.zeros_like(v1))

        @pl.when(jnp.logical_not(left))
        def _():
            put(0, -(dot3(factor_p[...], m2) + reach[...]), value_p[...] - dot3(factor_p[...], v2))

        outer = unpack_full(second[0:packed, :], width)
        put(jnp.where(left, 2, 3), -dot3(outer, m1),
            second[packed : packed + width, :] - dot3(outer, v1))


def join_kernel(message, total, inverse, hold):
    here, left = middle_slab()

    @pl.when(here)
    def _():
        sign = jnp.where(left, -1.0, 1.0)
        matrix = sign * (unpack_symmetric(message[...]) - total[...])

        def run(invert):
            found, size = invert(matrix, hold, 1 / 48, 5)
            inverse[...] = found
            return size

        guarded(run)


def join_solution(message, inverse, total, left):
    sign = jnp.where(left, -1.0, 1.0)
    return dot3(inverse[...], sign * (message[...] - total[...]))


def values_kernel(message, inverse, total, slope, offset, values):
    here, left = middle_slab()

    @pl.when(here)
    def _():
        middle = join_solution(message, inverse, total, left)
        values[...] = offset[...] + dot3(slope[...], middle)


def density_kernel(values, probes, probes_near, dens):
    here, _ = middle_slab()

    @pl.when(here)
    def _():
        n = probes.shape[0]
        terms = jnp.concatenate(
            [probes[...] * values[0:n, :], probes_near[...] * values[n:, :]], axis=0
        )
        dens[...] = dot6(jnp.ones((8, terms.shape[1]), F32), terms, NT)[0:1]


def middle_kernel(message, inverse, total, factor, value, out_first, out_middle):
    here, left = middle_slab()

    @pl.when(here)
    def _():
        middle = join_solution(message, inverse, total, left)
        sign = jnp.where(left, -1.0, 1.0)
        out_first[...] = value[...] + sign * dot3(factor[...], middle)
        out_middle[...] = middle


def back_kernel(step, couple, even, odd, probes, message, first, middle, known_p, known_q,
                factor_p, value_p, inverse_q, value_q, near, far, inner, reach, out_p, out_q,
                dens):
    _, left, distance = place()
    centre = lax.axis_size("slab") // 2 - 1
    width = couple.shape[1]

    @pl.when(jnp.logical_and(distance < centre, distance != step))
    def _():
        out_p[...] = known_p[...]
        out_q[...] = known_q[...]

    @pl.when(jnp.logical_and(distance == step, step == centre - 1))
    def _():
        xq = message[...]
        out_q[...] = xq
        out_p[...] = value_p[...] - dot3(factor_p[...], xq)

    @pl.when(jnp.logical_and(distance == step, step < centre - 1))
    def _():
        link = jnp.where(left, following((even, odd)).T, couple[0])
        xq = value_q[...] - dot3(inverse_q[...], dot3(link, message[...]))
        out_q[...] = xq
        out_p[...] = value_p[...] - dot3(factor_p[...], xq)

    @pl.when(distance == centre)
    def _():
        xi = inner[...] - dot3(near[...], first[...]) - dot3(far[...], middle[...])
        out_p[...] = xi
        out_q[...] = middle[...]

        @pl.when(jnp.logical_not(left))
        def _():
            out_q[...] = value_p[...] - dot3(factor_p[...], xi) - dot3(reach[...], middle[...])

    xp = out_p[...]
    xq = out_q[...]
    xa = jnp.where(left, xp, xq)
    xb = jnp.where(left, xq, xp)
    terms = jnp.concatenate([probes[0:width, :] * xa, probes[width:, :] * xb], axis=0)
    dens[...] = dot6(jnp.ones((8, terms.shape[1]), F32), terms, NT)[0:1]


def total_kernel(scale, cells, wide, *rest):
    parts, outs = rest[:-2], rest[-2:]
    total = parts[0][...]
    for part in parts[1:]:
        total = total + part[...]
    total = total * scale
    place_of = cells[...].astype(F32)
    lanes = wide.shape[2]
    values = total.shape[1] // lanes
    even = lax.axis_index("slab") % 2 == 0
    for out, high in zip(outs, (even, jnp.logical_not(even))):
        for k in range(values):
            out[k : k + 1, :] = total[:, k * lanes : (k + 1) * lanes]
        for k in range(cells.shape[1] // lanes):
            out[values + k : values + k + 1, :] = place_of[:, k * lanes : (k + 1) * lanes]
        put_planes(out, packet_planes(values, cells.shape[1] // lanes), wide, high)


def packet_planes(values, cells):
    return -(-(values + cells) // 8) * 8


def packet_row(packet, first, count):
    return jnp.concatenate([packet[first + k : first + k + 1, :] for k in range(count)], axis=1)


def poisson_kernel(rows_all, planes, paired, packet, near, far, dopant_grid, wide, out, density):
    slab, slabs = lax.axis_index("slab"), lax.axis_size("slab")
    depth, pitch, across = wide.shape
    depth = depth + 2 * SWEEPS
    first_z, first_x = region_start(out.shape[0], out.shape[1])
    n = density.shape[0]
    even = slab % 2 == 0
    alone = jnp.logical_or(slab == 0, slab == slabs - 1)
    count = n // across
    values = 2 * count if paired else count
    own, beside, beyond = [packet_row(p, 0, count) for p in (packet, near, far)]
    if paired:
        own = jnp.where(alone, packet_row(near, count, count), own)
        beside = jnp.where(alone, beside, packet_row(packet, count, count))
    density[...] = own.reshape(n)
    weights = jnp.concatenate([own, beside, jnp.where(alone, 0.0, beyond)], axis=1)
    orbitals = jnp.concatenate([packet_row(p, values, count) for p in (packet, near, far)], axis=1)
    orbitals = jnp.where(jnp.abs(orbitals) < 2.0**30, orbitals, -1.0).astype(jnp.int32)
    rows, ys = spots(orbitals, rows_all, depth, pitch, across, first_z, first_x)
    spread = ys * weights
    h = spread.astype(BF16)
    rest = spread - h.astype(F32)
    m = rest.astype(BF16)
    low = (rest - m.astype(F32)).astype(BF16)
    electron = one_pass(rows, h, NT) + (one_pass(rows, m, NT) + one_pass(rows, low, NT))
    electron = electron.reshape(depth, pitch, across)
    dopant = dopant_grid[...].reshape(depth, pitch, across)
    near_planes = near[packet_planes(values, count) :, :].reshape(SWEEPS, pitch, across)
    far_planes = far[packet_planes(values, count) :, :].reshape(SWEEPS, pitch, across)
    start = jnp.concatenate(
        [jnp.where(even, far_planes, near_planes), wide[...],
         jnp.where(even, near_planes, far_planes)],
        axis=0,
    )
    zs = lax.broadcasted_iota(jnp.int32, start.shape, 0) + first_z
    xs = lax.broadcasted_iota(jnp.int32, start.shape, 1) + first_x
    ys = lax.broadcasted_iota(jnp.int32, start.shape, 2)
    exists = (zs >= 0) & (zs < planes) & (xs >= 0) & (xs < rows_all)
    potential = jnp.where(exists, start, 0.0)
    start = potential
    strength = coupling_beta * jnp.abs(electron)
    for _ in range(SWEEPS):
        blank = jnp.zeros((1, pitch, across), F32)
        beside = jnp.concatenate([potential[1:], blank], axis=0)
        beside = beside + jnp.concatenate([blank, potential[:-1]], axis=0)
        beside = beside + pltpu.roll(potential, 1, 1) + pltpu.roll(potential, pitch - 1, 1)
        beside = beside + jnp.where(ys > 0, pltpu.roll(potential, 1, 2), 0.0)
        beside = beside + jnp.where(ys < across - 1, pltpu.roll(potential, across - 1, 2), 0.0)
        growth = jnp.exp(potential - start)
        residual = beside - 6.0 * potential + coupling_beta * (dopant - electron * growth)
        potential = potential + residual / (6.0 + strength * growth)
        potential = jnp.where(exists, potential, 0.0)
    halo = SWEEPS
    out[...] = potential[halo : halo + out.shape[0], halo : halo + out.shape[1], :]


VM = pl.BlockSpec(memory_space=pltpu.VMEM)
FAR = pl.BlockSpec(memory_space=pltpu.HBM)
GRANT = 16 << 20


def like(*shape, dtype=F32):
    return jax.ShapeDtypeStruct(shape, dtype)


def call(kernel, outs, args, scratch=(), distant=0, flops=10**8):
    args = list(args)
    for k in range(distant):
        args[k] = pltpu.with_memory_space_constraint(args[k], pltpu.HBM)
    own = [pltpu.VMEM(shape, F32) for shape in scratch]
    if distant:
        own += [pltpu.SemaphoreType.DMA((distant + 1,))]
    return pl.pallas_call(
        kernel,
        out_shape=outs,
        in_specs=[FAR] * distant + [VM] * (len(args) - distant),
        out_specs=jax.tree.map(lambda _: VM, outs),
        scratch_shapes=own,
        compiler_params=pltpu.CompilerParams(vmem_limit_bytes=GRANT),
        cost_estimate=pl.CostEstimate(flops=flops, bytes_accessed=10**6, transcendentals=0),
    )(*args)


def pairs_of(count, odd):
    found = []
    for first in range(1 if odd else 0, count - 1, 2):
        found += [(first, first + 1), (first + 1, first)]
    return found


def slab_exchange(value, odd):
    slabs, energies = lax.axis_size("slab"), lax.axis_size("energy")
    pairs = pairs_of(slabs, odd)
    busy = {a for a, _ in pairs}
    whole = [(a * energies + e, b * energies + e) for a, b in pairs for e in range(energies)]
    for a in range(slabs):
        if a not in busy:
            whole += [(a * energies + e, a * energies + (e ^ 1)) for e in range(energies)]
    return lax.ppermute(value, ("slab", "energy"), whole)


def energy_exchange(value, odd):
    energies = lax.axis_size("energy")
    pairs = pairs_of(energies, odd)
    if odd:
        pairs += [(energies - 1, 0), (0, energies - 1)]
    return lax.ppermute(value, "energy", pairs)


def program(energy_index, diag_blocks, couple, probes, orbital_cell, dopant_cells, initial_potential):
    width = diag_blocks.shape[1]
    probe_count = probes.shape[1]
    slabs = lax.axis_size("slab")
    energies = lax.axis_size("energy")
    half = slabs // 2
    square, column = like(width, width), like(width, probe_count)
    letter = like(width, probe_count)
    sq = (width, width)

    even = slab_exchange(couple[0], False)
    paired = half == 2
    odd = even
    if not paired:
        odd = lax.ppermute(couple[0], "slab", [(s + 1, s) for s in range(1, slabs - 1, 2)])

    message = None
    for t in range(half - 1):
        args = [diag_blocks, couple, probes, energy_index.reshape(1, 1)]
        if t > 0:
            if t > 1:
                _, _, distance = place()
                message = jnp.where(distance == t, message, kept[0])
                sources = jnp.where(distance == t, sources, kept[1])
            kept = message, sources
            args += [message, sources, even, odd]
        outs = (square, column, square, square, column, letter)
        if not paired:
            outs += (square, column, letter)
        state = call(
            functools.partial(stage_kernel, t, not paired), outs,
            args, (sq, diag_blocks.shape, couple.shape, probes.shape), 3,
        )
        if t == 0:
            prepared = state
        last = t == half - 2
        message = slab_exchange(state[5] if last else state[8], t % 2 == 1)
        if not last:
            sources = slab_exchange(state[7], t % 2 == 1)
    factor_p, value_p = state[:2]
    matrix, source, link, base, base_source, near_map, far_map, inner, reach = call(
        ready_kernel,
        (square, column, square, square, column, square, square, column, square),
        [couple, even, odd, *prepared[:5]], (sq,),
    )
    reduced, first_factor, reach = lax.optimization_barrier((state[4], prepared[0], reach))
    sources = slab_exchange(reduced, half % 2 == 1)

    depth, rows_here, across = initial_potential.shape
    halo = SWEEPS
    rows_all = rows_here * energies
    pitch = -(-(rows_here + 2 * halo) // 8) * 8
    strip = halo * pitch
    even_rows, odd_rows = call(rows_kernel, (like(depth, halo, across),) * 2, [initial_potential])
    got_even = energy_exchange(even_rows, False)
    got_odd = energy_exchange(odd_rows, True)
    cells = (depth + 2 * halo) * pitch
    second = call(
        pack_kernel, like(width + width // 2 + width, probe_count),
        [first_factor, prepared[1]],
    )
    if paired:
        probes_near = slab_exchange(probes, False)
        second = slab_exchange(second, False)
    dopant_grid = call(
        functools.partial(deposit_kernel, rows_all, pitch, depth, rows_here),
        like(cells, across), [dopant_cells.reshape(1, -1)],
    )
    solved, factor, total, sent = call(
        centre_kernel, (square, square, square, letter),
        [message, matrix, link, base], (sq,),
    )
    across_middle = slab_exchange(sent, half % 2 == 0)
    value, total_source = call(
        source_kernel, (column, column),
        [sources, source, link, base_source, solved],
    )
    sources_middle = slab_exchange(total_source, half % 2 == 0)
    wide = call(
        halo_kernel, like(depth, pitch, across),
        [initial_potential, *lax.optimization_barrier((got_even, got_odd, sent))[:2]],
    )
    inverse = call(join_kernel, square, [across_middle, total], (sq,))
    if paired:
        slope, offset = call(
            expand_kernel, (like(4 * width, width), like(4 * width, probe_count)),
            [second, factor, value, *prepared[:2], near_map, far_map, inner, reach],
        )
        values = call(
            values_kernel, like(4 * width, probe_count),
            [sources_middle, inverse, total_source, slope, offset],
        )
        dens = call(density_kernel, like(1, 4 * width), [values, probes, probes_near])
    else:
        first, middle = call(
            middle_kernel, (column, column),
            [sources_middle, inverse, total_source, factor, value],
        )
        centred = (lax.axis_index("slab") == half) | (lax.axis_index("slab") == half - 1)
        factor_p = jnp.where(centred, prepared[0], factor_p)
        value_p = jnp.where(centred, prepared[1], value_p)
        known_p, known_q = first, middle
        for t in range(half - 2, -1, -1):
            known_p, known_q, dens = call(
                functools.partial(back_kernel, t),
                (column, column, like(1, 2 * width)),
                [couple, even, odd, probes, slab_exchange(first if t == half - 2 else known_p, t % 2 == 1),
                 first, middle,
                 known_p, known_q, factor_p, value_p, state[6], state[7], near_map, far_map, inner,
                 reach],
            )
    parts = [dens] + [
        lax.ppermute(dens, "energy", [(e, (e + k) % energies) for e in range(energies)])
        for k in range(1, energies)
    ]
    spare = packet_planes(dens.shape[1] // across, orbital_cell.shape[0] // across)
    packet, packet_far = call(
        functools.partial(total_kernel, 1.0 / (probe_count * energies)),
        (like(spare + strip, across),) * 2, [orbital_cell.reshape(1, -1), wide, *parts],
    )
    near = slab_exchange(packet, False)
    far = slab_exchange(packet_far, True)

    def poisson(*refs):
        poisson_kernel(rows_all, depth * slabs, paired, *refs)

    potential, density = call(
        poisson, (like(depth, rows_here, across), like(2 * width)),
        [packet, near, far, dopant_grid, wide],
    )
    return (potential, density)


def solution(mesh):
    placed = (
        P("energy"),
        P(("cfg", "slab"), None, None),
        P(("cfg", "slab"), None, None),
        P("slab", None),
        P("slab"),
        P("cfg"),
        P(("cfg", "slab"), "energy", None),
    )
    return jax.shard_map(
        program,
        mesh=mesh,
        in_specs=placed,
        out_specs=(P(("cfg", "slab"), "energy", None), P(("cfg", "slab"))),
        check_vma=False,
    )
```

```python
import functools

import jax
import jax.numpy as jnp
from jax import lax
from jax.experimental import pallas as pl
from jax.experimental.pallas import tpu as pltpu
from jax.sharding import PartitionSpec as P


SWEEPS = 2

sigma_base = 0.02
sigma_step = 0.01
coupling_beta = 0.5
dopant_charge = 4.0

F32 = jnp.float32
BF16 = jnp.bfloat16
NT = (((1,), (1,)), ((), ()))
NN = (((1,), (0,)), ((), ()))


def split2(a):
    high = a.astype(BF16)
    return high, (a - high.astype(F32)).astype(BF16)


def one_pass(a, b, dims=NN):
    return lax.dot_general(a, b, dims, preferred_element_type=F32)


def dot3(a, b):
    ah, al = split2(a)
    bh, bl = split2(b)
    return one_pass(ah, bh) + (one_pass(ah, bl) + one_pass(al, bh))


def dot6(a, b, dims=NN):
    return lax.dot_general(
        a, b, dims, precision=lax.Precision.HIGHEST, preferred_element_type=F32
    )


def eye(n):
    return (
        lax.broadcasted_iota(jnp.int32, (n, n), 0) == lax.broadcasted_iota(jnp.int32, (n, n), 1)
    ).astype(F32)


def estimate(matrix, ratio, doublings):
    unit = eye(matrix.shape[0])
    square = dot3(matrix, matrix)
    sums = jnp.sum(jnp.abs(square), axis=0, keepdims=True)
    bound = jnp.sqrt(jnp.max(sums, axis=1, keepdims=True))
    first = 2.0 / (bound * (1.0 + ratio))
    tau = (1.0 + ratio) / (1.0 - ratio)
    for k in range(doublings):
        after = 2.0 * tau * tau - 1.0
        scale = (after + 1.0) / after
        if k == 0:
            grown = (2.0 * first) * unit - (first * first) * matrix
            squared = unit - (2.0 * first) * matrix + (first * first) * square
        else:
            grown = guess + dot3(guess, error)
            squared = dot3(error, error) if k + 1 < doublings else None
        guess = scale * grown
        if k + 1 < doublings:
            error = scale * squared - (scale - 1.0) * unit
        tau = after
    residual = unit - dot6(matrix, guess)
    step = one_pass(guess.astype(BF16), residual.astype(BF16))
    return guess + step, jnp.sum(residual * residual), first


def fast(matrix, hold, ratio, doublings):
    found, size, _ = estimate(matrix, ratio, doublings)
    return found, size


def careful(matrix, hold, ratio, doublings):
    unit = eye(matrix.shape[0])
    found, size, first = estimate(matrix, ratio, doublings)
    hold[...] = found

    @pl.when(jnp.logical_not(size < 0.9))
    def _():
        hold[...] = first * unit

    def go_on(state):
        count, last = state
        return jnp.logical_and(count < 64, jnp.logical_not(last < 1e-6))

    def newton(state):
        count, _ = state
        now = hold[...]
        left = unit - dot6(matrix, now)
        hold[...] = now + dot6(now, left)
        return count + 1, jnp.sum(left * left)

    lax.while_loop(go_on, newton, (jnp.int32(0), size))
    return hold[...], size


def guarded(run):
    worst = run(fast)

    @pl.when(jnp.logical_not(worst < 1e-4))
    def _():
        run(careful)


def pack_symmetric(matrix, out):
    half = matrix.shape[0] // 3
    out[0:half, :] = matrix[half : 2 * half, 0 : 2 * half]
    out[half : 2 * half, :] = matrix[2 * half :, 0 : 2 * half]
    out[2 * half : 3 * half, :] = jnp.concatenate(
        [matrix[0:half, 0:half], matrix[2 * half :, 2 * half :]], axis=1
    )


def unpack_symmetric(packed):
    third = packed.shape[0] // 3
    row1 = packed[0:third]
    row2 = packed[third : 2 * third]
    ends = packed[2 * third :]
    b10, b11 = row1[:, :third], row1[:, third:]
    b20, b21 = row2[:, :third], row2[:, third:]
    b00, b22 = ends[:, :third], ends[:, third:]
    return jnp.concatenate(
        [
            jnp.concatenate([b00, b10.T, b20.T], axis=1),
            jnp.concatenate([b10, b11, b21.T], axis=1),
            jnp.concatenate([b20, b21, b22], axis=1),
        ],
        axis=0,
    )


def place():
    slab, slabs = lax.axis_index("slab"), lax.axis_size("slab")
    left = slab < slabs // 2
    return slab, left, jnp.where(left, slab, slabs - 1 - slab)


def following(ahead):
    even, odd = ahead
    return jnp.where(lax.axis_index("slab") % 2 == 0, even[...], odd[...])


def take_block(message, couple, ahead, left):
    link_t = jnp.where(left, couple[0].T, following(ahead))
    link = jnp.where(left, couple[0], following(ahead).T)
    return dot3(link, dot3(unpack_symmetric(message[...]), link_t))


def take_column(message, couple, ahead, left):
    return dot3(jnp.where(left, couple[0], following(ahead).T), message[...])


def stage_kernel(step, inner_too, diag_far, couple_far, probes_far, energy, *rest):
    if step > 0:
        message, sources, even, odd, rest = rest[0], rest[1], rest[2], rest[3], rest[4:]
    factor_p, value_p, inverse_p, matrix_q, source_q, out = rest[:6]
    rest = rest[6:]
    if inner_too:
        inverse_q, value_q, out_inverse = rest[:3]
        rest = rest[3:]
    hold, diag, couple, probes, sems = rest
    _, left, distance = place()
    forward = lax.axis_index("slab") <= lax.axis_size("slab") // 2
    first = jnp.where(forward, 0, 1)
    width = diag.shape[1]
    loads = [
        pltpu.make_async_copy(diag_far.at[first], diag.at[0], sems.at[0]),
        pltpu.make_async_copy(couple_far, couple, sems.at[1]),
        pltpu.make_async_copy(probes_far, probes, sems.at[2]),
        pltpu.make_async_copy(diag_far.at[1 - first], diag.at[1], sems.at[3]),
    ]
    for load in loads:
        load.start()
    loads[0].wait()
    if step > 0:
        loads[1].wait()
    shift = sigma_base + sigma_step * energy[...].astype(F32)
    shifted = shift * eye(width)
    sp = diag[0] + shifted
    if step > 0:
        taken = jnp.logical_and(distance >= 1, distance <= step)
        ahead = (even, odd)
        sp = sp - jnp.where(taken, take_block(message, couple, ahead, left), 0.0)
        extra = jnp.where(taken, take_column(sources, couple, ahead, left), 0.0)

    def await_loads():
        for load in loads[2 if step > 0 else 1 :]:
            load.wait()

    def outer_block(invert):
        xp, size = invert(sp, hold, 1 / 16, 4)
        if invert is fast:
            await_loads()
        rp = probes[pl.ds(pl.multiple_of(first * width, width), width), :]
        rq = probes[pl.ds(pl.multiple_of((1 - first) * width, width), width), :]
        if step > 0:
            rp = rp - extra
        inner = couple[1]
        inner_t = inner.T
        apq = jnp.where(forward, inner_t, inner)
        aqp = jnp.where(forward, inner, inner_t)
        fp = dot3(xp, apq)
        yp = dot3(xp, rp)
        factor_p[...] = fp
        value_p[...] = yp
        sq = diag[1] + shifted - dot3(aqp, fp)
        return xp, yp, sq, rq - dot3(aqp, yp), size

    def run(invert):
        xp, _, sq, reduced, size = outer_block(invert)
        inverse_p[...] = xp
        matrix_q[...] = sq
        source_q[...] = reduced
        pack_symmetric(sq, out)
        if inner_too:
            xq, size_q = invert(sq, hold, 1 / 16, 4)
            inverse_q[...] = xq
            value_q[...] = dot3(xq, reduced)
            pack_symmetric(xq, out_inverse)
            size = jnp.maximum(size, size_q)
        return size

    guarded(run)


def pack_full(matrix, out):
    n = matrix.shape[0]
    lanes = out.shape[1]
    out[0:n, :] = matrix[:, 0:lanes]
    out[n : n + n // 2, :] = jnp.concatenate(
        [matrix[0 : n // 2, lanes:], matrix[n // 2 :, lanes:]], axis=1
    )


def unpack_full(packed, n):
    rest = packed[n : n + n // 2]
    lanes = packed.shape[1]
    tail = jnp.concatenate([rest[:, : n - lanes], rest[:, n - lanes :]], axis=0)
    return jnp.concatenate([packed[0:n], tail], axis=1)


def spots(index, rows_all, depth, pitch, across, first_z, first_x):
    plane = rows_all * across
    z = index // plane - first_z
    x = index // across % rows_all - first_x
    y = index % across
    inside = (z >= 0) & (z < depth) & (x >= 0) & (x < pitch)
    row = jnp.where(inside, z * pitch + x, -1)
    n = index.shape[1]
    pick_row = lax.broadcasted_iota(jnp.int32, (depth * pitch, n), 0) == row
    pick_y = lax.broadcasted_iota(jnp.int32, (across, n), 0) == y
    return pick_row.astype(F32).astype(BF16), pick_y.astype(F32)


def region_start(depth_here, rows_here):
    first_z = lax.axis_index("slab") * depth_here - SWEEPS
    return first_z, lax.axis_index("energy") * rows_here - SWEEPS


def pack_kernel(factor_p, value_p, out):
    _, _, distance = place()
    width = value_p.shape[0]
    packed = width + width // 2

    @pl.when(distance < lax.axis_size("slab") // 2 - 1)
    def _():
        pack_full(factor_p[...], out)
        out[packed : packed + width, :] = value_p[...]


def ready_kernel(couple, even, odd, factor_p, value_p, inverse_p, matrix_q, source_q, matrix,
                 source, link, base, base_source, near, far, inner, reach, hold):
    slab, _, _ = place()
    half = lax.axis_size("slab") // 2

    @pl.when(slab == half - 1)
    def _():
        behind = couple[0]
        behind_t = behind.T
        across = dot3(inverse_p[...], behind)
        near[...] = across
        far[...] = factor_p[...]
        inner[...] = value_p[...]
        matrix[...] = dot3(behind_t, across)
        source[...] = dot3(behind_t, value_p[...])
        link[...] = -dot3(behind_t, factor_p[...])
        base[...] = matrix_q[...]
        base_source[...] = source_q[...]

    @pl.when(slab == half)
    def _():
        behind = couple[0]
        behind_t = behind.T
        ahead = following((even, odd))
        ahead_t = ahead.T
        back = dot3(inverse_p[...], behind)
        reach[...] = back
        side = dot3(couple[1], back)
        side_t = side.T

        def run(invert):
            solved, size = invert(matrix_q[...], hold, 1 / 16, 4)
            found = dot3(solved, source_q[...])
            across = dot3(solved, ahead_t)
            aside = dot3(solved, side)
            near[...] = across
            far[...] = -aside
            inner[...] = found
            matrix[...] = dot3(ahead, across)
            source[...] = dot3(ahead, found)
            link[...] = -dot3(ahead, aside)
            base[...] = dot3(behind_t, back) + dot3(side_t, aside)
            base_source[...] = dot3(behind_t, value_p[...]) - dot3(side_t, found)
            return size

        guarded(run)


def rows_kernel(potential, even_out, odd_out):
    halo = even_out.shape[1]
    low, high = potential[:, :halo], potential[:, potential.shape[1] - halo :]
    odd = lax.axis_index("energy") % 2 == 1
    even_out[...] = jnp.where(odd, low, high)
    odd_out[...] = jnp.where(odd, high, low)


def deposit_kernel(rows_all, pitch, depth, rows_here, dopants, dopant):
    first_z, first_x = region_start(depth, rows_here)
    rows, ys = spots(dopants[...], rows_all, depth + 2 * SWEEPS, pitch, dopant.shape[1], first_z,
                     first_x)
    dopant[...] = dopant_charge * one_pass(rows, ys.astype(BF16), NT)


def halo_kernel(potential, got_even, got_odd, wide):
    depth, rows_here, across = potential.shape
    even_e = lax.axis_index("energy") % 2 == 0
    below = jnp.where(even_e, got_odd[...], got_even[...])
    above = jnp.where(even_e, got_even[...], got_odd[...])
    spare = wide.shape[1] - rows_here - 2 * SWEEPS
    parts = [below, potential[...], above]
    if spare > 0:
        parts.append(jnp.zeros((depth, spare, across), F32))
    wide[...] = jnp.concatenate(parts, axis=1)


def put_planes(out, start, wide, high):
    pitch = wide.shape[1]
    last = wide.shape[0] - SWEEPS
    for k in range(SWEEPS):
        plane = jnp.where(high, wide[last + k], wide[k])
        out[start + k * pitch : start + (k + 1) * pitch, :] = plane


def middle_slab():
    slab, left, _ = place()
    half = lax.axis_size("slab") // 2
    return jnp.logical_or(slab == half - 1, slab == half), left


def centre_kernel(message, matrix, link, base, solved, factor, total, out, hold):
    here, left = middle_slab()

    @pl.when(here)
    def _():
        block = unpack_symmetric(message[...]) - matrix[...]
        near = link[...]
        near_t = near.T
        sign = jnp.where(left, -1.0, 1.0)

        def run(invert):
            found, size = invert(block, hold, 1 / 16, 4)
            reach = dot3(found, near)
            both = base[...] + sign * dot3(near_t, reach)
            pack_symmetric(both, out)
            solved[...] = found
            factor[...] = reach
            total[...] = both
            return size

        guarded(run)


def source_kernel(message, source, link, base_source, solved, value, total):
    here, _ = middle_slab()

    @pl.when(here)
    def _():
        found = dot3(solved[...], message[...] - source[...])
        value[...] = found
        total[...] = base_source[...] - dot3(link[...].T, found)


def expand_kernel(second, factor, value, factor_p, value_p, near, far, inner, reach, slope,
                  offset):
    here, left = middle_slab()
    width = value.shape[0]
    packed = width + width // 2

    def put(block, m, v):
        at = pl.ds(pl.multiple_of(block * width, width), width)
        slope[at, :] = m
        offset[at, :] = v

    @pl.when(here)
    def _():
        m1 = jnp.where(left, -1.0, 1.0) * factor[...]
        v1 = value[...]
        put(jnp.where(left, 3, 2), m1, v1)
        m2 = -(dot3(near[...], m1) + far[...])
        v2 = inner[...] - dot3(near[...], v1)
        put(jnp.where(left, 0, 1), m2, v2)

        @pl.when(left)
        def _():
            put(1, eye(width), jnp.zeros_like(v1))

        @pl.when(jnp.logical_not(left))
        def _():
            put(0, -(dot3(factor_p[...], m2) + reach[...]), value_p[...] - dot3(factor_p[...], v2))

        outer = unpack_full(second[0:packed, :], width)
        put(jnp.where(left, 2, 3), -dot3(outer, m1),
            second[packed : packed + width, :] - dot3(outer, v1))


def join_kernel(message, total, inverse, hold):
    here, left = middle_slab()

    @pl.when(here)
    def _():
        sign = jnp.where(left, -1.0, 1.0)
        matrix = sign * (unpack_symmetric(message[...]) - total[...])

        def run(invert):
            found, size = invert(matrix, hold, 1 / 48, 5)
            inverse[...] = found
            return size

        guarded(run)


def join_solution(message, inverse, total, left):
    sign = jnp.where(left, -1.0, 1.0)
    return dot3(inverse[...], sign * (message[...] - total[...]))


def values_kernel(message, inverse, total, slope, offset, values):
    here, left = middle_slab()

    @pl.when(here)
    def _():
        middle = join_solution(message, inverse, total, left)
        values[...] = offset[...] + dot3(slope[...], middle)


def density_kernel(values, probes, probes_near, dens):
    here, _ = middle_slab()

    @pl.when(here)
    def _():
        n = probes.shape[0]
        terms = jnp.concatenate(
            [probes[...] * values[0:n, :], probes_near[...] * values[n:, :]], axis=0
        )
        dens[...] = dot6(jnp.ones((8, terms.shape[1]), F32), terms, NT)[0:1]


def middle_kernel(message, inverse, total, factor, value, out_first, out_middle):
    here, left = middle_slab()

    @pl.when(here)
    def _():
        middle = join_solution(message, inverse, total, left)
        sign = jnp.where(left, -1.0, 1.0)
        out_first[...] = value[...] + sign * dot3(factor[...], middle)
        out_middle[...] = middle


def back_kernel(step, couple, even, odd, probes, message, first, middle, known_p, known_q,
                factor_p, value_p, inverse_q, value_q, near, far, inner, reach, out_p, out_q,
                dens):
    _, left, distance = place()
    centre = lax.axis_size("slab") // 2 - 1
    width = couple.shape[1]

    @pl.when(jnp.logical_and(distance < centre, distance != step))
    def _():
        out_p[...] = known_p[...]
        out_q[...] = known_q[...]

    @pl.when(jnp.logical_and(distance == step, step == centre - 1))
    def _():
        xq = message[...]
        out_q[...] = xq
        out_p[...] = value_p[...] - dot3(factor_p[...], xq)

    @pl.when(jnp.logical_and(distance == step, step < centre - 1))
    def _():
        link = jnp.where(left, following((even, odd)).T, couple[0])
        xq = value_q[...] - dot3(inverse_q[...], dot3(link, message[...]))
        out_q[...] = xq
        out_p[...] = value_p[...] - dot3(factor_p[...], xq)

    @pl.when(distance == centre)
    def _():
        xi = inner[...] - dot3(near[...], first[...]) - dot3(far[...], middle[...])
        out_p[...] = xi
        out_q[...] = middle[...]

        @pl.when(jnp.logical_not(left))
        def _():
            out_q[...] = value_p[...] - dot3(factor_p[...], xi) - dot3(reach[...], middle[...])

    xp = out_p[...]
    xq = out_q[...]
    xa = jnp.where(left, xp, xq)
    xb = jnp.where(left, xq, xp)
    terms = jnp.concatenate([probes[0:width, :] * xa, probes[width:, :] * xb], axis=0)
    dens[...] = dot6(jnp.ones((8, terms.shape[1]), F32), terms, NT)[0:1]


def total_kernel(scale, cells, wide, *rest):
    parts, outs = rest[:-2], rest[-2:]
    total = parts[0][...]
    for part in parts[1:]:
        total = total + part[...]
    total = total * scale
    place_of = cells[...].astype(F32)
    lanes = wide.shape[2]
    values = total.shape[1] // lanes
    even = lax.axis_index("slab") % 2 == 0
    for out, high in zip(outs, (even, jnp.logical_not(even))):
        for k in range(values):
            out[k : k + 1, :] = total[:, k * lanes : (k + 1) * lanes]
        for k in range(cells.shape[1] // lanes):
            out[values + k : values + k + 1, :] = place_of[:, k * lanes : (k + 1) * lanes]
        put_planes(out, packet_planes(values, cells.shape[1] // lanes), wide, high)


def packet_planes(values, cells):
    return -(-(values + cells) // 8) * 8


def packet_row(packet, first, count):
    return jnp.concatenate([packet[first + k : first + k + 1, :] for k in range(count)], axis=1)


def poisson_kernel(rows_all, planes, paired, packet, near, far, dopant_grid, wide, out, density):
    slab, slabs = lax.axis_index("slab"), lax.axis_size("slab")
    depth, pitch, across = wide.shape
    depth = depth + 2 * SWEEPS
    first_z, first_x = region_start(out.shape[0], out.shape[1])
    n = density.shape[0]
    even = slab % 2 == 0
    alone = jnp.logical_or(slab == 0, slab == slabs - 1)
    count = n // across
    values = 2 * count if paired else count
    own, beside, beyond = [packet_row(p, 0, count) for p in (packet, near, far)]
    if paired:
        own = jnp.where(alone, packet_row(near, count, count), own)
        beside = jnp.where(alone, beside, packet_row(packet, count, count))
    density[...] = own.reshape(n)
    weights = jnp.concatenate([own, beside, jnp.where(alone, 0.0, beyond)], axis=1)
    orbitals = jnp.concatenate([packet_row(p, values, count) for p in (packet, near, far)], axis=1)
    orbitals = jnp.where(jnp.abs(orbitals) < 2.0**30, orbitals, -1.0).astype(jnp.int32)
    rows, ys = spots(orbitals, rows_all, depth, pitch, across, first_z, first_x)
    high = weights.astype(BF16).astype(F32)
    middle = (weights - high).astype(BF16).astype(F32)
    h = (ys * high).astype(BF16)
    m = (ys * middle).astype(BF16)
    low = (ys * (weights - high - middle)).astype(BF16)
    electron = one_pass(rows, h, NT) + (one_pass(rows, m, NT) + one_pass(rows, low, NT))
    electron = electron.reshape(depth, pitch, across)
    dopant = dopant_grid[...].reshape(depth, pitch, across)
    near_planes = near[packet_planes(values, count) :, :].reshape(SWEEPS, pitch, across)
    far_planes = far[packet_planes(values, count) :, :].reshape(SWEEPS, pitch, across)
    start = jnp.concatenate(
        [jnp.where(even, far_planes, near_planes), wide[...],
         jnp.where(even, near_planes, far_planes)],
        axis=0,
    )
    zs = lax.broadcasted_iota(jnp.int32, start.shape, 0) + first_z
    xs = lax.broadcasted_iota(jnp.int32, start.shape, 1) + first_x
    ys = lax.broadcasted_iota(jnp.int32, start.shape, 2)
    exists = (zs >= 0) & (zs < planes) & (xs >= 0) & (xs < rows_all)
    potential = jnp.where(exists, start, 0.0)
    start = potential
    strength = coupling_beta * jnp.abs(electron)
    for _ in range(SWEEPS):
        blank = jnp.zeros((1, pitch, across), F32)
        beside = jnp.concatenate([potential[1:], blank], axis=0)
        beside = beside + jnp.concatenate([blank, potential[:-1]], axis=0)
        beside = beside + pltpu.roll(potential, 1, 1) + pltpu.roll(potential, pitch - 1, 1)
        beside = beside + jnp.where(ys > 0, pltpu.roll(potential, 1, 2), 0.0)
        beside = beside + jnp.where(ys < across - 1, pltpu.roll(potential, across - 1, 2), 0.0)
        growth = jnp.exp(potential - start)
        residual = beside - 6.0 * potential + coupling_beta * (dopant - electron * growth)
        potential = potential + residual / (6.0 + strength * growth)
        potential = jnp.where(exists, potential, 0.0)
    halo = SWEEPS
    out[...] = potential[halo : halo + out.shape[0], halo : halo + out.shape[1], :]


VM = pl.BlockSpec(memory_space=pltpu.VMEM)
FAR = pl.BlockSpec(memory_space=pltpu.HBM)
GRANT = 16 << 20


def like(*shape, dtype=F32):
    return jax.ShapeDtypeStruct(shape, dtype)


def call(kernel, outs, args, scratch=(), distant=0, flops=10**8):
    args = list(args)
    for k in range(distant):
        args[k] = pltpu.with_memory_space_constraint(args[k], pltpu.HBM)
    own = [pltpu.VMEM(shape, F32) for shape in scratch]
    if distant:
        own += [pltpu.SemaphoreType.DMA((distant + 1,))]
    return pl.pallas_call(
        kernel,
        out_shape=outs,
        in_specs=[FAR] * distant + [VM] * (len(args) - distant),
        out_specs=jax.tree.map(lambda _: VM, outs),
        scratch_shapes=own,
        compiler_params=pltpu.CompilerParams(vmem_limit_bytes=GRANT),
        cost_estimate=pl.CostEstimate(flops=flops, bytes_accessed=10**6, transcendentals=0),
    )(*args)


def pairs_of(count, odd):
    found = []
    for first in range(1 if odd else 0, count - 1, 2):
        found += [(first, first + 1), (first + 1, first)]
    return found


def slab_exchange(value, odd):
    slabs, energies = lax.axis_size("slab"), lax.axis_size("energy")
    pairs = pairs_of(slabs, odd)
    busy = {a for a, _ in pairs}
    whole = [(a * energies + e, b * energies + e) for a, b in pairs for e in range(energies)]
    for a in range(slabs):
        if a not in busy:
            whole += [(a * energies + e, a * energies + (e ^ 1)) for e in range(energies)]
    return lax.ppermute(value, ("slab", "energy"), whole)


def energy_exchange(value, odd):
    energies = lax.axis_size("energy")
    pairs = pairs_of(energies, odd)
    if odd:
        pairs += [(energies - 1, 0), (0, energies - 1)]
    return lax.ppermute(value, "energy", pairs)


def program(energy_index, diag_blocks, couple, probes, orbital_cell, dopant_cells, initial_potential):
    width = diag_blocks.shape[1]
    probe_count = probes.shape[1]
    slabs = lax.axis_size("slab")
    energies = lax.axis_size("energy")
    half = slabs // 2
    square, column = like(width, width), like(width, probe_count)
    letter = like(width, probe_count)
    sq = (width, width)

    even = slab_exchange(couple[0], False)
    paired = half == 2
    odd = even
    if not paired:
        odd = lax.ppermute(couple[0], "slab", [(s + 1, s) for s in range(1, slabs - 1, 2)])

    message = None
    for t in range(half - 1):
        args = [diag_blocks, couple, probes, energy_index.reshape(1, 1)]
        if t > 0:
            if t > 1:
                _, _, distance = place()
                message = jnp.where(distance == t, message, kept[0])
                sources = jnp.where(distance == t, sources, kept[1])
            kept = message, sources
            args += [message, sources, even, odd]
        outs = (square, column, square, square, column, letter)
        if not paired:
            outs += (square, column, letter)
        state = call(
            functools.partial(stage_kernel, t, not paired), outs,
            args, (sq, diag_blocks.shape, couple.shape, probes.shape), 3,
        )
        if t == 0:
            prepared = state
        last = t == half - 2
        message = slab_exchange(state[5] if last else state[8], t % 2 == 1)
        if not last:
            sources = slab_exchange(state[7], t % 2 == 1)
    factor_p, value_p = state[:2]
    matrix, source, link, base, base_source, near_map, far_map, inner, reach = call(
        ready_kernel,
        (square, column, square, square, column, square, square, column, square),
        [couple, even, odd, *prepared[:5]], (sq,),
    )
    reduced, first_factor, reach = lax.optimization_barrier((state[4], prepared[0], reach))
    sources = slab_exchange(reduced, half % 2 == 1)

    depth, rows_here, across = initial_potential.shape
    halo = SWEEPS
    rows_all = rows_here * energies
    pitch = -(-(rows_here + 2 * halo) // 8) * 8
    strip = halo * pitch
    even_rows, odd_rows = call(rows_kernel, (like(depth, halo, across),) * 2, [initial_potential])
    got_even = energy_exchange(even_rows, False)
    got_odd = energy_exchange(odd_rows, True)
    cells = (depth + 2 * halo) * pitch
    second = call(
        pack_kernel, like(width + width // 2 + width, probe_count),
        [first_factor, prepared[1]],
    )
    if paired:
        probes_near = slab_exchange(probes, False)
        second = slab_exchange(second, False)
    dopant_grid = call(
        functools.partial(deposit_kernel, rows_all, pitch, depth, rows_here),
        like(cells, across), [dopant_cells.reshape(1, -1)],
    )
    solved, factor, total, sent = call(
        centre_kernel, (square, square, square, letter),
        [message, matrix, link, base], (sq,),
    )
    across_middle = slab_exchange(sent, half % 2 == 0)
    value, total_source = call(
        source_kernel, (column, column),
        [sources, source, link, base_source, solved],
    )
    sources_middle = slab_exchange(total_source, half % 2 == 0)
    wide = call(
        halo_kernel, like(depth, pitch, across),
        [initial_potential, *lax.optimization_barrier((got_even, got_odd, sent))[:2]],
    )
    inverse = call(join_kernel, square, [across_middle, total], (sq,))
    if paired:
        slope, offset = call(
            expand_kernel, (like(4 * width, width), like(4 * width, probe_count)),
            [second, factor, value, *prepared[:2], near_map, far_map, inner, reach],
        )
        values = call(
            values_kernel, like(4 * width, probe_count),
            [sources_middle, inverse, total_source, slope, offset],
        )
        dens = call(density_kernel, like(1, 4 * width), [values, probes, probes_near])
    else:
        first, middle = call(
            middle_kernel, (column, column),
            [sources_middle, inverse, total_source, factor, value],
        )
        centred = (lax.axis_index("slab") == half) | (lax.axis_index("slab") == half - 1)
        factor_p = jnp.where(centred, prepared[0], factor_p)
        value_p = jnp.where(centred, prepared[1], value_p)
        known_p, known_q = first, middle
        for t in range(half - 2, -1, -1):
            known_p, known_q, dens = call(
                functools.partial(back_kernel, t),
                (column, column, like(1, 2 * width)),
                [couple, even, odd, probes, slab_exchange(first if t == half - 2 else known_p, t % 2 == 1),
                 first, middle,
                 known_p, known_q, factor_p, value_p, state[6], state[7], near_map, far_map, inner,
                 reach],
            )
    parts = [dens] + [
        lax.ppermute(dens, "energy", [(e, e ^ k) for e in range(energies)])
        for k in range(1, energies)
    ]
    spare = packet_planes(dens.shape[1] // across, orbital_cell.shape[0] // across)
    packet, packet_far = call(
        functools.partial(total_kernel, 1.0 / (probe_count * energies)),
        (like(spare + strip, across),) * 2, [orbital_cell.reshape(1, -1), wide, *parts],
    )
    near = slab_exchange(packet, False)
    far = slab_exchange(packet_far, True)

    def poisson(*refs):
        poisson_kernel(rows_all, depth * slabs, paired, *refs)

    potential, density = call(
        poisson, (like(depth, rows_here, across), like(2 * width)),
        [packet, near, far, dopant_grid, wide],
    )
    return (potential, density)


def solution(mesh):
    placed = (
        P("energy"),
        P(("cfg", "slab"), None, None),
        P(("cfg", "slab"), None, None),
        P("slab", None),
        P("slab"),
        P("cfg"),
        P(("cfg", "slab"), "energy", None),
    )
    return jax.shard_map(
        program,
        mesh=mesh,
        in_specs=placed,
        out_specs=(P(("cfg", "slab"), "energy", None), P(("cfg", "slab"))),
        check_vma=False,
    )
```
